256 devices in a mesh: dp: 16 (over y, x_lo, core), tensor: 16 (over x_hi, z).
Axes of the slice: x: 4 (x_hi: 2, x_lo: 2; x = x_hi * 2 + x_lo), y: 4, z: 8, core: 2. Of those that a mesh axis runs over, the one named last changes fastest.
Arguments:
- activations: bfloat16 [8192, 8192], P('tensor', 'dp'), may hold values from -6 to 6
- cotangent: bfloat16 [8192, 8192], P('tensor', 'dp'), may hold values from -6 to 6
- gate_first: bfloat16 [64, 128, 448], P('tensor'), may hold values from -0.5 to 0.5
- up_first: bfloat16 [64, 128, 448], P('tensor'), may hold values from -0.5 to 0.5
- gate_second: bfloat16 [224, 128, 128], P('tensor'), may hold values from -0.5 to 0.5
- up_second: bfloat16 [224, 128, 128], P('tensor'), may hold values from -0.5 to 0.5
- down_first: bfloat16 [224, 128, 128], P('tensor'), may hold values from -0.5 to 0.5
- down_second: bfloat16 [64, 448, 128], P('tensor'), may hold values from -0.25 to 0.25
Outputs:
- input_grad: bfloat16 [8192, 8192], P('tensor', 'dp')
- gate_first_grad: float32 [64, 128, 448], P('tensor', 'dp')
- up_first_grad: float32 [64, 128, 448], P('tensor', 'dp')
- gate_second_grad: float32 [224, 128, 128], P('tensor', 'dp')
- up_second_grad: float32 [224, 128, 128], P('tensor', 'dp')
- down_first_grad: float32 [224, 128, 128], P('tensor', 'dp')
- down_second_grad: float32 [64, 448, 128], P('tensor', 'dp')
The draws below stay inside these ranges and needn't reach their ends.
All inputs are finite; a program needn't handle non-finite values.
Results may differ from the reference program's by a relative error of at most 0.023.
Values may be sent and summed in bfloat16 or wider, within the bound.
No kernel may reach another device: no remote copies, remote signals or barrier semaphores. Data moves between devices by JAX's collectives and lax.ppermute only.
A program may use at most 64 MiB of HBM per device.

```python
import jax
import jax.numpy as jnp
from jax import lax

D = 8192
BLOCK = 128
TOK_DEV = 512
NBD = 64
NBF = 224
WIDE = 448
SUB = 2
TOKENS = 8192
N_DP = 16


def block_scale(own_key, shape, pieces, low, largest):
    loudness, own = 1.0, jax.random.fold_in(own_key, 6)
    for dim, shards_of in pieces:
        heights = jnp.exp(jax.random.uniform(jax.random.fold_in(own, dim), (shards_of,), jnp.float32, low / len(pieces), largest / len(pieces)))
        loudness = loudness * jnp.repeat(heights, shape[dim] // shards_of).reshape([-1 if axis == dim else 1 for axis in range(len(shape))])
    return loudness


def scatter_about(rng, dims, spread, limit, pieces=(), held_as=jnp.bfloat16):
    level = block_scale(rng, dims, pieces, -0.22, 0.18) if pieces else 1.0
    entries = jax.random.normal(rng, dims, jnp.float32) * spread * level
    return jnp.minimum(jnp.maximum(entries, -limit), limit).astype(held_as)


def setup_inputs(seed: int = 0) -> dict:
    key_of = jax.random.split(jax.random.key(seed), 9)
    return {
        "activations": scatter_about(key_of[0], (D, TOKENS), 1.0, 6.0, ((0, 16), (1, 16))),
        "cotangent": scatter_about(key_of[1], (D, TOKENS), 1.0, 6.0, ((0, 16), (1, 16))),
        "gate_first": scatter_about(key_of[2], (NBD, BLOCK, WIDE), BLOCK ** -0.5, 0.5, ((0, 16),)),
        "up_first": scatter_about(key_of[3], (NBD, BLOCK, WIDE), BLOCK ** -0.5, 0.5, ((0, 16),)),
        "gate_second": scatter_about(key_of[4], (NBF, BLOCK, BLOCK), BLOCK ** -0.5, 0.5, ((0, 16),)),
        "up_second": scatter_about(key_of[5], (NBF, BLOCK, BLOCK), BLOCK ** -0.5, 0.5, ((0, 16),)),
        "down_first": scatter_about(key_of[6], (NBF, BLOCK, BLOCK), BLOCK ** -0.5, 0.5, ((0, 16),)),
        "down_second": scatter_about(key_of[7], (NBD, WIDE, BLOCK), WIDE ** -0.5, 0.25, ((0, 16),)),
    }


def product(form, left, right):
    return jnp.einsum(form, left.astype(jnp.float32), right.astype(jnp.float32))


def to_hidden(middle):
    token_count = middle.shape[2]
    return middle.reshape(NBD, NBF, SUB, token_count).transpose(1, 2, 0, 3).reshape(NBF, BLOCK, token_count)


def to_model(middle):
    token_count = middle.shape[2]
    return middle.reshape(NBF, SUB, NBD, token_count).transpose(2, 0, 1, 3).reshape(NBD, WIDE, token_count)


def reference(activations, cotangent, gate_first, up_first, gate_second, up_second, down_first, down_second):
    token_count = TOK_DEV
    x_blocks = activations.reshape(D, N_DP, token_count).transpose(1, 0, 2)
    dy_blocks = cotangent.reshape(D, N_DP, token_count).transpose(1, 0, 2)

    def one_block(carry, pair):
        x_now, dy_now = pair
        inputs = x_now.reshape(NBD, BLOCK, token_count)
        upstream = dy_now.reshape(NBD, BLOCK, token_count)
        gate_mid = product("ibj,ibt->ijt", gate_first, inputs).astype(jnp.bfloat16)
        up_mid = product("ibj,ibt->ijt", up_first, inputs).astype(jnp.bfloat16)
        gate_in = to_hidden(gate_mid)
        up_in = to_hidden(up_mid)
        gate_pre = product("cko,ckt->cot", gate_second, gate_in)
        up_pre = product("cko,ckt->cot", up_second, up_in)
        sigma_gate = jax.nn.sigmoid(gate_pre)
        act = (gate_pre * sigma_gate * up_pre).astype(jnp.bfloat16)
        down_mid = product("cbo,cbt->cot", down_first, act).astype(jnp.bfloat16)
        down_in = to_model(down_mid)
        back_mid = product("ijo,iot->ijt", down_second, upstream).astype(jnp.bfloat16)
        grad_ds = product("ijt,iot->ijo", down_in, upstream)
        back_hidden = to_hidden(back_mid)
        grad_df = product("cbt,cot->cbo", act, back_hidden)
        act_grad = product("cbo,cot->cbt", down_first, back_hidden)
        gate_back = (act_grad * up_pre * sigma_gate * (1.0 + gate_pre * (1.0 - sigma_gate))).astype(jnp.bfloat16)
        up_back = (act_grad * gate_pre * sigma_gate).astype(jnp.bfloat16)
        grad_gs = product("ckt,cot->cko", gate_in, gate_back)
        grad_us = product("ckt,cot->cko", up_in, up_back)
        gate_low = to_model(product("cko,cot->ckt", gate_second, gate_back).astype(jnp.bfloat16))
        up_low = to_model(product("cko,cot->ckt", up_second, up_back).astype(jnp.bfloat16))
        grad_gf = product("ibt,ijt->ibj", inputs, gate_low)
        grad_uf = product("ibt,ijt->ibj", inputs, up_low)
        back_x = product("ibj,ijt->ibt", gate_first, gate_low) + product("ibj,ijt->ibt", up_first, up_low)
        back_x = back_x.astype(jnp.bfloat16).reshape(D, token_count)
        sums = (carry[0] + grad_gf, carry[1] + grad_uf, carry[2] + grad_gs, carry[3] + grad_us, carry[4] + grad_df, carry[5] + grad_ds)
        return sums, back_x

    start = (jnp.zeros((NBD, BLOCK, WIDE), jnp.float32), jnp.zeros((NBD, BLOCK, WIDE), jnp.float32),
             jnp.zeros((NBF, BLOCK, BLOCK), jnp.float32), jnp.zeros((NBF, BLOCK, BLOCK), jnp.float32),
             jnp.zeros((NBF, BLOCK, BLOCK), jnp.float32), jnp.zeros((NBD, WIDE, BLOCK), jnp.float32))
    sums, back_all = lax.scan(one_block, start, (x_blocks, dy_blocks))
    input_grad = back_all.transpose(1, 0, 2).reshape(D, TOKENS)
    loss_scale = TOKENS ** -0.5
    return (input_grad, sums[0] * loss_scale, sums[1] * loss_scale, sums[2] * loss_scale,
            sums[3] * loss_scale, sums[4] * loss_scale, sums[5] * loss_scale)
```

```python
import jax
import jax.numpy as jnp
from jax import lax
from jax.sharding import Mesh
from jax.sharding import PartitionSpec as P

BLOCK = 128
SUB = 2
BF = jnp.bfloat16
F32 = jnp.float32
GROUP = ("y", "x_lo", "core")
AROUND = ("y", "x_lo", "core", "x_hi")
CHIPS = ("y", "x_lo", "x_hi")


def size(name):
    return lax.axis_size(name)


def shift(value, step):
    count = size("z")
    return lax.ppermute(value, "z", [(i, (i + step) % count) for i in range(count)])


def swap(value):
    return lax.ppermute(value, "x_hi", [(0, 1), (1, 0)])


def matmul(form, left, right):
    return jnp.einsum(form, left, right, preferred_element_type=F32)


def gather_tokens(array, me):
    blocks = array.shape[0] // BLOCK
    half = array.shape[1] // 2
    mine = lax.dynamic_slice_in_dim(array, me * half, half, 1)
    other = swap(lax.dynamic_slice_in_dim(array, (1 - me) * half, half, 1))
    low = jnp.where(me == 0, mine, other)
    high = jnp.where(me == 0, other, mine)
    own = jnp.stack([low, high]).reshape(2 * blocks, BLOCK, half)
    return own


def ring_gather(own):
    count = size("z")
    at = lax.axis_index("z")
    full = jnp.zeros((count,) + own.shape, own.dtype)
    full = lax.dynamic_update_index_in_dim(full, own, at, 0)
    right = left = own
    for step in range(1, count // 2):
        right, left = shift(right, 1), shift(left, -1)
        full = lax.dynamic_update_index_in_dim(full, right, (at - step) % count, 0)
        full = lax.dynamic_update_index_in_dim(full, left, (at + step) % count, 0)
    middle = own.shape[0] // 2
    right, left = shift(right[:middle], 1), shift(left[middle:], -1)
    last = jnp.concatenate([right, left])
    full = lax.dynamic_update_index_in_dim(full, last, (at + count // 2) % count, 0)
    return full.reshape((count * own.shape[0],) + own.shape[1:])


def ring_sum(parts):
    count = size("z")
    at = lax.axis_index("z")
    middle = parts.shape[1] // 2

    def part(step):
        return lax.dynamic_index_in_dim(parts, (at + step) % count, 0, keepdims=False).astype(F32)

    far = part(count // 2).astype(BF)
    right, left = shift(far[:middle], 1), shift(far[middle:], -1)
    for step in range(count // 2 - 1, 0, -1):
        ahead, behind = part(step), part(-step)
        if step == count // 2 - 1:
            ahead = jnp.concatenate([ahead[:middle] + right.astype(F32), ahead[middle:]])
            behind = jnp.concatenate([behind[:middle], behind[middle:] + left.astype(F32)])
        else:
            ahead, behind = ahead + right.astype(F32), behind + left.astype(F32)
        right, left = shift(ahead.astype(BF), 1), shift(behind.astype(BF), -1)
    return part(0) + right.astype(F32) + left.astype(F32)


def sum_groups(sent):
    sent = sent.astype(BF)
    pairs = lax.all_to_all(sent.transpose(2, 0, 1, 3, 4, 5), "core", 0, 0, tiled=True)
    pairs = (pairs[0].astype(F32) + pairs[1].astype(F32)).astype(BF)
    pairs = pairs.reshape((-1,) + pairs.shape[3:])
    chips = lax.all_to_all(pairs, CHIPS, 0, 0, tiled=True)
    return jnp.sum(chips.astype(F32), axis=0)


def shards(
    activations, cotangent, gate_first, up_first, gate_second, up_second, down_first, down_second
):
    tokens = activations.shape[1]
    per = gate_first.shape[0]
    wide = gate_first.shape[2]
    hid = gate_second.shape[0]
    ny, nx, nc, nh, nz = (size(a) for a in ("y", "x_lo", "core", "x_hi", "z"))
    ngroup = ny * nx * nc
    scale = (ngroup * tokens) ** (-0.5)
    me = lax.axis_index("x_hi")
    half = tokens // 2
    nbd = per * nh * nz
    each = hid * SUB
    rows = BLOCK // ngroup

    quarter = lax.axis_index(("x_lo", "core"))
    piece = each // (nx * nc)
    firsts = jnp.stack([gate_first.transpose(0, 2, 1), up_first.transpose(0, 2, 1), down_second])
    firsts = firsts.reshape(3, per, nh, nz, each, BLOCK)
    firsts = lax.dynamic_index_in_dim(firsts, lax.axis_index("y"), 1, keepdims=False)
    firsts = lax.dynamic_slice_in_dim(firsts, quarter * piece, piece, 3)
    firsts = jnp.pad(firsts, ((0, 0), (0, 0), (0, 0), (0, 8 - piece), (0, 0)))
    firsts = firsts.transpose(2, 0, 1, 3, 4)
    firsts = lax.all_to_all(firsts, "z", 0, 0, tiled=True)
    seconds = jnp.stack([gate_second, up_second, down_first])
    seconds = lax.dynamic_slice_in_dim(seconds, lax.axis_index(GROUP) * rows, rows, 2)
    sent = jnp.concatenate([firsts.reshape(-1, BLOCK), seconds.reshape(-1, BLOCK)])
    count_first = firsts.size // BLOCK
    held = lax.all_gather(sent, AROUND, axis=0, tiled=False)
    first_all = held[:, :count_first].reshape(ny, nx * nc, nh, nz, 3, nh, 8, BLOCK)
    first_all = first_all[:, :, :, :, :, :, :piece]
    first_all = first_all.transpose(4, 3, 2, 0, 5, 1, 6, 7).reshape(3, nbd, nh * each, BLOCK)
    second_all = held[:, count_first:].reshape(ngroup, nh, 3, hid, rows, BLOCK)
    second_all = second_all.transpose(2, 1, 3, 0, 4, 5).reshape(3, nh * hid, BLOCK, BLOCK)
    def turn(weight, axis):
        shape = weight.shape
        cut = shape[:axis] + (SUB, nh, nz, per) + shape[axis + 1 :]
        weight = weight.reshape(cut)
        return jnp.swapaxes(weight, axis + 1, axis + 2).reshape(shape)

    w_gate, w_up, w_down = first_all[0], first_all[1], first_all[2]
    s_gate, s_up = turn(second_all[0], 1), turn(second_all[1], 1)
    s_down = turn(second_all[2], 2)
    mine = nh * hid

    def to_hidden(mid):
        return mid.reshape(nbd, mine, SUB, half).transpose(1, 2, 0, 3).reshape(mine, BLOCK, half)

    def to_model(mid):
        return mid.reshape(mine, SUB, nbd, half).transpose(2, 0, 1, 3).reshape(nbd, mine * SUB, half)

    own_x = gather_tokens(activations, me)
    own_dy = gather_tokens(cotangent, me)
    x = ring_gather(own_x)
    own_dy, x = lax.optimization_barrier((own_dy, x))
    dy = ring_gather(own_dy)

    gate_in = to_hidden(matmul("ijb,ibt->ijt", w_gate, x).astype(BF))
    up_in = to_hidden(matmul("ijb,ibt->ijt", w_up, x).astype(BF))
    gate_pre = matmul("cko,ckt->cot", s_gate, gate_in)
    up_pre = matmul("cko,ckt->cot", s_up, up_in)
    sigma = jax.nn.sigmoid(gate_pre)
    act = (gate_pre * sigma * up_pre).astype(BF)
    down_in = to_model(matmul("cbo,cbt->cot", s_down, act).astype(BF))
    back_in = to_hidden(matmul("ijo,iot->ijt", w_down, dy).astype(BF))
    act_grad = matmul("cbo,cot->cbt", s_down, back_in)
    gate_back = (act_grad * up_pre * sigma * (1.0 + gate_pre * (1.0 - sigma))).astype(BF)
    up_back = (act_grad * gate_pre * sigma).astype(BF)
    gate_low = to_model(matmul("cko,cot->ckt", s_gate, gate_back).astype(BF))
    up_low = to_model(matmul("cko,cot->ckt", s_up, up_back).astype(BF))
    both = matmul("ijb,ijt->ibt", w_gate, gate_low) + matmul("ijb,ijt->ibt", w_up, up_low)
    parts = both.astype(BF).reshape(nz, nh * per, BLOCK, half)
    total = ring_sum(parts).astype(BF).reshape(nh, per * BLOCK, half)
    kept = lax.dynamic_index_in_dim(total, me, 0, keepdims=False)
    other = swap(lax.dynamic_index_in_dim(total, 1 - me, 0, keepdims=False))
    input_grad = jnp.concatenate(
        [jnp.where(me == 0, kept, other), jnp.where(me == 0, other, kept)], axis=1
    )

    grad_ds = matmul("ijt,iot->ijo", down_in, dy)
    grad_df = matmul("cbt,cot->cbo", act, back_in)
    grad_gs = matmul("ckt,cot->cko", gate_in, gate_back)
    grad_us = matmul("ckt,cot->cko", up_in, up_back)
    grad_gf = matmul("ibt,ijt->ibj", x, gate_low)
    grad_uf = matmul("ibt,ijt->ibj", x, up_low)

    def unturn(grad, axis):
        shape = grad.shape
        cut = shape[:axis] + (SUB, nz, nh, per) + shape[axis + 1 :]
        return jnp.swapaxes(grad.reshape(cut), axis + 1, axis + 2).reshape(shape)

    groups = (ny, nx, nc)
    later = jnp.stack(
        [
            unturn(grad_gs.astype(BF), 1),
            unturn(grad_us.astype(BF), 1),
            unturn(grad_df.astype(BF), 2),
        ]
    )
    later = later.reshape((3, nh, hid) + groups + (rows, BLOCK))
    later = later.transpose(3, 4, 5, 1, 0, 2, 6, 7).reshape(groups + (nh, -1, BLOCK))
    sums_ds = grad_ds.astype(BF).reshape(nz, nh, per, nh, each, BLOCK).transpose(0, 3, 1, 2, 4, 5)
    sums_ds = sums_ds.reshape(groups + (nh, per * each, BLOCK))
    reduced = sum_groups(jnp.concatenate([later, sums_ds], axis=4)) * scale
    split = 3 * hid * rows
    out_gs, out_us, out_df = reduced[:split].reshape(3, hid, rows, BLOCK)
    table = []
    for part in range(ngroup):
        for z in range(nz):
            to_z, side = part // nh, part % nh
            table.append((part * nz + z, (side * nz + z) * nz + to_z))
    out_ds = lax.ppermute(reduced[split:], GROUP + ("z",), table).reshape(per, each, BLOCK)

    firsts = jnp.concatenate([grad_gf.astype(BF), grad_uf.astype(BF)], axis=2)
    firsts = firsts.reshape((nz, nh, per) + groups + (rows, 2 * nh * each))
    firsts = firsts.transpose(3, 4, 5, 1, 0, 2, 6, 7).reshape(groups + (nh, -1, 2 * nh * each))
    firsts = sum_groups(firsts) * scale
    firsts = firsts.reshape(nz, per * rows, 2 * nh * each)
    firsts = lax.all_to_all(firsts, "z", 0, 0, tiled=True)
    firsts = firsts.reshape(nz, per, rows, 2, nh, each).transpose(3, 1, 2, 4, 0, 5)
    out_gf, out_uf = firsts.reshape(2, per, rows, wide)
    return input_grad, out_gf, out_uf, out_gs, out_us, out_df, out_ds


def solution(mesh):
    fine = Mesh(mesh.devices.reshape(4, 2, 2, 2, 8), ("y", "x_lo", "core", "x_hi", "z"))
    tensor = ("x_hi", "z")
    arrays = P(tensor, GROUP)
    weights = P(tensor, None, None)
    return jax.shard_map(
        shards,
        mesh=fine,
        in_specs=(arrays, arrays) + (weights,) * 6,
        out_specs=(arrays,) + (P(tensor, GROUP, None),) * 6,
        check_vma=False,
    )
```

```python
import functools
import jax
import jax.numpy as jnp
from jax import lax
from jax.experimental import pallas as pl
from jax.experimental.pallas import tpu as pltpu
from jax.sharding import Mesh
from jax.sharding import PartitionSpec as P

BLOCK = 128
SUB = 2
BF = jnp.bfloat16
F32 = jnp.float32
NBD = 64
HID = 14
MINE = 28
EACH = MINE * SUB
ROWS = 64
SLOTS = 3
PER = 4
VM = pl.BlockSpec(memory_space=pltpu.VMEM)


def first_weight(held, kind, i):
    return held[(i % PER) * 4 + kind, i // PER]


def second_weight(held, kind, c):
    side, own = c // HID, c % HID
    at = own // SLOTS
    slot = own - jnp.minimum(at * SLOTS, HID - SLOTS)
    start = 16 + (side * SLOTS + slot) * 2
    return held[kind * 5 + at, pl.ds(start, 2)].reshape(BLOCK, BLOCK)


def dot(left, right):
    return lax.dot_general(left, right, (((1,), (0,)), ((), ())), preferred_element_type=F32)


def dot_first(left, right):
    return lax.dot_general(left, right, (((0,), (0,)), ((), ())), preferred_element_type=F32)


def dot_last(left, right):
    return lax.dot_general(left, right, (((1,), (1,)), ((), ())), preferred_element_type=F32)


def scatter_rows(ref, i, value):
    value = value.astype(BF).astype(F32)
    for part in range(2):
        ref[part, pl.ds(i, EACH, stride=NBD), :] = value[:, part * 128 : part * 128 + 128]


def gather_rows(ref, i):
    parts = [ref[part, pl.ds(i, EACH, stride=NBD), :] for part in range(2)]
    return jnp.concatenate(parts, axis=1)


def hidden_rows(ref, c):
    at = pl.multiple_of(c * BLOCK, BLOCK)
    return jnp.concatenate([ref[part, pl.ds(at, BLOCK), :] for part in range(2)], axis=1)


def put_hidden(ref, c, value):
    at = pl.multiple_of(c * BLOCK, BLOCK)
    value = value.astype(BF).astype(F32)
    for part in range(2):
        ref[part, pl.ds(at, BLOCK), :] = value[:, part * 128 : part * 128 + 128]


def loop(count, unroll):
    def run(body):
        def step(at, carry):
            for k in range(unroll):
                body(at * unroll + k)
            return carry

        lax.fori_loop(0, count // unroll, step, 0)

    return run


def forward_kernel(x, held, gate_in, up_in, act, gate_pre, up_pre, down_mid, mid_g, mid_u):
    @loop(NBD, 4)
    def _(i):
        block = x[i]
        scatter_rows(mid_g, i, dot(first_weight(held, 0, i), block)[:EACH])
        scatter_rows(mid_u, i, dot(first_weight(held, 1, i), block)[:EACH])

    @loop(MINE, 2)
    def _(c):
        gate, up = hidden_rows(mid_g, c).astype(BF), hidden_rows(mid_u, c).astype(BF)
        gate_in[c], up_in[c] = gate, up
        pre_g = dot_first(second_weight(held, 0, c), gate)
        pre_u = dot_first(second_weight(held, 1, c), up)
        gate_pre[c], up_pre[c] = pre_g, pre_u
        value = (pre_g * jax.nn.sigmoid(pre_g) * pre_u).astype(BF)
        act[c] = value
        put_hidden(down_mid, c, dot_first(second_weight(held, 2, c), value))


def backward_kernel(dy, held, gate_pre, up_pre, back_in, gate_back, up_back, low, parts, mid, low_g, low_u):
    @loop(NBD, 4)
    def _(i):
        scatter_rows(mid, i, dot(first_weight(held, 2, i), dy[i])[:EACH])

    @loop(MINE, 2)
    def _(c):
        back = hidden_rows(mid, c).astype(BF)
        back_in[c] = back
        grad = dot(second_weight(held, 2, c), back)
        gate, up = gate_pre[c], up_pre[c]
        sigma = jax.nn.sigmoid(gate)
        to_gate = (grad * up * sigma * (1.0 + gate * (1.0 - sigma))).astype(BF)
        to_up = (grad * gate * sigma).astype(BF)
        gate_back[c], up_back[c] = to_gate, to_up
        put_hidden(low_g, c, dot(second_weight(held, 0, c), to_gate))
        put_hidden(low_u, c, dot(second_weight(held, 1, c), to_up))

    fill = jnp.zeros((ROWS - EACH, 256), F32)

    @loop(NBD, 4)
    def _(i):
        both = jnp.concatenate([gather_rows(low_g, i), fill, gather_rows(low_u, i), fill]).astype(BF)
        low[i] = both
        weight = jnp.concatenate([first_weight(held, 0, i), first_weight(held, 1, i)])
        side, at = i // 32, i % 32
        parts[(at // PER) * 8 + side * PER + at % PER] = dot_first(weight, both).astype(BF)


def put_rows(ref, side, at, value):
    for group in range(16):
        ref[group % 2, group // 2, side, at] = value[group * 8 : group * 8 + 8].astype(BF)


def second_grads_kernel(dy, down_mid, act, back_in, gate_in, up_in, gate_back, up_back, out):
    @loop(MINE, 1)
    def _(c):
        side, own = c // HID, c % HID
        put_rows(out, side, own, dot_last(gate_in[c], gate_back[c]))
        put_rows(out, side, HID + own, dot_last(up_in[c], up_back[c]))
        put_rows(out, side, 2 * HID + own, dot_last(act[c], back_in[c]))

    fill = jnp.zeros((4, BLOCK), F32)

    @loop(NBD, 2)
    def _(i):
        side, z, p = i // 32, i % 32 // PER, i % PER
        grad = dot_last(gather_rows(down_mid, i).astype(BF), dy[i])
        for half in range(2):
            rows = jnp.concatenate([grad[half * 28 : half * 28 + 28], fill])
            for k in range(4):
                out[half, z, side, 3 * HID + p * 4 + k] = rows[k * 8 : k * 8 + 8].astype(BF)


def first_grads_kernel(x, low, out):
    @loop(NBD, 2)
    def _(i):
        put_rows(out, i // 32, i % 32, dot_last(x[i], low[i]))


def call(kernel, outs, scratch, flops, *args):
    shapes = [jax.ShapeDtypeStruct(shape, dtype) for shape, dtype in outs]
    moved = sum(a.size * a.dtype.itemsize for a in args)
    return pl.pallas_call(
        kernel,
        out_shape=shapes,
        in_specs=[VM] * len(args),
        out_specs=[VM] * len(outs),
        scratch_shapes=[pltpu.VMEM(shape, dtype) for shape, dtype in scratch],
        compiler_params=pltpu.CompilerParams(vmem_limit_bytes=52 << 20),
        cost_estimate=pl.CostEstimate(flops=flops, bytes_accessed=moved, transcendentals=0),
    )(*args)


HIDDEN = ((MINE, BLOCK, 256), BF)
WIDER = ((MINE, BLOCK, 256), F32)
SPREAD = ((2, MINE * BLOCK, 128), F32)
ONE = 2 * 448 * 4 * 128 * 512


def forward(x, held):
    return call(forward_kernel, [HIDDEN, HIDDEN, HIDDEN, WIDER, WIDER, SPREAD], [SPREAD, SPREAD], 5 * ONE, x, held)


def backward(dy, held, gate_pre, up_pre):
    return call(
        backward_kernel,
        [HIDDEN, HIDDEN, HIDDEN, ((NBD, 2 * ROWS, 256), BF), ((NBD, BLOCK, 256), BF)],
        [SPREAD] * 3,
        6 * ONE,
        dy, held, gate_pre, up_pre,
    )


def second_grads(*args):
    return call(second_grads_kernel, [((2, 8, 2, 58, 8, 128), BF)], [], 4 * ONE, *args)[0]


def first_grads(x, low):
    return call(first_grads_kernel, [((2, 8, 2, 32, 8, 128), BF)], [], 2 * ONE, x, low)[0]


GROUP = ("y", "x_lo", "core")
CHIPS = ("y", "x_lo", "x_hi")
TENSOR = ("x_hi", "z")


def size(name):
    return lax.axis_size(name)


def shift(value, step):
    count = size("z")
    return lax.ppermute(value, "z", [(i, (i + step) % count) for i in range(count)])


def swap(value):
    return lax.ppermute(value, "x_hi", [(0, 1), (1, 0)])


def halves(array, me):
    blocks = array.shape[0] // BLOCK
    half = array.shape[1] // 2
    own = lax.dynamic_slice_in_dim(array, me * half, half, 1)
    other = swap(lax.dynamic_slice_in_dim(array, (1 - me) * half, half, 1))
    return own.reshape(blocks, BLOCK, half), other.reshape(blocks, BLOCK, half)


def ring_gather(own, other, me):
    count = size("z")
    at = lax.axis_index("z")
    full = jnp.zeros((2, count) + own.shape, own.dtype)

    def put(full, value, side, step):
        where = (side, (at + step) % count) + (0,) * value.ndim
        return lax.dynamic_update_slice(full, value[None, None], where)

    full = put(full, own, me, 0)
    full = put(full, other, 1 - me, 0)
    sides = [(own, me), (other, 1 - me)]
    right, left = [own, other], [own, other]
    for step in range(1, count // 2):
        for k, (_, side) in enumerate(sides):
            right[k], left[k] = shift(right[k], 1), shift(left[k], -1)
            full = put(full, right[k], side, -step)
            full = put(full, left[k], side, step)
    full = put(full, shift(right[0], 1), me, count // 2)
    full = put(full, shift(left[1], -1), 1 - me, count // 2)
    return full.reshape((2 * count * own.shape[0],) + own.shape[1:])


def sum_groups(sent):
    pairs = lax.all_to_all(sent, "core", 0, 0, tiled=True)
    pairs = (pairs[0].astype(F32) + pairs[1].astype(F32)).astype(BF)
    pairs = pairs.reshape((-1,) + pairs.shape[2:])
    chips = lax.all_to_all(pairs, CHIPS, 0, 0, tiled=True)
    return jnp.sum(chips.astype(F32), axis=0)


def gather_weights(gate_first, up_first, gate_second, up_second, down_first, down_second):
    nh, nz = size("x_hi"), size("z")
    y, kind = lax.axis_index("y"), lax.axis_index(("x_lo", "core"))
    hid = gate_second.shape[0]
    each = hid * SUB
    take = functools.partial(lax.dynamic_index_in_dim, index=y, axis=0, keepdims=False)
    gate, up = take(gate_first).T, take(up_first).T
    first = jnp.where(kind == 0, gate, jnp.where(kind == 1, up, take(down_second)))
    first = first.reshape(nh, nz, each, BLOCK).transpose(1, 0, 2, 3).reshape(nz, nh * each, BLOCK)
    first = jnp.pad(first, ((0, 0), (0, ROWS - nh * each), (0, 0)))
    first = jnp.broadcast_to(first[None], (nh,) + first.shape).reshape(nh * nz, ROWS, BLOCK)
    first = lax.all_to_all(first, TENSOR, 0, 0, tiled=True)
    d = lax.axis_index(GROUP)
    kind, at = d // 5, jnp.minimum((d % 5) * SLOTS, hid - SLOTS)
    take = functools.partial(lax.dynamic_slice_in_dim, start_index=at, slice_size=SLOTS, axis=0)
    second = jnp.where(
        kind == 0, take(gate_second), jnp.where(kind == 1, take(up_second), take(down_first))
    )
    other = swap(second)
    me = lax.axis_index("x_hi")
    second = jnp.concatenate([jnp.where(me == 0, second, other), jnp.where(me == 0, other, second)])
    second = second.reshape(-1, ROWS, BLOCK)
    return lax.all_gather(jnp.concatenate([first, second]), GROUP, axis=0, tiled=False)


def shards(
    activations, cotangent, gate_first, up_first, gate_second, up_second, down_first, down_second
):
    tokens = activations.shape[1]
    per = gate_first.shape[0]
    wide = gate_first.shape[2]
    hid = gate_second.shape[0]
    ny, nx, nc, nh, nz = (size(a) for a in ("y", "x_lo", "core", "x_hi", "z"))
    ngroup = ny * nx * nc
    scale = (ngroup * tokens) ** (-0.5)
    me = lax.axis_index("x_hi")
    half = tokens // 2
    each = hid * SUB
    rows = BLOCK // ngroup

    held = gather_weights(gate_first, up_first, gate_second, up_second, down_first, down_second)
    x_own, x_other = halves(activations, me)
    dy_own, dy_other = halves(cotangent, me)
    x = ring_gather(x_own, x_other, me)
    dy = ring_gather(dy_own, dy_other, me)

    gate_in, up_in, act, gate_pre, up_pre, down_mid = forward(x, held)
    back_in, gate_back, up_back, low, parts = backward(dy, held, gate_pre, up_pre)

    total = lax.psum_scatter(parts, "z", scatter_dimension=0, tiled=True)
    total = total.reshape(nh, per * BLOCK, half)
    kept = lax.dynamic_index_in_dim(total, me, 0, keepdims=False)
    other = swap(lax.dynamic_index_in_dim(total, 1 - me, 0, keepdims=False))
    input_grad = jnp.concatenate(
        [jnp.where(me == 0, kept, other), jnp.where(me == 0, other, kept)], axis=1
    )

    later = second_grads(dy, down_mid, act, back_in, gate_in, up_in, gate_back, up_back)
    later = sum_groups(later) * scale
    out_gs, out_us, out_df = later[: 3 * hid].reshape(3, hid, rows, BLOCK)
    table = []
    for part in range(ngroup):
        for z in range(nz):
            to_z, side = part // nh, part % nh
            table.append((part * nz + z, (side * nz + z) * nz + to_z))
    out_ds = lax.ppermute(later[3 * hid :], GROUP + ("z",), table)
    out_ds = out_ds.reshape(per, -1, BLOCK)[:, :each]

    firsts = sum_groups(first_grads(x, low)) * scale
    firsts = firsts.reshape(nz, per * rows, 2 * ROWS)
    firsts = lax.all_to_all(firsts, "z", 0, 0, tiled=True)
    firsts = firsts.reshape(nz, per, rows, 2, ROWS)[..., : nh * each]
    firsts = firsts.reshape(nz, per, rows, 2, nh, each).transpose(3, 1, 2, 4, 0, 5)
    out_gf, out_uf = firsts.reshape(2, per, rows, wide)
    return input_grad, out_gf, out_uf, out_gs, out_us, out_df, out_ds


def solution(mesh):
    fine = Mesh(mesh.devices.reshape(4, 2, 2, 2, 8), ("y", "x_lo", "core", "x_hi", "z"))
    arrays = P(TENSOR, GROUP)
    weights = P(TENSOR, None, None)
    return jax.shard_map(
        shards,
        mesh=fine,
        in_specs=(arrays, arrays) + (weights,) * 6,
        out_specs=(arrays,) + (P(TENSOR, GROUP, None),) * 6,
        check_vma=False,
    )
```

```python
import functools
import jax
import jax.numpy as jnp
import numpy as np
from jax import lax
from jax.experimental import pallas as pl
from jax.experimental.pallas import tpu as pltpu
from jax.sharding import Mesh
from jax.sharding import PartitionSpec as P

BLOCK = 128
SUB = 2
BF = jnp.bfloat16
F32 = jnp.float32
NBD = 64
HID = 14
MINE = 28
EACH = MINE * SUB
ROWS = 64
SLOTS = 3
PER = 4
TOK = 256
VM = pl.BlockSpec(memory_space=pltpu.VMEM)
SM = pl.BlockSpec(memory_space=pltpu.SMEM)


def first_weight(held, kind, i):
    return held[(i % PER) * 4 + kind, i // PER]


def second_weight(held, kind, c):
    side, own = c // HID, c % HID
    at = own // SLOTS
    slot = own - jnp.minimum(at * SLOTS, HID - SLOTS)
    start = (side * SLOTS + slot) * 2
    return held[kind * 5 + at, pl.ds(start, 2)].reshape(BLOCK, BLOCK)


def dot(left, right):
    return lax.dot_general(left, right, (((1,), (0,)), ((), ())), preferred_element_type=F32)


def dot_first(left, right):
    return lax.dot_general(left, right, (((0,), (0,)), ((), ())), preferred_element_type=F32)


def dot_last(left, right):
    return lax.dot_general(left, right, (((1,), (1,)), ((), ())), preferred_element_type=F32)


def loop(count, unroll):
    def run(body):
        def step(at, carry):
            body([at * unroll + k for k in range(unroll)])
            return carry

        lax.fori_loop(0, count // unroll, step, 0)

    return run


def collect(where, shards, out):
    me, z = where[0], where[1]
    for k, shard in enumerate(shards):
        side = me if k % 2 == 0 else 1 - me
        out[pl.ds(side * 32 + lax.rem(z + k // 2, 8) * PER, PER)] = shard[...]


def turn(swap, source, target, outer):
    tiles = [source[:, k * 16 : k * 16 + 16, :].reshape(256, TOK) for k in range(4)]
    tiles = [dot(swap[...], tile).astype(BF).reshape(16, 16, TOK) for tile in tiles]
    for k, tile in enumerate(tiles):
        target[k * 16 : k * 16 + 16, pl.ds(outer, 16), :] = tile


def forward_first_kernel(where, swap, held, *refs):
    shards, (x, gate_in, up_in, mid_g, mid_u) = refs[:16], refs[16:]
    collect(where, shards, x)

    def group(at, carry):
        @loop(16, 4)
        def _(ks):
            weights = [
                jnp.concatenate([first_weight(held, 0, at * 16 + k), first_weight(held, 1, at * 16 + k)])
                for k in ks
            ]
            mids = [dot(w, x[at * 16 + k]).astype(BF) for w, k in zip(weights, ks)]
            for mid, k in zip(mids, ks):
                mid_g[k] = mid[:ROWS]
                mid_u[k] = mid[ROWS:]

        outer = pl.multiple_of(at * 16, 16)
        turn(swap, mid_g, gate_in, outer)
        turn(swap, mid_u, up_in, outer)
        return carry

    lax.fori_loop(0, 4, group, 0)


def hidden(ref, c):
    return ref[pl.ds(c * SUB, SUB)].reshape(BLOCK, TOK)


def turn_back(swap, source, target, unit):
    def group(at, carry):
        tiles = [
            source[k * 16 : k * 16 + 16, pl.ds(pl.multiple_of(at * 16, 16), 16), :].reshape(256, TOK)
            for k in range(4)
        ]
        tiles = [dot(swap[...], tile).astype(BF).reshape(16, 16, TOK) for tile in tiles]
        for k, tile in enumerate(tiles):
            target[pl.ds(at * 16, 16), unit + k * 16 : unit + k * 16 + 16, :] = tile
        return carry

    lax.fori_loop(0, 4, group, 0)


def forward_second_kernel(swap, held, gate_in, up_in, act, to_gate, to_up, down_in, down_mid):
    down_mid[EACH:] = jnp.zeros((ROWS - EACH, NBD, TOK), BF)

    @loop(MINE, 2)
    def _(cs):
        gates = [dot_first(second_weight(held, 0, c), hidden(gate_in, c)) for c in cs]
        ups = [dot_first(second_weight(held, 1, c), hidden(up_in, c)) for c in cs]
        sigmas = [jax.nn.sigmoid(g) for g in gates]
        acts = [(g * s * u).astype(BF) for g, s, u in zip(gates, sigmas, ups)]
        downs = [dot_first(second_weight(held, 2, c), a) for c, a in zip(cs, acts)]
        for c, g, s, u, a, d in zip(cs, gates, sigmas, ups, acts, downs):
            to_gate[c], to_up[c], act[c] = u * s * (1.0 + g * (1.0 - s)), g * s, a
            down_mid[pl.ds(c * SUB, SUB)] = d.astype(BF).reshape(SUB, NBD, TOK)

    turn_back(swap, down_mid, down_in, 0)


def backward_kernel(where, swap, held_first, held_second, to_gate, to_up, *refs):
    shards = refs[:16]
    dy, back_in, gate_back, up_back, low, parts, mid, low_g, low_u = refs[16:]
    collect(where, shards, dy)
    low_g[EACH:] = jnp.zeros((ROWS - EACH, NBD, TOK), BF)
    low_u[EACH:] = jnp.zeros((ROWS - EACH, NBD, TOK), BF)

    def group(at, carry):
        @loop(16, 4)
        def _(ks):
            mids = [dot(first_weight(held_first, 2, at * 16 + k), dy[at * 16 + k]).astype(BF) for k in ks]
            for value, k in zip(mids, ks):
                mid[k] = value

        turn(swap, mid, back_in, pl.multiple_of(at * 16, 16))
        return carry

    lax.fori_loop(0, 4, group, 0)

    @loop(MINE, 2)
    def _(cs):
        grads = [dot(second_weight(held_second, 2, c), hidden(back_in, c)) for c in cs]
        to_gates = [(grad * to_gate[c]).astype(BF) for c, grad in zip(cs, grads)]
        to_ups = [(grad * to_up[c]).astype(BF) for c, grad in zip(cs, grads)]
        lows_g = [dot(second_weight(held_second, 0, c), v) for c, v in zip(cs, to_gates)]
        lows_u = [dot(second_weight(held_second, 1, c), v) for c, v in zip(cs, to_ups)]
        for c, g, u, lg, lu in zip(cs, to_gates, to_ups, lows_g, lows_u):
            gate_back[c], up_back[c] = g, u
            low_g[pl.ds(c * SUB, SUB)] = lg.astype(BF).reshape(SUB, NBD, TOK)
            low_u[pl.ds(c * SUB, SUB)] = lu.astype(BF).reshape(SUB, NBD, TOK)

    turn_back(swap, low_g, low, 0)
    turn_back(swap, low_u, low, ROWS)

    @loop(NBD, 4)
    def _(blocks):
        weights = [
            jnp.concatenate([first_weight(held_first, 0, i), first_weight(held_first, 1, i)]) for i in blocks
        ]
        values = [dot_first(w, low[i]).astype(BF) for w, i in zip(weights, blocks)]
        for i, value in zip(blocks, values):
            side, at = i // 32, i % 32
            parts[(at // PER) * 8 + side * PER + at % PER] = value


def put_rows(ref, side, at, value):
    for group in range(16):
        ref[group % 2, group // 2, side, at] = value[group * 8 : group * 8 + 8].astype(BF)


def second_grads_kernel(dy, down_in, act, back_in, gate_in, up_in, gate_back, up_back, out):
    @loop(MINE, 2)
    def _(cs):
        grads = [
            (
                dot_last(hidden(gate_in, c), gate_back[c]),
                dot_last(hidden(up_in, c), up_back[c]),
                dot_last(act[c], hidden(back_in, c)),
            )
            for c in cs
        ]
        for c, grad in zip(cs, grads):
            for k in range(3):
                put_rows(out, c // HID, k * HID + c % HID, grad[k])

    fill = jnp.zeros((4, BLOCK), F32)

    @loop(NBD, 4)
    def _(blocks):
        grads = [dot_last(down_in[i], dy[i]) for i in blocks]
        for i, grad in zip(blocks, grads):
            side, z, p = i // 32, i % 32 // PER, i % PER
            for half in range(2):
                rows = jnp.concatenate([grad[half * 28 : half * 28 + 28], fill])
                for k in range(4):
                    out[half, z, side, 3 * HID + p * 4 + k] = rows[k * 8 : k * 8 + 8].astype(BF)


def first_grads_kernel(x, low, out):
    @loop(NBD, 4)
    def _(blocks):
        grads = [dot_last(x[i], low[i]) for i in blocks]
        for i, grad in zip(blocks, grads):
            put_rows(out, i // 32, i % 32, grad)


def call(kernel, outs, scratch, flops, *args):
    shapes = [jax.ShapeDtypeStruct(shape, dtype) for shape, dtype in outs]
    moved = sum(a.size * a.dtype.itemsize for a in args)
    return pl.pallas_call(
        kernel,
        out_shape=shapes,
        in_specs=[SM if a.dtype == jnp.int32 else VM for a in args],
        out_specs=[VM] * len(outs),
        scratch_shapes=[pltpu.VMEM(shape, dtype) for shape, dtype in scratch],
        compiler_params=pltpu.CompilerParams(vmem_limit_bytes=48 << 20),
        cost_estimate=pl.CostEstimate(flops=flops, bytes_accessed=moved, transcendentals=0),
    )(*args)


HIDDEN = ((MINE, BLOCK, TOK), BF)
WIDER = ((MINE, BLOCK, TOK), F32)
SPREAD = ((ROWS, NBD, TOK), BF)
MODEL = ((NBD, BLOCK, TOK), BF)
TILE = ((16, ROWS, TOK), BF)
ONE = 2 * 448 * 4 * 128 * 512


def swap_table():
    at = np.arange(256)
    table = np.zeros((256, 256), np.float32)
    table[at, at % 16 * 16 + at // 16] = 1.0
    return jnp.asarray(table, BF)


def forward_first(where, swap, held, shards):
    return call(forward_first_kernel, [MODEL, SPREAD, SPREAD], [TILE, TILE], 6 * ONE, where, swap, held, *shards)


def forward_second(swap, held, gate_in, up_in):
    outs = [HIDDEN, WIDER, WIDER, SPREAD]
    return call(forward_second_kernel, outs, [SPREAD], 5 * ONE, swap, held, gate_in, up_in)


def backward(where, swap, held_first, held_second, to_gate, to_up, shards):
    return call(
        backward_kernel,
        [MODEL, SPREAD, HIDDEN, HIDDEN, MODEL, MODEL],
        [TILE, SPREAD, SPREAD],
        12 * ONE,
        where, swap, held_first, held_second, to_gate, to_up, *shards,
    )


def second_grads(*args):
    return call(second_grads_kernel, [((2, 8, 2, 58, 8, 128), BF)], [], 4 * ONE, *args)[0]


def first_grads(x, low):
    return call(first_grads_kernel, [((2, 8, 2, 32, 8, 128), BF)], [], 2 * ONE, x, low)[0]


GROUP = ("y", "x_lo", "core")
CHIPS = ("y", "x_lo", "x_hi")
TENSOR = ("x_hi", "z")


def size(name):
    return lax.axis_size(name)


def shift(value, step):
    count = size("z")
    return lax.ppermute(value, "z", [(i, (i + step) % count) for i in range(count)])


def swap(value):
    return lax.ppermute(value, "x_hi", [(0, 1), (1, 0)])


def halves(array, me):
    blocks = array.shape[0] // BLOCK
    half = array.shape[1] // 2
    own = lax.dynamic_slice_in_dim(array, me * half, half, 1)
    other = swap(lax.dynamic_slice_in_dim(array, (1 - me) * half, half, 1))
    return own.reshape(blocks, BLOCK, half), other.reshape(blocks, BLOCK, half)


def ring_gather(own, other):
    count = size("z")
    found = [[None, None] for _ in range(count)]
    found[0] = [own, other]
    right, left = [own, other], [own, other]
    for step in range(1, count // 2):
        for k in range(2):
            right[k], left[k] = shift(right[k], 1), shift(left[k], -1)
            found[count - step][k], found[step][k] = right[k], left[k]
    found[count // 2] = [shift(right[0], 1), shift(left[1], -1)]
    return [shard for pair in found for shard in pair]


def sum_groups(sent):
    pairs = lax.all_to_all(sent, "core", 0, 0, tiled=True)
    pairs = (pairs[0].astype(F32) + pairs[1].astype(F32)).astype(BF)
    pairs = pairs.reshape((-1,) + pairs.shape[2:])
    chips = lax.all_to_all(pairs, CHIPS, 0, 0, tiled=True)
    return jnp.sum(chips.astype(F32), axis=0)


def gather_first(gate_first, up_first, down_second):
    nh, nz = size("x_hi"), size("z")
    y, kind = lax.axis_index("y"), lax.axis_index(("x_lo", "core"))
    each = gate_first.shape[2] // (nh * nz)
    take = functools.partial(lax.dynamic_index_in_dim, index=y, axis=0, keepdims=False)
    gate, up = take(gate_first).T, take(up_first).T
    first = jnp.where(kind == 0, gate, jnp.where(kind == 1, up, take(down_second)))
    first = first.reshape(nh, nz, each, BLOCK).transpose(1, 0, 2, 3).reshape(nz, nh * each, BLOCK)
    first = jnp.pad(first, ((0, 0), (0, ROWS - nh * each), (0, 0)))
    first = jnp.broadcast_to(first[None], (nh,) + first.shape).reshape(nh * nz, ROWS, BLOCK)
    first = lax.all_to_all(first, TENSOR, 0, 0, tiled=True)
    return lax.all_gather(first, GROUP, axis=0, tiled=False)


def gather_second(gate_second, up_second, down_first):
    hid = gate_second.shape[0]
    d = lax.axis_index(GROUP)
    kind, at = d // 5, jnp.minimum((d % 5) * SLOTS, hid - SLOTS)
    take = functools.partial(lax.dynamic_slice_in_dim, start_index=at, slice_size=SLOTS, axis=0)
    second = jnp.where(
        kind == 0, take(gate_second), jnp.where(kind == 1, take(up_second), take(down_first))
    )
    other = swap(second)
    me = lax.axis_index("x_hi")
    second = jnp.concatenate([jnp.where(me == 0, second, other), jnp.where(me == 0, other, second)])
    return lax.all_gather(second.reshape(-1, ROWS, BLOCK), GROUP, axis=0, tiled=False)


def shards(
    activations, cotangent, gate_first, up_first, gate_second, up_second, down_first, down_second
):
    tokens = activations.shape[1]
    per = gate_first.shape[0]
    wide = gate_first.shape[2]
    hid = gate_second.shape[0]
    ny, nx, nc, nh, nz = (size(a) for a in ("y", "x_lo", "core", "x_hi", "z"))
    ngroup = ny * nx * nc
    scale = (ngroup * tokens) ** (-0.5)
    me = lax.axis_index("x_hi")
    half = tokens // 2
    each = hid * SUB
    rows = BLOCK // ngroup

    where = jnp.stack([me, lax.axis_index("z")]).astype(jnp.int32)
    table = swap_table()
    x_own, x_other = halves(activations, me)
    held_second = gather_second(gate_second, up_second, down_first)
    xs = ring_gather(x_own, x_other)
    dy_own, dy_other = halves(cotangent, me)
    weights = (gate_first, up_first, down_second)
    weights, _ = lax.optimization_barrier((weights, (xs[2], xs[14])))
    held_first = gather_first(*weights)
    (dy_own, dy_other), _ = lax.optimization_barrier(((dy_own, dy_other), (xs[2], xs[14])))
    dys = ring_gather(dy_own, dy_other)

    x, gate_in, up_in = forward_first(where, table, held_first, xs)
    act, to_gate, to_up, down_in = forward_second(table, held_second, gate_in, up_in)
    dy, back_in, gate_back, up_back, low, parts = backward(
        where, table, held_first, held_second, to_gate, to_up, dys
    )

    total = lax.psum_scatter(parts, "z", scatter_dimension=0, tiled=True)
    total = total.reshape(nh, per * BLOCK, half)
    kept = lax.dynamic_index_in_dim(total, me, 0, keepdims=False)
    other = swap(lax.dynamic_index_in_dim(total, 1 - me, 0, keepdims=False))
    input_grad = jnp.concatenate(
        [jnp.where(me == 0, kept, other), jnp.where(me == 0, other, kept)], axis=1
    )

    later = second_grads(dy, down_in, act, back_in, gate_in, up_in, gate_back, up_back)
    later = sum_groups(later) * scale
    out_gs, out_us, out_df = later[: 3 * hid].reshape(3, hid, rows, BLOCK)
    pairs = []
    for part in range(ngroup):
        for z in range(nz):
            to_z, side = part // nh, part % nh
            pairs.append((part * nz + z, (side * nz + z) * nz + to_z))
    out_ds = lax.ppermute(later[3 * hid :], GROUP + ("z",), pairs)
    out_ds = out_ds.reshape(per, -1, BLOCK)[:, :each]

    firsts = sum_groups(first_grads(x, low)) * scale
    firsts = firsts.reshape(nz, per * rows, 2 * ROWS)
    firsts = lax.all_to_all(firsts, "z", 0, 0, tiled=True)
    firsts = firsts.reshape(nz, per, rows, 2, ROWS)[..., : nh * each]
    firsts = firsts.reshape(nz, per, rows, 2, nh, each).transpose(3, 1, 2, 4, 0, 5)
    out_gf, out_uf = firsts.reshape(2, per, rows, wide)
    return input_grad, out_gf, out_uf, out_gs, out_us, out_df, out_ds


def solution(mesh):
    fine = Mesh(mesh.devices.reshape(4, 2, 2, 2, 8), ("y", "x_lo", "core", "x_hi", "z"))
    arrays = P(TENSOR, GROUP)
    weights = P(TENSOR, None, None)
    return jax.shard_map(
        shards,
        mesh=fine,
        in_specs=(arrays, arrays) + (weights,) * 6,
        out_specs=(arrays,) + (P(TENSOR, GROUP, None),) * 6,
        check_vma=False,
    )
```

```python
import functools
import jax
import jax.numpy as jnp
import numpy as np
from jax import lax
from jax.experimental import pallas as pl
from jax.experimental.pallas import tpu as pltpu
from jax.sharding import Mesh
from jax.sharding import PartitionSpec as P

BLOCK = 128
SUB = 2
BF = jnp.bfloat16
F32 = jnp.float32
NBD = 64
HID = 14
MINE = 28
EACH = MINE * SUB
ROWS = 64
SLOTS = 3
PER = 4
TOK = 256
VM = pl.BlockSpec(memory_space=pltpu.VMEM)
SM = pl.BlockSpec(memory_space=pltpu.SMEM)


def first_weight(held, kind, i):
    return held[(i % PER) * 4 + kind, i // PER]


def second_weight(held, kind, c):
    side, own = c // HID, c % HID
    at = own // SLOTS
    slot = own - jnp.minimum(at * SLOTS, HID - SLOTS)
    return held[(kind * 5 + at) * 2 + side, slot]


def dot(left, right):
    return lax.dot_general(left, right, (((1,), (0,)), ((), ())), preferred_element_type=F32)


def dot_first(left, right):
    return lax.dot_general(left, right, (((0,), (0,)), ((), ())), preferred_element_type=F32)


def dot_last(left, right):
    return lax.dot_general(left, right, (((1,), (1,)), ((), ())), preferred_element_type=F32)


def loop(count, unroll):
    def run(body):
        def step(at, carry):
            body([at * unroll + k for k in range(unroll)])
            return carry

        lax.fori_loop(0, count // unroll, step, 0)

    return run


def collect(where, shards, out):
    me, z = where[0], where[1]
    for k, shard in enumerate(shards):
        side = me if k % 2 == 0 else 1 - me
        out[pl.ds(side * 32 + lax.rem(z + k // 2, 8) * PER, PER)] = shard[...]


def turn(swap, source, target, outer):
    tiles = [source[:, k * 16 : k * 16 + 16, :].reshape(256, TOK) for k in range(4)]
    tiles = [dot(swap[...], tile).astype(BF).reshape(16, 16, TOK) for tile in tiles]
    for k, tile in enumerate(tiles):
        target[k * 16 : k * 16 + 16, pl.ds(outer, 16), :] = tile


def forward_first_kernel(where, swap, held, *refs):
    shards, (x, gate_in, up_in, mid_g, mid_u) = refs[:16], refs[16:]
    collect(where, shards, x)

    def group(at, carry):
        @loop(16, 4)
        def _(ks):
            weights = [
                jnp.concatenate([first_weight(held, 0, at * 16 + k), first_weight(held, 1, at * 16 + k)])
                for k in ks
            ]
            mids = [dot(w, x[at * 16 + k]).astype(BF) for w, k in zip(weights, ks)]
            for mid, k in zip(mids, ks):
                mid_g[k] = mid[:ROWS]
                mid_u[k] = mid[ROWS:]

        outer = pl.multiple_of(at * 16, 16)
        turn(swap, mid_g, gate_in, outer)
        turn(swap, mid_u, up_in, outer)
        return carry

    lax.fori_loop(0, 4, group, 0)


def hidden(ref, c):
    return ref[pl.ds(c * SUB, SUB)].reshape(BLOCK, TOK)


def turn_back(swap, source, target, unit):
    def group(at, carry):
        tiles = [
            source[k * 16 : k * 16 + 16, pl.ds(pl.multiple_of(at * 16, 16), 16), :].reshape(256, TOK)
            for k in range(4)
        ]
        tiles = [dot(swap[...], tile).astype(BF).reshape(16, 16, TOK) for tile in tiles]
        for k, tile in enumerate(tiles):
            target[pl.ds(at * 16, 16), unit + k * 16 : unit + k * 16 + 16, :] = tile
        return carry

    lax.fori_loop(0, 4, group, 0)


def forward_second_kernel(swap, held, gate_in, up_in, act, to_gate, to_up, down_in, down_mid):
    down_mid[EACH:] = jnp.zeros((ROWS - EACH, NBD, TOK), BF)

    @loop(MINE, 2)
    def _(cs):
        gates = [dot_first(second_weight(held, 0, c), hidden(gate_in, c)) for c in cs]
        ups = [dot_first(second_weight(held, 1, c), hidden(up_in, c)) for c in cs]
        sigmas = [jax.nn.sigmoid(g) for g in gates]
        acts = [(g * s * u).astype(BF) for g, s, u in zip(gates, sigmas, ups)]
        downs = [dot_first(second_weight(held, 2, c), a) for c, a in zip(cs, acts)]
        for c, g, s, u, a, d in zip(cs, gates, sigmas, ups, acts, downs):
            to_gate[c], to_up[c], act[c] = u * s * (1.0 + g * (1.0 - s)), g * s, a
            down_mid[pl.ds(c * SUB, SUB)] = d.astype(BF).reshape(SUB, NBD, TOK)

    turn_back(swap, down_mid, down_in, 0)


def backward_kernel(where, swap, held_first, held_second, to_gate, to_up, *refs):
    shards = refs[:16]
    dy, back_in, gate_back, up_back, low, parts, mid, low_g, low_u = refs[16:]
    collect(where, shards, dy)
    low_g[EACH:] = jnp.zeros((ROWS - EACH, NBD, TOK), BF)
    low_u[EACH:] = jnp.zeros((ROWS - EACH, NBD, TOK), BF)

    def group(at, carry):
        @loop(16, 4)
        def _(ks):
            mids = [dot(first_weight(held_first, 2, at * 16 + k), dy[at * 16 + k]).astype(BF) for k in ks]
            for value, k in zip(mids, ks):
                mid[k] = value

        turn(swap, mid, back_in, pl.multiple_of(at * 16, 16))
        return carry

    lax.fori_loop(0, 4, group, 0)

    @loop(MINE, 2)
    def _(cs):
        grads = [dot(second_weight(held_second, 2, c), hidden(back_in, c)) for c in cs]
        to_gates = [(grad * to_gate[c]).astype(BF) for c, grad in zip(cs, grads)]
        to_ups = [(grad * to_up[c]).astype(BF) for c, grad in zip(cs, grads)]
        lows_g = [dot(second_weight(held_second, 0, c), v) for c, v in zip(cs, to_gates)]
        lows_u = [dot(second_weight(held_second, 1, c), v) for c, v in zip(cs, to_ups)]
        for c, g, u, lg, lu in zip(cs, to_gates, to_ups, lows_g, lows_u):
            gate_back[c], up_back[c] = g, u
            low_g[pl.ds(c * SUB, SUB)] = lg.astype(BF).reshape(SUB, NBD, TOK)
            low_u[pl.ds(c * SUB, SUB)] = lu.astype(BF).reshape(SUB, NBD, TOK)

    turn_back(swap, low_g, low, 0)
    turn_back(swap, low_u, low, ROWS)

    @loop(NBD, 4)
    def _(blocks):
        weights = [
            jnp.concatenate([first_weight(held_first, 0, i), first_weight(held_first, 1, i)]) for i in blocks
        ]
        values = [dot_first(w, low[i]).astype(BF) for w, i in zip(weights, blocks)]
        for i, value in zip(blocks, values):
            side, at = i // 32, i % 32
            parts[(at // PER) * 8 + side * PER + at % PER] = value


def put(keep, send, core, index, even, odd):
    keep[index] = jnp.where(core == 0, even, odd).astype(BF)
    send[index] = jnp.where(core == 0, odd, even).astype(BF)


def put_rows(keep, send, core, side, at, value):
    for pair in range(8):
        rows = value[pair * 16 : pair * 16 + 16]
        put(keep, send, core, (pair, side, at), rows[:8], rows[8:])


def second_grads_kernel(
    where, dy, down_in, act, back_in, gate_in, up_in, gate_back, up_back, keep, send
):
    step, core = pl.program_id(0), where[2]

    @pl.when(step < MINE // 2)
    def _():
        grads = []
        for k in range(2):
            rows = slice(k * SUB, k * SUB + SUB)
            grads.append(
                (
                    dot_last(gate_in[rows].reshape(BLOCK, TOK), gate_back[k]),
                    dot_last(up_in[rows].reshape(BLOCK, TOK), up_back[k]),
                    dot_last(act[k], back_in[rows].reshape(BLOCK, TOK)),
                )
            )
        for k in range(2):
            c = step * 2 + k
            for kind in range(3):
                put_rows(keep, send, core, c // HID, kind * HID + c % HID, grads[k][kind])

    fill = jnp.zeros((4, BLOCK), F32)
    grads = [dot_last(down_in[k], dy[k]) for k in range(PER)]
    side, z = step // 8, step % 8
    for p, grad in enumerate(grads):
        even, odd = [jnp.concatenate([grad[g * 28 : g * 28 + 28], fill]) for g in range(2)]
        for k in range(4):
            rows = slice(k * 8, k * 8 + 8)
            put(keep, send, core, (z, side, 3 * HID + p * 4 + k), even[rows], odd[rows])


def first_grads_kernel(where, x, low, keep, send):
    step, core = pl.program_id(0), where[2]
    grads = [dot_last(x[k], low[k]) for k in range(8)]
    for k, grad in enumerate(grads):
        i = step * 8 + k
        put_rows(keep, send, core, i // 32, i % 32, grad)


def call(kernel, outs, scratch, flops, *args):
    shapes = [jax.ShapeDtypeStruct(shape, dtype) for shape, dtype in outs]
    moved = sum(a.size * a.dtype.itemsize for a in args)
    return pl.pallas_call(
        kernel,
        out_shape=shapes,
        in_specs=[SM if a.dtype == jnp.int32 else VM for a in args],
        out_specs=[VM] * len(outs),
        scratch_shapes=[pltpu.VMEM(shape, dtype) for shape, dtype in scratch],
        compiler_params=pltpu.CompilerParams(vmem_limit_bytes=48 << 20),
        cost_estimate=pl.CostEstimate(flops=flops, bytes_accessed=moved, transcendentals=0),
    )(*args)


HIDDEN = ((MINE, BLOCK, TOK), BF)
WIDER = ((MINE, BLOCK, TOK), F32)
SPREAD = ((ROWS, NBD, TOK), BF)
MODEL = ((NBD, BLOCK, TOK), BF)
TILE = ((16, ROWS, TOK), BF)
ONE = 2 * 448 * 4 * 128 * 512


def swap_table():
    at = np.arange(256)
    table = np.zeros((256, 256), np.float32)
    table[at, at % 16 * 16 + at // 16] = 1.0
    return jnp.asarray(table, BF)


def forward_first(where, swap, held, shards):
    return call(forward_first_kernel, [MODEL, SPREAD, SPREAD], [TILE, TILE], 6 * ONE, where, swap, held, *shards)


def forward_second(swap, held, gate_in, up_in):
    outs = [HIDDEN, WIDER, WIDER, SPREAD]
    return call(forward_second_kernel, outs, [SPREAD], 5 * ONE, swap, held, gate_in, up_in)


def backward(where, swap, held_first, held_second, to_gate, to_up, shards):
    return call(
        backward_kernel,
        [MODEL, SPREAD, HIDDEN, HIDDEN, MODEL, MODEL],
        [TILE, SPREAD, SPREAD],
        12 * ONE,
        where, swap, held_first, held_second, to_gate, to_up, *shards,
    )


def blocks_of(array, count, last=None):
    def index(step):
        return (step if last is None else jnp.minimum(step, last),) + (0,) * (array.ndim - 1)

    return pl.BlockSpec((count,) + array.shape[1:], index)


def grads_call(kernel, steps, specs, blocks, flops, where, *args):
    shape = (8, 2, blocks, 8, BLOCK)
    moved = sum(a.size * a.dtype.itemsize for a in args)
    return pl.pallas_call(
        kernel,
        grid=(steps,),
        out_shape=[jax.ShapeDtypeStruct(shape, BF)] * 2,
        in_specs=[SM] + specs,
        out_specs=[pl.BlockSpec(shape, lambda step: (0,) * 5)] * 2,
        compiler_params=pltpu.CompilerParams(vmem_limit_bytes=32 << 20),
        cost_estimate=pl.CostEstimate(flops=flops, bytes_accessed=moved, transcendentals=0),
    )(where, *args)


def second_grads(where, *args):
    specs = [blocks_of(a, PER) for a in args[:2]]
    last = MINE // 2 - 1
    specs += [blocks_of(a, 4 if a.shape[0] == NBD else 2, last) for a in args[2:]]
    return grads_call(second_grads_kernel, NBD // PER, specs, 3 * HID + 16, 4 * ONE, where, *args)


def first_grads(where, x, low):
    return grads_call(first_grads_kernel, 8, [blocks_of(x, 8), blocks_of(low, 8)], 32, 2 * ONE, where, x, low)


GROUP = ("y", "x_lo", "core")
CHIPS = ("y", "x_lo", "x_hi")
TENSOR = ("x_hi", "z")


def size(name):
    return lax.axis_size(name)


def shift(value, step):
    count = size("z")
    return lax.ppermute(value, "z", [(i, (i + step) % count) for i in range(count)])


def swap(value):
    return lax.ppermute(value, "x_hi", [(0, 1), (1, 0)])


def halves(array, me):
    blocks = array.shape[0] // BLOCK
    half = array.shape[1] // 2
    own = lax.dynamic_slice_in_dim(array, me * half, half, 1)
    other = swap(lax.dynamic_slice_in_dim(array, (1 - me) * half, half, 1))
    return own.reshape(blocks, BLOCK, half), other.reshape(blocks, BLOCK, half)


def ring_gather(own, other):
    count = size("z")
    found = [[None, None] for _ in range(count)]
    found[0] = [own, other]
    right, left = [own, other], [own, other]
    for step in range(1, count // 2):
        for k in range(2):
            right[k], left[k] = shift(right[k], 1), shift(left[k], -1)
            found[count - step][k], found[step][k] = right[k], left[k]
    found[count // 2] = [shift(right[0], 1), shift(left[1], -1)]
    return [shard for pair in found for shard in pair]


def sum_groups(keep, send):
    found = lax.ppermute(send, "core", [(0, 1), (1, 0)])
    pairs = (keep.astype(F32) + found.astype(F32)).astype(BF)
    pairs = pairs.reshape((-1,) + pairs.shape[2:])
    return lax.all_to_all(pairs, CHIPS, 0, 0, tiled=True)


def total_of(chips):
    return jnp.sum(chips.astype(F32), axis=0)


def gather_first(gate_first, up_first, down_second, after):
    nh, nz = size("x_hi"), size("z")
    y, kind = lax.axis_index("y"), lax.axis_index(("x_lo", "core"))
    for value in after:
        y = y + (value[0, 0, 0].astype(F32) * 0.0).astype(jnp.int32)
    each = gate_first.shape[2] // (nh * nz)
    take = functools.partial(lax.dynamic_index_in_dim, index=y, axis=0, keepdims=False)
    gate, up = take(gate_first).T, take(up_first).T
    first = jnp.where(kind == 0, gate, jnp.where(kind == 1, up, take(down_second)))
    first = first.reshape(nh, nz, each, BLOCK).transpose(1, 0, 2, 3).reshape(nz, nh * each, BLOCK)
    first = jnp.pad(first, ((0, 0), (0, ROWS - nh * each), (0, 0)))
    first = jnp.broadcast_to(first[None], (nh,) + first.shape).reshape(nh * nz, ROWS, BLOCK)
    first = lax.all_to_all(first, TENSOR, 0, 0, tiled=True)
    return lax.all_gather(first, GROUP, axis=0, tiled=False)


def gather_second(gate_second, up_second, down_first):
    hid = gate_second.shape[0]
    d = lax.axis_index(GROUP)
    kind, at = d // 5, jnp.minimum((d % 5) * SLOTS, hid - SLOTS)
    take = functools.partial(lax.dynamic_slice_in_dim, start_index=at, slice_size=SLOTS, axis=0)
    second = jnp.where(
        kind == 0, take(gate_second), jnp.where(kind == 1, take(up_second), take(down_first))
    )
    group = GROUP + ("x_hi",)
    sent = jnp.broadcast_to(second[None], (lax.axis_size(group),) + second.shape)
    return lax.all_to_all(sent, group, 0, 0, tiled=True)


def shards(
    activations, cotangent, gate_first, up_first, gate_second, up_second, down_first, down_second
):
    tokens = activations.shape[1]
    per = gate_first.shape[0]
    wide = gate_first.shape[2]
    hid = gate_second.shape[0]
    ny, nx, nc, nh, nz = (size(a) for a in ("y", "x_lo", "core", "x_hi", "z"))
    ngroup = ny * nx * nc
    scale = (ngroup * tokens) ** (-0.5)
    me = lax.axis_index("x_hi")
    half = tokens // 2
    each = hid * SUB
    rows = BLOCK // ngroup

    where = jnp.stack([me, lax.axis_index("z"), lax.axis_index("core")]).astype(jnp.int32)
    table = swap_table()
    x_own, x_other = halves(activations, me)
    dy_own, dy_other = halves(cotangent, me)
    held_second = gather_second(gate_second, up_second, down_first)
    xs = ring_gather(x_own, x_other)
    after = [xs[3], xs[15], dy_other]
    held_first = gather_first(gate_first, up_first, down_second, after)
    (dy_own, dy_other), _ = lax.optimization_barrier(((dy_own, dy_other), (xs[2], xs[14])))
    dys = ring_gather(dy_own, dy_other)

    x, gate_in, up_in = forward_first(where, table, held_first, xs)
    act, to_gate, to_up, down_in = forward_second(table, held_second, gate_in, up_in)
    dy, back_in, gate_back, up_back, low, parts = backward(
        where, table, held_first, held_second, to_gate, to_up, dys
    )

    total = lax.psum_scatter(parts, "z", scatter_dimension=0, tiled=True)
    total = total.reshape(nh, per * BLOCK, half)
    kept = lax.dynamic_index_in_dim(total, me, 0, keepdims=False)
    other = swap(lax.dynamic_index_in_dim(total, 1 - me, 0, keepdims=False))

    firsts = sum_groups(*first_grads(where, x, low))
    later = sum_groups(
        *second_grads(where, dy, down_in, act, back_in, gate_in, up_in, gate_back, up_back)
    )
    later, other = lax.optimization_barrier((later, other))
    input_grad = jnp.concatenate(
        [jnp.where(me == 0, kept, other), jnp.where(me == 0, other, kept)], axis=1
    )
    later = total_of(later) * scale
    out_gs, out_us, out_df = later[: 3 * hid].reshape(3, hid, rows, BLOCK)
    pairs = []
    for part in range(ngroup):
        for z in range(nz):
            to_z, side = part // nh, part % nh
            pairs.append((part * nz + z, (side * nz + z) * nz + to_z))
    out_ds = lax.ppermute(later[3 * hid :], GROUP + ("z",), pairs)
    out_ds = out_ds.reshape(per, -1, BLOCK)[:, :each]

    firsts = total_of(firsts) * scale
    firsts = firsts.reshape(nz, per * rows, 2 * ROWS)
    firsts = lax.all_to_all(firsts, "z", 0, 0, tiled=True)
    firsts = firsts.reshape(nz, per, rows, 2, ROWS)[..., : nh * each]
    firsts = firsts.reshape(nz, per, rows, 2, nh, each).transpose(3, 1, 2, 4, 0, 5)
    out_gf, out_uf = firsts.reshape(2, per, rows, wide)
    return input_grad, out_gf, out_uf, out_gs, out_us, out_df, out_ds


def solution(mesh):
    fine = Mesh(mesh.devices.reshape(4, 2, 2, 2, 8), ("y", "x_lo", "core", "x_hi", "z"))
    arrays = P(TENSOR, GROUP)
    weights = P(TENSOR, None, None)
    return jax.shard_map(
        shards,
        mesh=fine,
        in_specs=(arrays, arrays) + (weights,) * 6,
        out_specs=(arrays,) + (P(TENSOR, GROUP, None),) * 6,
        check_vma=False,
    )
```

```python
import functools
import jax
import jax.numpy as jnp
import numpy as np
from jax import lax
from jax.experimental import pallas as pl
from jax.experimental.pallas import tpu as pltpu
from jax.sharding import Mesh
from jax.sharding import PartitionSpec as P

BLOCK = 128
SUB = 2
BF = jnp.bfloat16
F32 = jnp.float32
NBD = 64
HID = 14
MINE = 28
EACH = MINE * SUB
ROWS = 64
SLOTS = 3
PER = 4
TOK = 256
VM = pl.BlockSpec(memory_space=pltpu.VMEM)
SM = pl.BlockSpec(memory_space=pltpu.SMEM)


def first_weight(held, kind, i):
    return held[(i % PER) * 4 + kind, i // PER]


def second_weight(held, kind, c):
    side, own = c // HID, c % HID
    at = own // SLOTS
    slot = own - jnp.minimum(at * SLOTS, HID - SLOTS)
    start = 16 + (side * SLOTS + slot) * 2
    return held[kind * 5 + at, pl.ds(start, 2)].reshape(BLOCK, BLOCK)


def dot(left, right):
    return lax.dot_general(left, right, (((1,), (0,)), ((), ())), preferred_element_type=F32)


def dot_first(left, right):
    return lax.dot_general(left, right, (((0,), (0,)), ((), ())), preferred_element_type=F32)


def dot_last(left, right):
    return lax.dot_general(left, right, (((1,), (1,)), ((), ())), preferred_element_type=F32)


def loop(count, unroll):
    def run(body):
        def step(at, carry):
            body([at * unroll + k for k in range(unroll)])
            return carry

        lax.fori_loop(0, count // unroll, step, 0)

    return run


def collect(where, shards, out):
    me, z = where[0], where[1]
    for k, shard in enumerate(shards):
        side = me if k % 2 == 0 else 1 - me
        out[pl.ds(side * 32 + lax.rem(z + k // 2, 8) * PER, PER)] = shard[...]


def turn(swap, source, target, outer):
    tiles = [source[:, k * 16 : k * 16 + 16, :].reshape(256, TOK) for k in range(4)]
    tiles = [dot(swap[...], tile).astype(BF).reshape(16, 16, TOK) for tile in tiles]
    for k, tile in enumerate(tiles):
        target[k * 16 : k * 16 + 16, pl.ds(outer, 16), :] = tile


def forward_first_kernel(where, swap, held, *refs):
    shards, (x, gate_in, up_in, mid_g, mid_u) = refs[:16], refs[16:]
    collect(where, shards, x)

    def group(at, carry):
        @loop(16, 4)
        def _(ks):
            weights = [
                jnp.concatenate([first_weight(held, 0, at * 16 + k), first_weight(held, 1, at * 16 + k)])
                for k in ks
            ]
            mids = [dot(w, x[at * 16 + k]).astype(BF) for w, k in zip(weights, ks)]
            for mid, k in zip(mids, ks):
                mid_g[k] = mid[:ROWS]
                mid_u[k] = mid[ROWS:]

        outer = pl.multiple_of(at * 16, 16)
        turn(swap, mid_g, gate_in, outer)
        turn(swap, mid_u, up_in, outer)
        return carry

    lax.fori_loop(0, 4, group, 0)


def hidden(ref, c):
    return ref[pl.ds(c * SUB, SUB)].reshape(BLOCK, TOK)


def turn_back(swap, source, target, unit):
    def group(at, carry):
        tiles = [
            source[k * 16 : k * 16 + 16, pl.ds(pl.multiple_of(at * 16, 16), 16), :].reshape(256, TOK)
            for k in range(4)
        ]
        tiles = [dot(swap[...], tile).astype(BF).reshape(16, 16, TOK) for tile in tiles]
        for k, tile in enumerate(tiles):
            target[pl.ds(at * 16, 16), unit + k * 16 : unit + k * 16 + 16, :] = tile
        return carry

    lax.fori_loop(0, 4, group, 0)


def forward_second_kernel(swap, held, gate_in, up_in, act, to_gate, to_up, down_in, down_mid):
    down_mid[EACH:] = jnp.zeros((ROWS - EACH, NBD, TOK), BF)

    @loop(MINE, 2)
    def _(cs):
        gates = [dot_first(second_weight(held, 0, c), hidden(gate_in, c)) for c in cs]
        ups = [dot_first(second_weight(held, 1, c), hidden(up_in, c)) for c in cs]
        sigmas = [jax.nn.sigmoid(g) for g in gates]
        acts = [(g * s * u).astype(BF) for g, s, u in zip(gates, sigmas, ups)]
        downs = [dot_first(second_weight(held, 2, c), a) for c, a in zip(cs, acts)]
        for c, g, s, u, a, d in zip(cs, gates, sigmas, ups, acts, downs):
            to_gate[c], to_up[c], act[c] = u * s * (1.0 + g * (1.0 - s)), g * s, a
            down_mid[pl.ds(c * SUB, SUB)] = d.astype(BF).reshape(SUB, NBD, TOK)

    turn_back(swap, down_mid, down_in, 0)


def backward_kernel(where, swap, held, to_gate, to_up, *refs):
    shards = refs[:16]
    dy, back_in, gate_back, up_back, low, parts, mid, low_g, low_u = refs[16:]
    collect(where, shards, dy)
    low_g[EACH:] = jnp.zeros((ROWS - EACH, NBD, TOK), BF)
    low_u[EACH:] = jnp.zeros((ROWS - EACH, NBD, TOK), BF)

    def group(at, carry):
        @loop(16, 4)
        def _(ks):
            mids = [dot(first_weight(held, 2, at * 16 + k), dy[at * 16 + k]).astype(BF) for k in ks]
            for value, k in zip(mids, ks):
                mid[k] = value

        turn(swap, mid, back_in, pl.multiple_of(at * 16, 16))
        return carry

    lax.fori_loop(0, 4, group, 0)

    @loop(MINE, 2)
    def _(cs):
        grads = [dot(second_weight(held, 2, c), hidden(back_in, c)) for c in cs]
        to_gates = [(grad * to_gate[c]).astype(BF) for c, grad in zip(cs, grads)]
        to_ups = [(grad * to_up[c]).astype(BF) for c, grad in zip(cs, grads)]
        lows_g = [dot(second_weight(held, 0, c), v) for c, v in zip(cs, to_gates)]
        lows_u = [dot(second_weight(held, 1, c), v) for c, v in zip(cs, to_ups)]
        for c, g, u, lg, lu in zip(cs, to_gates, to_ups, lows_g, lows_u):
            gate_back[c], up_back[c] = g, u
            low_g[pl.ds(c * SUB, SUB)] = lg.astype(BF).reshape(SUB, NBD, TOK)
            low_u[pl.ds(c * SUB, SUB)] = lu.astype(BF).reshape(SUB, NBD, TOK)

    turn_back(swap, low_g, low, 0)
    turn_back(swap, low_u, low, ROWS)

    @loop(NBD, 4)
    def _(blocks):
        weights = [
            jnp.concatenate([first_weight(held, 0, i), first_weight(held, 1, i)]) for i in blocks
        ]
        values = [dot_first(w, low[i]).astype(BF) for w, i in zip(weights, blocks)]
        for i, value in zip(blocks, values):
            side, at = i // 32, i % 32
            parts[(at // PER) * 8 + side * PER + at % PER] = value


def put(keep, send, core, index, even, odd):
    keep[index] = jnp.where(core == 0, even, odd).astype(BF)
    send[index] = jnp.where(core == 0, odd, even).astype(BF)


def put_rows(keep, send, core, side, at, value):
    for pair in range(8):
        rows = value[pair * 16 : pair * 16 + 16]
        put(keep, send, core, (pair, side, at), rows[:8], rows[8:])


def grads_kernel(
    where, x, low, dy, down_in, act, back_in, gate_in, up_in, gate_back, up_back, keep, send
):
    step, core = pl.program_id(0), where[2]

    @pl.when(step < MINE // 2)
    def _():
        grads = []
        for k in range(2):
            rows = slice(k * SUB, k * SUB + SUB)
            grads.append(
                (
                    dot_last(gate_in[rows].reshape(BLOCK, TOK), gate_back[k]),
                    dot_last(up_in[rows].reshape(BLOCK, TOK), up_back[k]),
                    dot_last(act[k], back_in[rows].reshape(BLOCK, TOK)),
                )
            )
        for k in range(2):
            c = step * 2 + k
            for kind in range(3):
                put_rows(keep, send, core, c // HID, kind * HID + c % HID, grads[k][kind])

    fill = jnp.zeros((4, BLOCK), F32)
    grads = [dot_last(down_in[k], dy[k]) for k in range(PER)]
    firsts = [dot_last(x[k], low[k]) for k in range(PER)]
    side, z = step // 8, step % 8
    for p, grad in enumerate(grads):
        even, odd = [jnp.concatenate([grad[g * 28 : g * 28 + 28], fill]) for g in range(2)]
        for k in range(4):
            rows = slice(k * 8, k * 8 + 8)
            put(keep, send, core, (z, side, 3 * HID + p * 4 + k), even[rows], odd[rows])
    for p, grad in enumerate(firsts):
        put_rows(keep, send, core, side, 3 * HID + 16 + z * PER + p, grad)


def call(kernel, outs, scratch, flops, *args):
    shapes = [jax.ShapeDtypeStruct(shape, dtype) for shape, dtype in outs]
    moved = sum(a.size * a.dtype.itemsize for a in args)
    return pl.pallas_call(
        kernel,
        out_shape=shapes,
        in_specs=[SM if a.dtype == jnp.int32 else VM for a in args],
        out_specs=[VM] * len(outs),
        scratch_shapes=[pltpu.VMEM(shape, dtype) for shape, dtype in scratch],
        compiler_params=pltpu.CompilerParams(vmem_limit_bytes=48 << 20),
        cost_estimate=pl.CostEstimate(flops=flops, bytes_accessed=moved, transcendentals=0),
    )(*args)


HIDDEN = ((MINE, BLOCK, TOK), BF)
WIDER = ((MINE, BLOCK, TOK), F32)
SPREAD = ((ROWS, NBD, TOK), BF)
MODEL = ((NBD, BLOCK, TOK), BF)
TILE = ((16, ROWS, TOK), BF)
ONE = 2 * 448 * 4 * 128 * 512


def swap_table():
    at = np.arange(256)
    table = np.zeros((256, 256), np.float32)
    table[at, at % 16 * 16 + at // 16] = 1.0
    return jnp.asarray(table, BF)


def forward_first(where, swap, held, shards):
    return call(forward_first_kernel, [MODEL, SPREAD, SPREAD], [TILE, TILE], 6 * ONE, where, swap, held, *shards)


def forward_second(swap, held, gate_in, up_in):
    outs = [HIDDEN, WIDER, WIDER, SPREAD]
    return call(forward_second_kernel, outs, [SPREAD], 5 * ONE, swap, held, gate_in, up_in)


def backward(where, swap, held, to_gate, to_up, shards):
    return call(
        backward_kernel,
        [MODEL, SPREAD, HIDDEN, HIDDEN, MODEL, MODEL],
        [TILE, SPREAD, SPREAD],
        12 * ONE,
        where, swap, held, to_gate, to_up, *shards,
    )


def blocks_of(array, count, last=None):
    def index(step):
        return (step if last is None else jnp.minimum(step, last),) + (0,) * (array.ndim - 1)

    return pl.BlockSpec((count,) + array.shape[1:], index)


def grads(where, x, low, dy, down_in, act, back_in, gate_in, up_in, gate_back, up_back):
    last = MINE // 2 - 1
    args = (x, low, dy, down_in, act, back_in, gate_in, up_in, gate_back, up_back)
    specs = [blocks_of(a, PER) for a in args[:4]]
    specs += [blocks_of(a, 4 if a.shape[0] == ROWS else 2, last) for a in args[4:]]
    shape = (8, 2, 3 * HID + 16 + 32, 8, BLOCK)
    moved = sum(a.size * a.dtype.itemsize for a in args)
    return pl.pallas_call(
        grads_kernel,
        grid=(NBD // PER,),
        out_shape=[jax.ShapeDtypeStruct(shape, BF)] * 2,
        in_specs=[SM] + specs,
        out_specs=[pl.BlockSpec(shape, lambda step: (0,) * 5)] * 2,
        compiler_params=pltpu.CompilerParams(vmem_limit_bytes=32 << 20),
        cost_estimate=pl.CostEstimate(flops=6 * ONE, bytes_accessed=moved, transcendentals=0),
    )(where, *args)


GROUP = ("y", "x_lo", "core")
CHIPS = ("y", "x_lo", "x_hi")
TENSOR = ("x_hi", "z")


def size(name):
    return lax.axis_size(name)


def shift(value, step):
    count = size("z")
    return lax.ppermute(value, "z", [(i, (i + step) % count) for i in range(count)])


def swap(value):
    return lax.ppermute(value, "x_hi", [(0, 1), (1, 0)])


def halves(array, me):
    blocks = array.shape[0] // BLOCK
    half = array.shape[1] // 2
    own = lax.dynamic_slice_in_dim(array, me * half, half, 1)
    other = swap(lax.dynamic_slice_in_dim(array, (1 - me) * half, half, 1))
    return own.reshape(blocks, BLOCK, half), other.reshape(blocks, BLOCK, half)


def ring_gather(own, other):
    count = size("z")
    found = [[None, None] for _ in range(count)]
    found[0] = [own, other]
    right, left = [own, other], [own, other]
    for step in range(1, count // 2):
        for k in range(2):
            right[k], left[k] = shift(right[k], 1), shift(left[k], -1)
            found[count - step][k], found[step][k] = right[k], left[k]
    found[count // 2] = [shift(right[0], 1), shift(left[1], -1)]
    return [shard for pair in found for shard in pair]


def sum_groups(keep, send):
    found = lax.ppermute(send, "core", [(0, 1), (1, 0)])
    pairs = (keep.astype(F32) + found.astype(F32)).astype(BF)
    pairs = pairs.reshape((-1,) + pairs.shape[2:])
    return lax.all_to_all(pairs, CHIPS, 0, 0, tiled=True)


def total_of(chips):
    return jnp.sum(chips.astype(F32), axis=0)


def share_first(gate_first, up_first, down_second):
    nh, nz = size("x_hi"), size("z")
    y, kind = lax.axis_index("y"), lax.axis_index(("x_lo", "core"))
    each = gate_first.shape[2] // (nh * nz)
    take = functools.partial(lax.dynamic_index_in_dim, index=y, axis=0, keepdims=False)
    gate, up = take(gate_first).T, take(up_first).T
    first = jnp.where(kind == 0, gate, jnp.where(kind == 1, up, take(down_second)))
    first = first.reshape(nh, nz, each, BLOCK).transpose(1, 0, 2, 3).reshape(nz, nh * each, BLOCK)
    first = jnp.pad(first, ((0, 0), (0, ROWS - nh * each), (0, 0)))
    first = jnp.broadcast_to(first[None], (nh,) + first.shape).reshape(nh * nz, ROWS, BLOCK)
    return lax.all_to_all(first, TENSOR, 0, 0, tiled=True)


def share_second(gate_second, up_second, down_first):
    hid = gate_second.shape[0]
    d = lax.axis_index(GROUP)
    kind, at = d // 5, jnp.minimum((d % 5) * SLOTS, hid - SLOTS)
    take = functools.partial(lax.dynamic_slice_in_dim, start_index=at, slice_size=SLOTS, axis=0)
    second = jnp.where(
        kind == 0, take(gate_second), jnp.where(kind == 1, take(up_second), take(down_first))
    )
    other = swap(second)
    me = lax.axis_index("x_hi")
    second = jnp.concatenate([jnp.where(me == 0, second, other), jnp.where(me == 0, other, second)])
    return second.reshape(-1, ROWS, BLOCK)


def shards(
    activations, cotangent, gate_first, up_first, gate_second, up_second, down_first, down_second
):
    tokens = activations.shape[1]
    per = gate_first.shape[0]
    wide = gate_first.shape[2]
    hid = gate_second.shape[0]
    ny, nx, nc, nh, nz = (size(a) for a in ("y", "x_lo", "core", "x_hi", "z"))
    ngroup = ny * nx * nc
    scale = (ngroup * tokens) ** (-0.5)
    me = lax.axis_index("x_hi")
    half = tokens // 2
    each = hid * SUB
    rows = BLOCK // ngroup

    where = jnp.stack([me, lax.axis_index("z"), lax.axis_index("core")]).astype(jnp.int32)
    table = swap_table()
    x_own, x_other = halves(activations, me)
    dy_own, dy_other = halves(cotangent, me)
    xs = ring_gather(x_own, x_other)
    dys = ring_gather(dy_own, dy_other)
    weights = (gate_first, up_first, down_second)
    begun = (x_other, dy_other, xs[2], xs[14], dys[2], dys[14])
    weights, _ = lax.optimization_barrier((weights, begun))
    first = share_first(*weights)
    second = share_second(gate_second, up_second, down_first)
    held = lax.all_gather(jnp.concatenate([first, second]), GROUP, axis=0, tiled=False)

    x, gate_in, up_in = forward_first(where, table, held, xs)
    act, to_gate, to_up, down_in = forward_second(table, held, gate_in, up_in)
    dy, back_in, gate_back, up_back, low, parts = backward(where, table, held, to_gate, to_up, dys)

    total = lax.psum_scatter(parts, "z", scatter_dimension=0, tiled=True)
    total = total.reshape(nh, per * BLOCK, half)
    kept = lax.dynamic_index_in_dim(total, me, 0, keepdims=False)
    other = swap(lax.dynamic_index_in_dim(total, 1 - me, 0, keepdims=False))

    chips = sum_groups(
        *grads(where, x, low, dy, down_in, act, back_in, gate_in, up_in, gate_back, up_back)
    )
    input_grad = jnp.concatenate(
        [jnp.where(me == 0, kept, other), jnp.where(me == 0, other, kept)], axis=1
    )
    summed = total_of(chips) * scale
    later, firsts = summed[: 3 * hid + 16], summed[3 * hid + 16 :]
    out_gs, out_us, out_df = later[: 3 * hid].reshape(3, hid, rows, BLOCK)
    pairs = []
    for part in range(ngroup):
        for z in range(nz):
            to_z, side = part // nh, part % nh
            pairs.append((part * nz + z, (side * nz + z) * nz + to_z))
    out_ds = lax.ppermute(later[3 * hid :], GROUP + ("z",), pairs)
    out_ds = out_ds.reshape(per, -1, BLOCK)[:, :each]

    firsts = firsts.reshape(nz, per * rows, 2 * ROWS)
    firsts = lax.all_to_all(firsts, "z", 0, 0, tiled=True)
    firsts = firsts.reshape(nz, per, rows, 2, ROWS)[..., : nh * each]
    firsts = firsts.reshape(nz, per, rows, 2, nh, each).transpose(3, 1, 2, 4, 0, 5)
    out_gf, out_uf = firsts.reshape(2, per, rows, wide)
    return input_grad, out_gf, out_uf, out_gs, out_us, out_df, out_ds


def solution(mesh):
    fine = Mesh(mesh.devices.reshape(4, 2, 2, 2, 8), ("y", "x_lo", "core", "x_hi", "z"))
    arrays = P(TENSOR, GROUP)
    weights = P(TENSOR, None, None)
    return jax.shard_map(
        shards,
        mesh=fine,
        in_specs=(arrays, arrays) + (weights,) * 6,
        out_specs=(arrays,) + (P(TENSOR, GROUP, None),) * 6,
        check_vma=False,
    )
```

```python
import functools
import jax
import jax.numpy as jnp
import numpy as np
from jax import lax
from jax.experimental import pallas as pl
from jax.experimental.pallas import tpu as pltpu
from jax.sharding import Mesh
from jax.sharding import PartitionSpec as P

BLOCK = 128
SUB = 2
BF = jnp.bfloat16
F32 = jnp.float32
NBD = 64
HID = 14
MINE = 28
EACH = MINE * SUB
ROWS = 64
SLOTS = 3
PER = 4
TOK = 256
VM = pl.BlockSpec(memory_space=pltpu.VMEM)
SM = pl.BlockSpec(memory_space=pltpu.SMEM)


def first_weight(held, kind, i):
    return held[(i % PER) * 4 + kind, i // PER]


def second_weight(held, kind, c):
    side, own = c // HID, c % HID
    at = own // SLOTS
    slot = own - jnp.minimum(at * SLOTS, HID - SLOTS)
    start = 16 + (side * SLOTS + slot) * 2
    return held[kind * 5 + at, pl.ds(start, 2)].reshape(BLOCK, BLOCK)


def dot(left, right):
    return lax.dot_general(left, right, (((1,), (0,)), ((), ())), preferred_element_type=F32)


def dot_first(left, right):
    return lax.dot_general(left, right, (((0,), (0,)), ((), ())), preferred_element_type=F32)


def dot_last(left, right):
    return lax.dot_general(left, right, (((1,), (1,)), ((), ())), preferred_element_type=F32)


def loop(count, unroll):
    def run(body):
        def step(at, carry):
            body([at * unroll + k for k in range(unroll)])
            return carry

        lax.fori_loop(0, count // unroll, step, 0)

    return run


def collect(where, shards, out):
    me, z = where[0], where[1]
    for k, shard in enumerate(shards):
        side = me if k % 2 == 0 else 1 - me
        out[pl.ds(side * 32 + lax.rem(z + k // 2, 8) * PER, PER)] = shard[...]


def turn(swap, source, target, outer):
    tiles = [source[:, k * 16 : k * 16 + 16, :].reshape(256, TOK) for k in range(4)]
    tiles = [dot(swap[...], tile).astype(BF).reshape(16, 16, TOK) for tile in tiles]
    for k, tile in enumerate(tiles):
        target[k * 16 : k * 16 + 16, pl.ds(outer, 16), :] = tile


def forward_first_kernel(where, swap, held, *refs):
    shards, (x, gate_in, up_in, mid_g, mid_u) = refs[:16], refs[16:]
    collect(where, shards, x)

    def group(at, carry):
        @loop(16, 4)
        def _(ks):
            weights = [
                jnp.concatenate([first_weight(held, 0, at * 16 + k), first_weight(held, 1, at * 16 + k)])
                for k in ks
            ]
            mids = [dot(w, x[at * 16 + k]).astype(BF) for w, k in zip(weights, ks)]
            for mid, k in zip(mids, ks):
                mid_g[k] = mid[:ROWS]
                mid_u[k] = mid[ROWS:]

        outer = pl.multiple_of(at * 16, 16)
        turn(swap, mid_g, gate_in, outer)
        turn(swap, mid_u, up_in, outer)
        return carry

    lax.fori_loop(0, 4, group, 0)


def hidden(ref, c):
    return ref[pl.ds(c * SUB, SUB)].reshape(BLOCK, TOK)


def turn_back(swap, source, target, unit):
    def group(at, carry):
        tiles = [
            source[k * 16 : k * 16 + 16, pl.ds(pl.multiple_of(at * 16, 16), 16), :].reshape(256, TOK)
            for k in range(4)
        ]
        tiles = [dot(swap[...], tile).astype(BF).reshape(16, 16, TOK) for tile in tiles]
        for k, tile in enumerate(tiles):
            target[pl.ds(at * 16, 16), unit + k * 16 : unit + k * 16 + 16, :] = tile
        return carry

    lax.fori_loop(0, 4, group, 0)


def forward_second_kernel(swap, held, gate_in, up_in, act, to_gate, to_up, down_in, down_mid):
    down_mid[EACH:] = jnp.zeros((ROWS - EACH, NBD, TOK), BF)

    @loop(MINE, 2)
    def _(cs):
        gates = [dot_first(second_weight(held, 0, c), hidden(gate_in, c)) for c in cs]
        ups = [dot_first(second_weight(held, 1, c), hidden(up_in, c)) for c in cs]
        sigmas = [jax.nn.sigmoid(g) for g in gates]
        acts = [(g * s * u).astype(BF) for g, s, u in zip(gates, sigmas, ups)]
        downs = [dot_first(second_weight(held, 2, c), a) for c, a in zip(cs, acts)]
        for c, g, s, u, a, d in zip(cs, gates, sigmas, ups, acts, downs):
            to_gate[c], to_up[c], act[c] = u * s * (1.0 + g * (1.0 - s)), g * s, a
            down_mid[pl.ds(c * SUB, SUB)] = d.astype(BF).reshape(SUB, NBD, TOK)

    turn_back(swap, down_mid, down_in, 0)


def backward_kernel(where, swap, held, to_gate, to_up, *refs):
    shards = refs[:16]
    dy, back_in, gate_back, up_back, low, parts, mid, low_g, low_u = refs[16:]
    collect(where, shards, dy)
    low_g[EACH:] = jnp.zeros((ROWS - EACH, NBD, TOK), BF)
    low_u[EACH:] = jnp.zeros((ROWS - EACH, NBD, TOK), BF)

    def group(at, carry):
        @loop(16, 4)
        def _(ks):
            mids = [dot(first_weight(held, 2, at * 16 + k), dy[at * 16 + k]).astype(BF) for k in ks]
            for value, k in zip(mids, ks):
                mid[k] = value

        turn(swap, mid, back_in, pl.multiple_of(at * 16, 16))
        return carry

    lax.fori_loop(0, 4, group, 0)

    @loop(MINE, 2)
    def _(cs):
        grads = [dot(second_weight(held, 2, c), hidden(back_in, c)) for c in cs]
        to_gates = [(grad * to_gate[c]).astype(BF) for c, grad in zip(cs, grads)]
        to_ups = [(grad * to_up[c]).astype(BF) for c, grad in zip(cs, grads)]
        lows_g = [dot(second_weight(held, 0, c), v) for c, v in zip(cs, to_gates)]
        lows_u = [dot(second_weight(held, 1, c), v) for c, v in zip(cs, to_ups)]
        for c, g, u, lg, lu in zip(cs, to_gates, to_ups, lows_g, lows_u):
            gate_back[c], up_back[c] = g, u
            low_g[pl.ds(c * SUB, SUB)] = lg.astype(BF).reshape(SUB, NBD, TOK)
            low_u[pl.ds(c * SUB, SUB)] = lu.astype(BF).reshape(SUB, NBD, TOK)

    turn_back(swap, low_g, low, 0)
    turn_back(swap, low_u, low, ROWS)

    @loop(NBD, 4)
    def _(blocks):
        weights = [
            jnp.concatenate([first_weight(held, 0, i), first_weight(held, 1, i)]) for i in blocks
        ]
        values = [dot_first(w, low[i]).astype(BF) for w, i in zip(weights, blocks)]
        for i, value in zip(blocks, values):
            side, at = i // 32, i % 32
            parts[(at // PER) * 8 + side * PER + at % PER] = value


def put(keep, send, core, index, even, odd):
    keep[index] = jnp.where(core == 0, even, odd).astype(BF)
    send[index] = jnp.where(core == 0, odd, even).astype(BF)


def put_rows(keep, send, core, side, at, value):
    for pair in range(8):
        rows = value[pair * 16 : pair * 16 + 16]
        put(keep, send, core, (pair, side, at), rows[:8], rows[8:])


def grads_kernel(
    where, x, low, dy, down_in, act, back_in, gate_in, up_in, gate_back, up_back, keep, send
):
    step, core = pl.program_id(0), where[2]

    @pl.when(step < MINE // 2)
    def _():
        grads = []
        for k in range(2):
            rows = slice(k * SUB, k * SUB + SUB)
            grads.append(
                (
                    dot_last(gate_in[rows].reshape(BLOCK, TOK), gate_back[k]),
                    dot_last(up_in[rows].reshape(BLOCK, TOK), up_back[k]),
                    dot_last(act[k], back_in[rows].reshape(BLOCK, TOK)),
                )
            )
        for k in range(2):
            c = step * 2 + k
            for kind in range(3):
                put_rows(keep, send, core, c // HID, kind * HID + c % HID, grads[k][kind])

    fill = jnp.zeros((4, BLOCK), F32)
    grads = [dot_last(down_in[k], dy[k]) for k in range(PER)]
    firsts = [dot_last(x[k], low[k]) for k in range(PER)]
    side, z = step // 8, step % 8
    for p, grad in enumerate(grads):
        even, odd = [jnp.concatenate([grad[g * 28 : g * 28 + 28], fill]) for g in range(2)]
        for k in range(4):
            rows = slice(k * 8, k * 8 + 8)
            put(keep, send, core, (z, side, 3 * HID + p * 4 + k), even[rows], odd[rows])
    for p, grad in enumerate(firsts):
        put_rows(keep, send, core, side, 3 * HID + 16 + z * PER + p, grad)


def call(kernel, outs, scratch, flops, *args):
    shapes = [jax.ShapeDtypeStruct(shape, dtype) for shape, dtype in outs]
    moved = sum(a.size * a.dtype.itemsize for a in args)
    return pl.pallas_call(
        kernel,
        out_shape=shapes,
        in_specs=[SM if a.dtype == jnp.int32 else VM for a in args],
        out_specs=[VM] * len(outs),
        scratch_shapes=[pltpu.VMEM(shape, dtype) for shape, dtype in scratch],
        compiler_params=pltpu.CompilerParams(vmem_limit_bytes=60 << 20),
        cost_estimate=pl.CostEstimate(flops=flops, bytes_accessed=moved, transcendentals=0),
    )(*args)


HIDDEN = ((MINE, BLOCK, TOK), BF)
WIDER = ((MINE, BLOCK, TOK), F32)
SPREAD = ((ROWS, NBD, TOK), BF)
MODEL = ((NBD, BLOCK, TOK), BF)
TILE = ((16, ROWS, TOK), BF)
ONE = 2 * 448 * 4 * 128 * 512


def swap_table():
    at = np.arange(256)
    table = np.zeros((256, 256), np.float32)
    table[at, at % 16 * 16 + at // 16] = 1.0
    return jnp.asarray(table, BF)


def forward_first(where, swap, held, shards):
    return call(forward_first_kernel, [MODEL, SPREAD, SPREAD], [TILE, TILE], 6 * ONE, where, swap, held, *shards)


def forward_second(swap, held, gate_in, up_in):
    outs = [HIDDEN, WIDER, WIDER, SPREAD]
    return call(forward_second_kernel, outs, [SPREAD], 5 * ONE, swap, held, gate_in, up_in)


def backward(where, swap, held, to_gate, to_up, shards):
    return call(
        backward_kernel,
        [MODEL, SPREAD, HIDDEN, HIDDEN, MODEL, MODEL],
        [TILE, SPREAD, SPREAD],
        12 * ONE,
        where, swap, held, to_gate, to_up, *shards,
    )


def blocks_of(array, count, last=None):
    def index(step):
        return (step if last is None else jnp.minimum(step, last),) + (0,) * (array.ndim - 1)

    return pl.BlockSpec((count,) + array.shape[1:], index)


def grads(where, x, low, dy, down_in, act, back_in, gate_in, up_in, gate_back, up_back):
    last = MINE // 2 - 1
    args = (x, low, dy, down_in, act, back_in, gate_in, up_in, gate_back, up_back)
    specs = [blocks_of(a, PER) for a in args[:4]]
    specs += [blocks_of(a, 4 if a.shape[0] == ROWS else 2, last) for a in args[4:]]
    shape = (8, 2, 3 * HID + 16 + 32, 8, BLOCK)
    moved = sum(a.size * a.dtype.itemsize for a in args)
    return pl.pallas_call(
        grads_kernel,
        grid=(NBD // PER,),
        out_shape=[jax.ShapeDtypeStruct(shape, BF)] * 2,
        in_specs=[SM] + specs,
        out_specs=[pl.BlockSpec(shape, lambda step: (0,) * 5)] * 2,
        compiler_params=pltpu.CompilerParams(vmem_limit_bytes=60 << 20),
        cost_estimate=pl.CostEstimate(flops=6 * ONE, bytes_accessed=moved, transcendentals=0),
    )(where, *args)


GROUP = ("y", "x_lo", "core")
CHIPS = ("y", "x_lo", "x_hi")
TENSOR = ("x_hi", "z")


def size(name):
    return lax.axis_size(name)


def shift(value, step):
    count = size("z")
    return lax.ppermute(value, "z", [(i, (i + step) % count) for i in range(count)])


def swap(value):
    return lax.ppermute(value, "x_hi", [(0, 1), (1, 0)])


def halves(array, me):
    blocks = array.shape[0] // BLOCK
    half = array.shape[1] // 2
    own = lax.dynamic_slice_in_dim(array, me * half, half, 1)
    other = swap(lax.dynamic_slice_in_dim(array, (1 - me) * half, half, 1))
    return own.reshape(blocks, BLOCK, half), other.reshape(blocks, BLOCK, half)


def ring_step(step, right, left, found):
    count = size("z")
    if step < count // 2:
        right, left = [shift(v, 1) for v in right], [shift(v, -1) for v in left]
        found[count - step], found[step] = right, left
    else:
        found[step] = [shift(right[0], 1), shift(left[1], -1)]
    return right, left


def flat(found):
    return [shard for step in range(size("z")) for shard in found[step]]


def sum_groups(keep, send):
    found = lax.ppermute(send, "core", [(0, 1), (1, 0)])
    pairs = (keep.astype(F32) + found.astype(F32)).astype(BF)
    pairs = pairs.reshape((-1,) + pairs.shape[2:])
    return lax.all_to_all(pairs, CHIPS, 0, 0, tiled=True)


def total_of(chips):
    return jnp.sum(chips.astype(F32), axis=0)


def share_first(gate_first, up_first, down_second):
    nh, nz = size("x_hi"), size("z")
    y, kind = lax.axis_index("y"), lax.axis_index(("x_lo", "core"))
    each = gate_first.shape[2] // (nh * nz)
    take = functools.partial(lax.dynamic_index_in_dim, index=y, axis=0, keepdims=False)
    gate, up = take(gate_first).T, take(up_first).T
    first = jnp.where(kind == 0, gate, jnp.where(kind == 1, up, take(down_second)))
    first = first.reshape(nh, nz, each, BLOCK).transpose(1, 0, 2, 3).reshape(nz, nh * each, BLOCK)
    first = jnp.pad(first, ((0, 0), (0, ROWS - nh * each), (0, 0)))
    first = jnp.broadcast_to(first[None], (nh,) + first.shape).reshape(nh * nz, ROWS, BLOCK)
    return lax.all_to_all(first, TENSOR, 0, 0, tiled=True)


def share_second(gate_second, up_second, down_first):
    hid = gate_second.shape[0]
    d = lax.axis_index(GROUP)
    kind, at = d // 5, jnp.minimum((d % 5) * SLOTS, hid - SLOTS)
    take = functools.partial(lax.dynamic_slice_in_dim, start_index=at, slice_size=SLOTS, axis=0)
    second = jnp.where(
        kind == 0, take(gate_second), jnp.where(kind == 1, take(up_second), take(down_first))
    )
    other = swap(second)
    me = lax.axis_index("x_hi")
    second = jnp.concatenate([jnp.where(me == 0, second, other), jnp.where(me == 0, other, second)])
    return second.reshape(-1, ROWS, BLOCK)


def shards(
    activations, cotangent, gate_first, up_first, gate_second, up_second, down_first, down_second
):
    tokens = activations.shape[1]
    per = gate_first.shape[0]
    wide = gate_first.shape[2]
    hid = gate_second.shape[0]
    ny, nx, nc, nh, nz = (size(a) for a in ("y", "x_lo", "core", "x_hi", "z"))
    ngroup = ny * nx * nc
    scale = (ngroup * tokens) ** (-0.5)
    me = lax.axis_index("x_hi")
    half = tokens // 2
    each = hid * SUB
    rows = BLOCK // ngroup

    where = jnp.stack([me, lax.axis_index("z"), lax.axis_index("core")]).astype(jnp.int32)
    table = swap_table()
    x_own, x_other = halves(activations, me)
    dy_own, dy_other = halves(cotangent, me)
    first = share_first(gate_first, up_first, down_second)
    second = share_second(gate_second, up_second, down_first)
    held = lax.all_gather(jnp.concatenate([first, second]), GROUP, axis=0, tiled=False)

    steps = nz // 2
    xs, dys = {0: [x_own, x_other]}, {0: [dy_own, dy_other]}
    state = (xs[0], xs[0])
    for step in range(1, steps + 1):
        state = ring_step(step, *state, xs)
    state, _ = lax.optimization_barrier(((dys[0], dys[0]), (xs[2], xs[nz - 2])))
    for step in range(1, steps - 1):
        state = ring_step(step, *state, dys)
    shards_x, _ = lax.optimization_barrier((flat(xs), state))
    x, gate_in, up_in = forward_first(where, table, held, shards_x)
    state = ring_step(steps - 1, *state, dys)
    state, gate_in, up_in = lax.optimization_barrier((state, gate_in, up_in))
    ring_step(steps, *state, dys)
    act, to_gate, to_up, down_in = forward_second(table, held, gate_in, up_in)
    dy, back_in, gate_back, up_back, low, parts = backward(
        where, table, held, to_gate, to_up, flat(dys)
    )

    total = lax.psum_scatter(parts, "z", scatter_dimension=0, tiled=True)
    total = total.reshape(nh, per * BLOCK, half)
    kept = lax.dynamic_index_in_dim(total, me, 0, keepdims=False)
    other = swap(lax.dynamic_index_in_dim(total, 1 - me, 0, keepdims=False))

    chips = sum_groups(
        *grads(where, x, low, dy, down_in, act, back_in, gate_in, up_in, gate_back, up_back)
    )
    input_grad = jnp.concatenate(
        [jnp.where(me == 0, kept, other), jnp.where(me == 0, other, kept)], axis=1
    )
    summed = total_of(chips) * scale
    later, firsts = summed[: 3 * hid + 16], summed[3 * hid + 16 :]
    out_gs, out_us, out_df = later[: 3 * hid].reshape(3, hid, rows, BLOCK)
    pairs = []
    for part in range(ngroup):
        for z in range(nz):
            to_z, side = part // nh, part % nh
            pairs.append((part * nz + z, (side * nz + z) * nz + to_z))
    out_ds = lax.ppermute(later[3 * hid :], GROUP + ("z",), pairs)
    out_ds = out_ds.reshape(per, -1, BLOCK)[:, :each]

    firsts = firsts.reshape(nz, per * rows, 2 * ROWS)
    firsts = lax.all_to_all(firsts, "z", 0, 0, tiled=True)
    firsts = firsts.reshape(nz, per, rows, 2, ROWS)[..., : nh * each]
    firsts = firsts.reshape(nz, per, rows, 2, nh, each).transpose(3, 1, 2, 4, 0, 5)
    out_gf, out_uf = firsts.reshape(2, per, rows, wide)
    return input_grad, out_gf, out_uf, out_gs, out_us, out_df, out_ds


def solution(mesh):
    fine = Mesh(mesh.devices.reshape(4, 2, 2, 2, 8), ("y", "x_lo", "core", "x_hi", "z"))
    arrays = P(TENSOR, GROUP)
    weights = P(TENSOR, None, None)
    return jax.shard_map(
        shards,
        mesh=fine,
        in_specs=(arrays, arrays) + (weights,) * 6,
        out_specs=(arrays,) + (P(TENSOR, GROUP, None),) * 6,
        check_vma=False,
    )
```

```python
import functools
import jax
import jax.numpy as jnp
import numpy as np
from jax import lax
from jax.experimental import pallas as pl
from jax.experimental.pallas import tpu as pltpu
from jax.sharding import Mesh
from jax.sharding import PartitionSpec as P

BLOCK = 128
SUB = 2
BF = jnp.bfloat16
F32 = jnp.float32
NBD = 64
HID = 14
MINE = 28
EACH = MINE * SUB
ROWS = 64
SLOTS = 3
PER = 4
TOK = 256
VM = pl.BlockSpec(memory_space=pltpu.VMEM)
SM = pl.BlockSpec(memory_space=pltpu.SMEM)


def first_weight(held, kind, i):
    return held[(i % PER) * 4 + kind, i // PER]


def second_weight(held, kind, c):
    side, own = c // HID, c % HID
    at = own // SLOTS
    slot = own - jnp.minimum(at * SLOTS, HID - SLOTS)
    start = 16 + (side * SLOTS + slot) * 2
    return held[kind * 5 + at, pl.ds(start, 2)].reshape(BLOCK, BLOCK)


def dot(left, right):
    return lax.dot_general(left, right, (((1,), (0,)), ((), ())), preferred_element_type=F32)


def dot_first(left, right):
    return lax.dot_general(left, right, (((0,), (0,)), ((), ())), preferred_element_type=F32)


def dot_last(left, right):
    return lax.dot_general(left, right, (((1,), (1,)), ((), ())), preferred_element_type=F32)


def loop(count, unroll):
    def run(body):
        def step(at, carry):
            body([at * unroll + k for k in range(unroll)])
            return carry

        lax.fori_loop(0, count // unroll, step, 0)

    return run


def collect(where, shards, out):
    me, z = where[0], where[1]
    for k, shard in enumerate(shards):
        side = me if k % 2 == 0 else 1 - me
        out[pl.ds(side * 32 + lax.rem(z + k // 2, 8) * PER, PER)] = shard[...]


def turn(swap, source, target, outer):
    tiles = [source[:, k * 16 : k * 16 + 16, :].reshape(256, TOK) for k in range(4)]
    tiles = [dot(swap[...], tile).astype(BF).reshape(16, 16, TOK) for tile in tiles]
    for k, tile in enumerate(tiles):
        target[k * 16 : k * 16 + 16, pl.ds(outer, 16), :] = tile


def forward_first_kernel(where, swap, held, *refs):
    shards, (x, gate_in, up_in, mid_g, mid_u) = refs[:16], refs[16:]
    collect(where, shards, x)

    def group(at, carry):
        @loop(16, 4)
        def _(ks):
            weights = [
                jnp.concatenate([first_weight(held, 0, at * 16 + k), first_weight(held, 1, at * 16 + k)])
                for k in ks
            ]
            mids = [dot(w, x[at * 16 + k]).astype(BF) for w, k in zip(weights, ks)]
            for mid, k in zip(mids, ks):
                mid_g[k] = mid[:ROWS]
                mid_u[k] = mid[ROWS:]

        outer = pl.multiple_of(at * 16, 16)
        turn(swap, mid_g, gate_in, outer)
        turn(swap, mid_u, up_in, outer)
        return carry

    lax.fori_loop(0, 4, group, 0)


def hidden(ref, c):
    return ref[pl.ds(c * SUB, SUB)].reshape(BLOCK, TOK)


def turn_back(swap, source, target, unit):
    def group(at, carry):
        tiles = [
            source[k * 16 : k * 16 + 16, pl.ds(pl.multiple_of(at * 16, 16), 16), :].reshape(256, TOK)
            for k in range(4)
        ]
        tiles = [dot(swap[...], tile).astype(BF).reshape(16, 16, TOK) for tile in tiles]
        for k, tile in enumerate(tiles):
            target[pl.ds(at * 16, 16), unit + k * 16 : unit + k * 16 + 16, :] = tile
        return carry

    lax.fori_loop(0, 4, group, 0)


def forward_second_kernel(swap, held, gate_in, up_in, act, to_gate, to_up, down_in, down_mid):
    down_mid[EACH:] = jnp.zeros((ROWS - EACH, NBD, TOK), BF)

    @loop(MINE, 2)
    def _(cs):
        gates = [dot_first(second_weight(held, 0, c), hidden(gate_in, c)) for c in cs]
        ups = [dot_first(second_weight(held, 1, c), hidden(up_in, c)) for c in cs]
        sigmas = [jax.nn.sigmoid(g) for g in gates]
        acts = [(g * s * u).astype(BF) for g, s, u in zip(gates, sigmas, ups)]
        downs = [dot_first(second_weight(held, 2, c), a) for c, a in zip(cs, acts)]
        for c, g, s, u, a, d in zip(cs, gates, sigmas, ups, acts, downs):
            to_gate[c], to_up[c], act[c] = u * s * (1.0 + g * (1.0 - s)), g * s, a
            down_mid[pl.ds(c * SUB, SUB)] = d.astype(BF).reshape(SUB, NBD, TOK)

    turn_back(swap, down_mid, down_in, 0)


def backward_kernel(where, swap, held, to_gate, to_up, *refs):
    shards = refs[:16]
    dy, back_in, gate_back, up_back, low, parts, mid, low_g, low_u = refs[16:]
    collect(where, shards, dy)
    low_g[EACH:] = jnp.zeros((ROWS - EACH, NBD, TOK), BF)
    low_u[EACH:] = jnp.zeros((ROWS - EACH, NBD, TOK), BF)

    def group(at, carry):
        @loop(16, 4)
        def _(ks):
            mids = [dot(first_weight(held, 2, at * 16 + k), dy[at * 16 + k]).astype(BF) for k in ks]
            for value, k in zip(mids, ks):
                mid[k] = value

        turn(swap, mid, back_in, pl.multiple_of(at * 16, 16))
        return carry

    lax.fori_loop(0, 4, group, 0)

    @loop(MINE, 2)
    def _(cs):
        grads = [dot(second_weight(held, 2, c), hidden(back_in, c)) for c in cs]
        to_gates = [(grad * to_gate[c]).astype(BF) for c, grad in zip(cs, grads)]
        to_ups = [(grad * to_up[c]).astype(BF) for c, grad in zip(cs, grads)]
        lows_g = [dot(second_weight(held, 0, c), v) for c, v in zip(cs, to_gates)]
        lows_u = [dot(second_weight(held, 1, c), v) for c, v in zip(cs, to_ups)]
        for c, g, u, lg, lu in zip(cs, to_gates, to_ups, lows_g, lows_u):
            gate_back[c], up_back[c] = g, u
            low_g[pl.ds(c * SUB, SUB)] = lg.astype(BF).reshape(SUB, NBD, TOK)
            low_u[pl.ds(c * SUB, SUB)] = lu.astype(BF).reshape(SUB, NBD, TOK)

    turn_back(swap, low_g, low, 0)
    turn_back(swap, low_u, low, ROWS)

    @loop(NBD, 4)
    def _(blocks):
        weights = [
            jnp.concatenate([first_weight(held, 0, i), first_weight(held, 1, i)]) for i in blocks
        ]
        values = [dot_first(w, low[i]).astype(BF) for w, i in zip(weights, blocks)]
        for i, value in zip(blocks, values):
            side, at = i // 32, i % 32
            parts[(at // PER) * 8 + side * PER + at % PER] = value


def put(keep, send, core, index, even, odd):
    keep[index] = jnp.where(core == 0, even, odd).astype(BF)
    send[index] = jnp.where(core == 0, odd, even).astype(BF)


def put_rows(keep, send, core, side, at, value):
    for pair in range(8):
        rows = value[pair * 16 : pair * 16 + 16]
        put(keep, send, core, (pair, side, at), rows[:8], rows[8:])


def second_grads_kernel(
    where, dy, down_in, act, back_in, gate_in, up_in, gate_back, up_back, keep, send
):
    step, core = pl.program_id(0), where[2]

    @pl.when(step < MINE // 4)
    def _():
        for k in range(4):
            rows = slice(k * SUB, k * SUB + SUB)
            c = step * 4 + k
            three = (
                dot_last(gate_in[rows].reshape(BLOCK, TOK), gate_back[k]),
                dot_last(up_in[rows].reshape(BLOCK, TOK), up_back[k]),
                dot_last(act[k], back_in[rows].reshape(BLOCK, TOK)),
            )
            for kind in range(3):
                put_rows(keep, send, core, c // HID, kind * HID + c % HID, three[kind])

    fill = jnp.zeros((4, BLOCK), F32)
    grads = [dot_last(down_in[k], dy[k]) for k in range(8)]
    for n, grad in enumerate(grads):
        side, z, p = step // 4, step % 4 * 2 + n // PER, n % PER
        even, odd = [jnp.concatenate([grad[g * 28 : g * 28 + 28], fill]) for g in range(2)]
        for k in range(4):
            rows = slice(k * 8, k * 8 + 8)
            put(keep, send, core, (z, side, 3 * HID + p * 4 + k), even[rows], odd[rows])


def first_grads_kernel(where, x, low, keep, send):
    step, core = pl.program_id(0), where[2]
    grads = [dot_last(x[k], low[k]) for k in range(8)]
    for k, grad in enumerate(grads):
        i = step * 8 + k
        put_rows(keep, send, core, i // 32, i % 32, grad)


def join_kernel(pieces, gate, up):
    for z in range(8):
        value = pieces[z]
        for side in range(2):
            at = side * 224 + z * 28
            gate[:, at : at + 28] = value[:, side * 28 : side * 28 + 28]
            up[:, at : at + 28] = value[:, ROWS + side * 28 : ROWS + side * 28 + 28]


def call(kernel, outs, scratch, flops, *args):
    shapes = [jax.ShapeDtypeStruct(shape, dtype) for shape, dtype in outs]
    moved = sum(a.size * a.dtype.itemsize for a in args)
    return pl.pallas_call(
        kernel,
        out_shape=shapes,
        in_specs=[SM if a.dtype == jnp.int32 else VM for a in args],
        out_specs=[VM] * len(outs),
        scratch_shapes=[pltpu.VMEM(shape, dtype) for shape, dtype in scratch],
        compiler_params=pltpu.CompilerParams(vmem_limit_bytes=60 << 20),
        cost_estimate=pl.CostEstimate(flops=flops, bytes_accessed=moved, transcendentals=0),
    )(*args)


HIDDEN = ((MINE, BLOCK, TOK), BF)
WIDER = ((MINE, BLOCK, TOK), F32)
SPREAD = ((ROWS, NBD, TOK), BF)
MODEL = ((NBD, BLOCK, TOK), BF)
TILE = ((16, ROWS, TOK), BF)
ONE = 2 * 448 * 4 * 128 * 512


def swap_table():
    at = np.arange(256)
    table = np.zeros((256, 256), np.float32)
    table[at, at % 16 * 16 + at // 16] = 1.0
    return jnp.asarray(table, BF)


def forward_first(where, swap, held, shards):
    return call(forward_first_kernel, [MODEL, SPREAD, SPREAD], [TILE, TILE], 6 * ONE, where, swap, held, *shards)


def forward_second(swap, held, gate_in, up_in):
    outs = [HIDDEN, WIDER, WIDER, SPREAD]
    return call(forward_second_kernel, outs, [SPREAD], 5 * ONE, swap, held, gate_in, up_in)


def backward(where, swap, held, to_gate, to_up, shards):
    return call(
        backward_kernel,
        [MODEL, SPREAD, HIDDEN, HIDDEN, MODEL, MODEL],
        [TILE, SPREAD, SPREAD],
        12 * ONE,
        where, swap, held, to_gate, to_up, *shards,
    )


def blocks_of(array, count, last=None):
    def index(step):
        return (step if last is None else jnp.minimum(step, last),) + (0,) * (array.ndim - 1)

    return pl.BlockSpec((count,) + array.shape[1:], index)


def grads_call(kernel, specs, blocks, flops, where, *args):
    shape = (8, 2, blocks, 8, BLOCK)
    moved = sum(a.size * a.dtype.itemsize for a in args)
    return pl.pallas_call(
        kernel,
        grid=(8,),
        out_shape=[jax.ShapeDtypeStruct(shape, BF)] * 2,
        in_specs=[SM] + specs,
        out_specs=[pl.BlockSpec(shape, lambda step: (0,) * 5)] * 2,
        compiler_params=pltpu.CompilerParams(vmem_limit_bytes=60 << 20),
        cost_estimate=pl.CostEstimate(flops=flops, bytes_accessed=moved, transcendentals=0),
    )(where, *args)


def second_grads(where, *args):
    specs = [blocks_of(a, 8) for a in args[:2]]
    specs += [blocks_of(a, 8 if a.shape[0] == ROWS else 4, MINE // 4 - 1) for a in args[2:]]
    return grads_call(second_grads_kernel, specs, 3 * HID + 16, 4 * ONE, where, *args)


def first_grads(where, x, low):
    return grads_call(first_grads_kernel, [blocks_of(x, 8), blocks_of(low, 8)], 32, 2 * ONE, where, x, low)


def join(pieces):
    outs = [((pieces.shape[1], 448), F32)] * 2
    return call(join_kernel, outs, [], ONE // 64, pieces)


GROUP = ("y", "x_lo", "core")
CHIPS = ("y", "x_lo", "x_hi")
TENSOR = ("x_hi", "z")


def size(name):
    return lax.axis_size(name)


def shift(value, step):
    count = size("z")
    return lax.ppermute(value, "z", [(i, (i + step) % count) for i in range(count)])


def swap(value):
    return lax.ppermute(value, "x_hi", [(0, 1), (1, 0)])


def halves(array, me):
    blocks = array.shape[0] // BLOCK
    half = array.shape[1] // 2
    own = lax.dynamic_slice_in_dim(array, me * half, half, 1)
    other = swap(lax.dynamic_slice_in_dim(array, (1 - me) * half, half, 1))
    return own.reshape(blocks, BLOCK, half), other.reshape(blocks, BLOCK, half)


def ring_step(step, right, left, found):
    count = size("z")
    if step < count // 2:
        right, left = [shift(v, 1) for v in right], [shift(v, -1) for v in left]
        found[count - step], found[step] = right, left
    else:
        found[step] = [shift(right[0], 1), shift(left[1], -1)]
    return right, left


def flat(found):
    return [shard for step in range(size("z")) for shard in found[step]]


def sum_cores(keep, send):
    found = lax.ppermute(send, "core", [(0, 1), (1, 0)])
    pairs = (keep.astype(F32) + found.astype(F32)).astype(BF)
    return pairs.reshape((-1,) + pairs.shape[2:])


def to_chips(pairs):
    return lax.all_to_all(pairs, CHIPS, 0, 0, tiled=True)


def total_of(chips):
    return jnp.sum(chips.astype(F32), axis=0)


def share_first(gate_first, up_first, down_second):
    nh, nz = size("x_hi"), size("z")
    y, kind = lax.axis_index("y"), lax.axis_index(("x_lo", "core"))
    each = gate_first.shape[2] // (nh * nz)
    take = functools.partial(lax.dynamic_index_in_dim, index=y, axis=0, keepdims=False)
    gate, up = take(gate_first).T, take(up_first).T
    first = jnp.where(kind == 0, gate, jnp.where(kind == 1, up, take(down_second)))
    first = first.reshape(nh, nz, each, BLOCK).transpose(1, 0, 2, 3).reshape(nz, nh * each, BLOCK)
    first = jnp.pad(first, ((0, 0), (0, ROWS - nh * each), (0, 0)))
    first = jnp.broadcast_to(first[None], (nh,) + first.shape).reshape(nh * nz, ROWS, BLOCK)
    return lax.all_to_all(first, TENSOR, 0, 0, tiled=True)


def share_second(gate_second, up_second, down_first):
    hid = gate_second.shape[0]
    d = lax.axis_index(GROUP)
    kind, at = d // 5, jnp.minimum((d % 5) * SLOTS, hid - SLOTS)
    take = functools.partial(lax.dynamic_slice_in_dim, start_index=at, slice_size=SLOTS, axis=0)
    second = jnp.where(
        kind == 0, take(gate_second), jnp.where(kind == 1, take(up_second), take(down_first))
    )
    other = swap(second)
    me = lax.axis_index("x_hi")
    second = jnp.concatenate([jnp.where(me == 0, second, other), jnp.where(me == 0, other, second)])
    return second.reshape(-1, ROWS, BLOCK)


def shards(
    activations, cotangent, gate_first, up_first, gate_second, up_second, down_first, down_second
):
    tokens = activations.shape[1]
    per = gate_first.shape[0]
    wide = gate_first.shape[2]
    hid = gate_second.shape[0]
    ny, nx, nc, nh, nz = (size(a) for a in ("y", "x_lo", "core", "x_hi", "z"))
    ngroup = ny * nx * nc
    scale = (ngroup * tokens) ** (-0.5)
    me = lax.axis_index("x_hi")
    half = tokens // 2
    each = hid * SUB
    rows = BLOCK // ngroup

    where = jnp.stack([me, lax.axis_index("z"), lax.axis_index("core")]).astype(jnp.int32)
    table = swap_table()
    x_own, x_other = halves(activations, me)
    dy_own, dy_other = halves(cotangent, me)
    first = share_first(gate_first, up_first, down_second)
    second = share_second(gate_second, up_second, down_first)
    held = lax.all_gather(jnp.concatenate([first, second]), GROUP, axis=0, tiled=False)

    steps = nz // 2
    xs, dys = {0: [x_own, x_other]}, {0: [dy_own, dy_other]}
    state = (xs[0], xs[0])
    for step in range(1, steps + 1):
        state = ring_step(step, *state, xs)
    state, _ = lax.optimization_barrier(((dys[0], dys[0]), (xs[1][0], xs[nz - 1][0])))
    for step in range(1, steps - 1):
        state = ring_step(step, *state, dys)
    shards_x, _ = lax.optimization_barrier((flat(xs), state))
    x, gate_in, up_in = forward_first(where, table, held, shards_x)
    state = ring_step(steps - 1, *state, dys)
    state, gate_in, up_in = lax.optimization_barrier((state, gate_in, up_in))
    ring_step(steps, *state, dys)
    act, to_gate, to_up, down_in = forward_second(table, held, gate_in, up_in)
    dy, back_in, gate_back, up_back, low, parts = backward(
        where, table, held, to_gate, to_up, flat(dys)
    )

    total = lax.psum_scatter(parts, "z", scatter_dimension=0, tiled=True)
    total = total.reshape(nh, per * BLOCK, half)
    kept = lax.dynamic_index_in_dim(total, me, 0, keepdims=False)
    other = swap(lax.dynamic_index_in_dim(total, 1 - me, 0, keepdims=False))

    later = second_grads(where, dy, down_in, act, back_in, gate_in, up_in, gate_back, up_back)
    x, later = lax.optimization_barrier((x, later))
    firsts = sum_cores(*first_grads(where, x, low))
    later = to_chips(sum_cores(*later))
    firsts, later = lax.optimization_barrier((firsts, later))
    firsts = to_chips(firsts)
    firsts, other = lax.optimization_barrier((firsts, other))
    input_grad = jnp.concatenate(
        [jnp.where(me == 0, kept, other), jnp.where(me == 0, other, kept)], axis=1
    )
    later = total_of(later) * scale
    firsts = total_of(firsts) * scale
    out_gs, out_us, out_df = later[: 3 * hid].reshape(3, hid, rows, BLOCK)
    pairs = []
    for part in range(ngroup):
        for z in range(nz):
            to_z, side = part // nh, part % nh
            pairs.append((part * nz + z, (side * nz + z) * nz + to_z))
    out_ds = lax.ppermute(later[3 * hid :], GROUP + ("z",), pairs)
    out_ds = out_ds.reshape(per, -1, BLOCK)[:, :each]

    firsts = firsts.reshape(nz, per * rows, 2 * ROWS)
    firsts = lax.all_to_all(firsts, "z", 0, 0, tiled=True)
    out_gf, out_uf = [value.reshape(per, rows, wide) for value in join(firsts)]
    return input_grad, out_gf, out_uf, out_gs, out_us, out_df, out_ds


def solution(mesh):
    fine = Mesh(mesh.devices.reshape(4, 2, 2, 2, 8), ("y", "x_lo", "core", "x_hi", "z"))
    arrays = P(TENSOR, GROUP)
    weights = P(TENSOR, None, None)
    return jax.shard_map(
        shards,
        mesh=fine,
        in_specs=(arrays, arrays) + (weights,) * 6,
        out_specs=(arrays,) + (P(TENSOR, GROUP, None),) * 6,
        check_vma=False,
    )
```

```python
import functools
import jax
import jax.numpy as jnp
import numpy as np
from jax import lax
from jax.experimental import pallas as pl
from jax.experimental.pallas import tpu as pltpu
from jax.sharding import Mesh
from jax.sharding import PartitionSpec as P

BLOCK = 128
SUB = 2
BF = jnp.bfloat16
F32 = jnp.float32
NBD = 64
HID = 14
MINE = 28
EACH = MINE * SUB
ROWS = 64
SLOTS = 3
PER = 4
TOK = 256
VM = pl.BlockSpec(memory_space=pltpu.VMEM)
SM = pl.BlockSpec(memory_space=pltpu.SMEM)


def first_weight(held, kind, i):
    return held[(i % PER) * 4 + kind, i // PER]


def second_weight(held, kind, c):
    side, own = c // HID, c % HID
    at = own // SLOTS
    slot = own - jnp.minimum(at * SLOTS, HID - SLOTS)
    start = (side * SLOTS + slot) * 2
    return held[kind * 5 + at, pl.ds(start, 2)].reshape(BLOCK, BLOCK)


def dot(left, right):
    return lax.dot_general(left, right, (((1,), (0,)), ((), ())), preferred_element_type=F32)


def dot_first(left, right):
    return lax.dot_general(left, right, (((0,), (0,)), ((), ())), preferred_element_type=F32)


def dot_last(left, right):
    return lax.dot_general(left, right, (((1,), (1,)), ((), ())), preferred_element_type=F32)


def loop(count, unroll):
    def run(body):
        def step(at, carry):
            body([at * unroll + k for k in range(unroll)])
            return carry

        lax.fori_loop(0, count // unroll, step, 0)

    return run


def copy(pairs, sems, first=0):
    copies = [pltpu.make_async_copy(a, b, sems.at[first + k]) for k, (a, b) in enumerate(pairs)]
    for one in copies:
        one.start()
    return copies


def wait(copies):
    for one in copies:
        one.wait()


def placed(where, shards, out):
    me, z = where[0], where[1]
    for k, shard in enumerate(shards):
        side = me if k % 2 == 0 else 1 - me
        yield shard, out.at[pl.ds(side * 32 + lax.rem(z + k // 2, 8) * PER, PER)]


def turn(swap, source, target, outer):
    tiles = [source[:, k * 16 : k * 16 + 16, :].reshape(256, TOK) for k in range(4)]
    tiles = [dot(swap[...], tile).astype(BF).reshape(16, 16, TOK) for tile in tiles]
    for k, tile in enumerate(tiles):
        target[k * 16 : k * 16 + 16, pl.ds(outer, 16), :] = tile


def forward_first_kernel(where, swap, held_all, *refs):
    shards, (x_out, gate_out, up_out) = refs[:16], refs[16:19]
    x, held, gate_in, up_in, mid_g, mid_u, ins, outs = refs[19:]
    arrive = copy(list(placed(where, shards, x)) + [(held_all.at[:, pl.ds(0, 16)], held)], ins)
    wait(arrive)
    leave = copy([(x, x_out)], outs)
    for at in range(4):

        @loop(16, 4)
        def _(ks, at=at):
            weights = [
                jnp.concatenate([first_weight(held, 0, at * 16 + k), first_weight(held, 1, at * 16 + k)])
                for k in ks
            ]
            mids = [dot(w, x[at * 16 + k]).astype(BF) for w, k in zip(weights, ks)]
            for mid, k in zip(mids, ks):
                mid_g[k] = mid[:ROWS]
                mid_u[k] = mid[ROWS:]

        turn(swap, mid_g, gate_in, at * 16)
        turn(swap, mid_u, up_in, at * 16)
        part = pl.ds(at * 16, 16)
        pairs = [(gate_in.at[:, part], gate_out.at[:, part]), (up_in.at[:, part], up_out.at[:, part])]
        leave += copy(pairs, outs, 1 + 2 * at)
    wait(leave)


def hidden(ref, c):
    return ref[pl.ds(c * SUB, SUB)].reshape(BLOCK, TOK)


def turn_back(swap, source, target, unit):
    def group(at, carry):
        tiles = [
            source[k * 16 : k * 16 + 16, pl.ds(pl.multiple_of(at * 16, 16), 16), :].reshape(256, TOK)
            for k in range(4)
        ]
        tiles = [dot(swap[...], tile).astype(BF).reshape(16, 16, TOK) for tile in tiles]
        for k, tile in enumerate(tiles):
            target[pl.ds(at * 16, 16), unit + k * 16 : unit + k * 16 + 16, :] = tile
        return carry

    lax.fori_loop(0, 4, group, 0)


def forward_second_kernel(swap, held_all, gate_from, up_from, *refs):
    act_out, to_gate_out, to_up_out, down_out = refs[:4]
    held, gate_in, up_in, act, to_gate, to_up, down_in, down_mid, ins, outs = refs[4:]
    wait(copy([(held_all.at[:, pl.ds(16, 12)], held), (gate_from, gate_in), (up_from, up_in)], ins))
    down_mid[EACH:] = jnp.zeros((ROWS - EACH, NBD, TOK), BF)
    leave = []
    for part in range(2):

        @loop(HID, 2)
        def _(owns, part=part):
            cs = [part * HID + own for own in owns]
            gates = [dot_first(second_weight(held, 0, c), hidden(gate_in, c)) for c in cs]
            ups = [dot_first(second_weight(held, 1, c), hidden(up_in, c)) for c in cs]
            sigmas = [jax.nn.sigmoid(g) for g in gates]
            acts = [(g * s * u).astype(BF) for g, s, u in zip(gates, sigmas, ups)]
            downs = [dot_first(second_weight(held, 2, c), a) for c, a in zip(cs, acts)]
            for c, g, s, u, a, d in zip(cs, gates, sigmas, ups, acts, downs):
                to_gate[c], to_up[c], act[c] = u * s * (1.0 + g * (1.0 - s)), g * s, a
                down_mid[pl.ds(c * SUB, SUB)] = d.astype(BF).reshape(SUB, NBD, TOK)

        rows = pl.ds(part * HID, HID)
        pairs = [(to_gate, to_gate_out), (to_up, to_up_out), (act, act_out)]
        leave += copy([(a.at[rows], b.at[rows]) for a, b in pairs], outs, 3 * part)
    turn_back(swap, down_mid, down_in, 0)
    wait(leave + copy([(down_in, down_out)], outs, 6))


def backward_kernel(where, swap, held_all, to_gate_from, to_up_from, *refs):
    shards, out = refs[:16], refs[16:22]
    dy, held, held_second, to_gate, to_up, back_in, gate_back, up_back = refs[22:30]
    low, parts, mid, low_g, low_u, ins, outs = refs[30:]
    arrive = copy(list(placed(where, shards, dy)) + [(held_all.at[:, pl.ds(0, 16)], held)], ins)
    pairs = [(held_all.at[:, pl.ds(16, 12)], held_second), (to_gate_from, to_gate), (to_up_from, to_up)]
    later = copy(pairs, ins, 17)
    low_g[EACH:] = jnp.zeros((ROWS - EACH, NBD, TOK), BF)
    low_u[EACH:] = jnp.zeros((ROWS - EACH, NBD, TOK), BF)
    wait(arrive)
    leave = copy([(dy, out[0])], outs)

    def group(at, carry):
        @loop(16, 4)
        def _(ks):
            mids = [dot(first_weight(held, 2, at * 16 + k), dy[at * 16 + k]).astype(BF) for k in ks]
            for value, k in zip(mids, ks):
                mid[k] = value

        turn(swap, mid, back_in, pl.multiple_of(at * 16, 16))
        return carry

    lax.fori_loop(0, 4, group, 0)
    leave += copy([(back_in, out[1])], outs, 1)
    wait(later)

    @loop(MINE, 2)
    def _(cs):
        grads = [dot(second_weight(held_second, 2, c), hidden(back_in, c)) for c in cs]
        to_gates = [(grad * to_gate[c]).astype(BF) for c, grad in zip(cs, grads)]
        to_ups = [(grad * to_up[c]).astype(BF) for c, grad in zip(cs, grads)]
        lows_g = [dot(second_weight(held_second, 0, c), v) for c, v in zip(cs, to_gates)]
        lows_u = [dot(second_weight(held_second, 1, c), v) for c, v in zip(cs, to_ups)]
        for c, g, u, lg, lu in zip(cs, to_gates, to_ups, lows_g, lows_u):
            gate_back[c], up_back[c] = g, u
            low_g[pl.ds(c * SUB, SUB)] = lg.astype(BF).reshape(SUB, NBD, TOK)
            low_u[pl.ds(c * SUB, SUB)] = lu.astype(BF).reshape(SUB, NBD, TOK)

    leave += copy([(gate_back, out[2]), (up_back, out[3])], outs, 2)
    turn_back(swap, low_g, low, 0)
    turn_back(swap, low_u, low, ROWS)
    leave += copy([(low, out[4])], outs, 4)
    for part in range(4):

        @loop(16, 4)
        def _(ks, part=part):
            at = [part * 16 + k for k in ks]
            blocks = [k % 8 // PER * 32 + k // 8 * PER + k % PER for k in at]
            weights = [
                jnp.concatenate([first_weight(held, 0, i), first_weight(held, 1, i)]) for i in blocks
            ]
            values = [dot_first(w, low[i]).astype(BF) for w, i in zip(weights, blocks)]
            for k, value in zip(at, values):
                parts[k] = value

        rows = pl.ds(part * 16, 16)
        leave += copy([(parts.at[rows], out[5].at[rows])], outs, 5 + part)
    wait(leave)


def put(keep, send, core, index, even, odd):
    keep[index] = jnp.where(core == 0, even, odd).astype(BF)
    send[index] = jnp.where(core == 0, odd, even).astype(BF)


def put_rows(keep, send, core, side, at, value):
    for pair in range(8):
        rows = value[pair * 16 : pair * 16 + 16]
        put(keep, send, core, (pair, side, at), rows[:8], rows[8:])


def second_grads_kernel(
    where, dy, down_in, act, back_in, gate_in, up_in, gate_back, up_back, keep, send
):
    step, core = pl.program_id(0), where[2]

    @pl.when(step < MINE // 4)
    def _():
        for k in range(4):
            rows = slice(k * SUB, k * SUB + SUB)
            c = step * 4 + k
            three = (
                dot_last(gate_in[rows].reshape(BLOCK, TOK), gate_back[k]),
                dot_last(up_in[rows].reshape(BLOCK, TOK), up_back[k]),
                dot_last(act[k], back_in[rows].reshape(BLOCK, TOK)),
            )
            for kind in range(3):
                put_rows(keep, send, core, c // HID, kind * HID + c % HID, three[kind])

    fill = jnp.zeros((4, BLOCK), F32)
    grads = [dot_last(down_in[k], dy[k]) for k in range(8)]
    for n, grad in enumerate(grads):
        side, z, p = step // 4, step % 4 * 2 + n // PER, n % PER
        even, odd = [jnp.concatenate([grad[g * 28 : g * 28 + 28], fill]) for g in range(2)]
        for k in range(4):
            rows = slice(k * 8, k * 8 + 8)
            put(keep, send, core, (z, side, 3 * HID + p * 4 + k), even[rows], odd[rows])


def first_grads_kernel(where, x, low, keep, send):
    step, core = pl.program_id(0), where[2]
    grads = [dot_last(x[k], low[k]) for k in range(8)]
    for k, grad in enumerate(grads):
        i = step * 8 + k
        put_rows(keep, send, core, i // 32, i % 32, grad)


def join_kernel(pieces, gate, up):
    for z in range(8):
        value = pieces[z]
        for side in range(2):
            at = side * 224 + z * 28
            gate[:, at : at + 28] = value[:, side * 28 : side * 28 + 28]
            up[:, at : at + 28] = value[:, ROWS + side * 28 : ROWS + side * 28 + 28]


def call(kernel, outs, scratch, flops, *args):
    shapes = [jax.ShapeDtypeStruct(shape, dtype) for shape, dtype in outs]
    moved = sum(a.size * a.dtype.itemsize for a in args)
    return pl.pallas_call(
        kernel,
        out_shape=shapes,
        in_specs=[SM if a.dtype == jnp.int32 else VM for a in args],
        out_specs=[VM] * len(outs),
        scratch_shapes=[pltpu.VMEM(shape, dtype) for shape, dtype in scratch],
        compiler_params=pltpu.CompilerParams(vmem_limit_bytes=60 << 20),
        cost_estimate=pl.CostEstimate(flops=flops, bytes_accessed=moved, transcendentals=0),
    )(*args)


ANY = pl.BlockSpec(memory_space=pl.ANY)
HIDDEN = ((MINE, BLOCK, TOK), BF)
WIDER = ((MINE, BLOCK, TOK), F32)
SPREAD = ((ROWS, NBD, TOK), BF)
MODEL = ((NBD, BLOCK, TOK), BF)
TILE = ((16, ROWS, TOK), BF)
FIRST = ((16, 16, ROWS, BLOCK), BF)
SECOND = ((16, 12, ROWS, BLOCK), BF)
ONE = 2 * 448 * 4 * 128 * 512


def swap_table():
    at = np.arange(256)
    table = np.zeros((256, 256), np.float32)
    table[at, at % 16 * 16 + at // 16] = 1.0
    return jnp.asarray(table, BF)


def copying(kernel, outs, scratch, arrivals, flops, near, *args):
    moved = sum(a.size * a.dtype.itemsize for a in args)
    specs = [SM if a.dtype == jnp.int32 else VM for a in args[:near]] + [ANY] * (len(args) - near)
    return pl.pallas_call(
        kernel,
        out_shape=[jax.ShapeDtypeStruct(shape, dtype) for shape, dtype in outs],
        in_specs=specs,
        out_specs=[ANY] * len(outs),
        scratch_shapes=[pltpu.VMEM(shape, dtype) for shape, dtype in scratch]
        + [pltpu.SemaphoreType.DMA((arrivals,)), pltpu.SemaphoreType.DMA((9,))],
        compiler_params=pltpu.CompilerParams(vmem_limit_bytes=60 << 20),
        cost_estimate=pl.CostEstimate(flops=flops, bytes_accessed=moved, transcendentals=0),
    )(*args)


def forward_first(where, swap, held, shards):
    outs = [MODEL, SPREAD, SPREAD]
    scratch = [MODEL, FIRST, SPREAD, SPREAD, TILE, TILE]
    return copying(forward_first_kernel, outs, scratch, 17, 6 * ONE, 2, where, swap, held, *shards)


def forward_second(swap, held, gate_in, up_in):
    outs = [HIDDEN, WIDER, WIDER, SPREAD]
    scratch = [SECOND, SPREAD, SPREAD, HIDDEN, WIDER, WIDER, SPREAD, SPREAD]
    return copying(forward_second_kernel, outs, scratch, 3, 5 * ONE, 1, swap, held, gate_in, up_in)


def backward(where, swap, held, to_gate, to_up, shards):
    outs = [MODEL, SPREAD, HIDDEN, HIDDEN, MODEL, MODEL]
    scratch = [MODEL, FIRST, SECOND, WIDER, WIDER, SPREAD, HIDDEN, HIDDEN, MODEL, MODEL]
    scratch += [TILE, SPREAD, SPREAD]
    return copying(
        backward_kernel, outs, scratch, 20, 12 * ONE, 2, where, swap, held, to_gate, to_up, *shards
    )


def blocks_of(array, count, last=None):
    def index(step):
        return (step if last is None else jnp.minimum(step, last),) + (0,) * (array.ndim - 1)

    return pl.BlockSpec((count,) + array.shape[1:], index)


def grads_call(kernel, specs, blocks, flops, where, *args):
    shape = (8, 2, blocks, 8, BLOCK)
    moved = sum(a.size * a.dtype.itemsize for a in args)
    return pl.pallas_call(
        kernel,
        grid=(8,),
        out_shape=[jax.ShapeDtypeStruct(shape, BF)] * 2,
        in_specs=[SM] + specs,
        out_specs=[pl.BlockSpec(shape, lambda step: (0,) * 5)] * 2,
        compiler_params=pltpu.CompilerParams(vmem_limit_bytes=60 << 20),
        cost_estimate=pl.CostEstimate(flops=flops, bytes_accessed=moved, transcendentals=0),
    )(where, *args)


def second_grads(where, *args):
    specs = [blocks_of(a, 8) for a in args[:2]]
    specs += [blocks_of(a, 8 if a.shape[0] == ROWS else 4, MINE // 4 - 1) for a in args[2:]]
    return grads_call(second_grads_kernel, specs, 3 * HID + 16, 4 * ONE, where, *args)


def first_grads(where, x, low):
    return grads_call(first_grads_kernel, [blocks_of(x, 8), blocks_of(low, 8)], 32, 2 * ONE, where, x, low)


def join(pieces):
    outs = [((pieces.shape[1], 448), F32)] * 2
    return call(join_kernel, outs, [], ONE // 64, pieces)


GROUP = ("y", "x_lo", "core")
CHIPS = ("y", "x_lo", "x_hi")
TENSOR = ("x_hi", "z")


def size(name):
    return lax.axis_size(name)


def shift(value, step):
    count = size("z")
    return lax.ppermute(value, "z", [(i, (i + step) % count) for i in range(count)])


def swap(value):
    return lax.ppermute(value, "x_hi", [(0, 1), (1, 0)])


def halves(array, me):
    blocks = array.shape[0] // BLOCK
    half = array.shape[1] // 2
    own = lax.dynamic_slice_in_dim(array, me * half, half, 1)
    other = swap(lax.dynamic_slice_in_dim(array, (1 - me) * half, half, 1))
    return own.reshape(blocks, BLOCK, half), other.reshape(blocks, BLOCK, half)


def ring_step(step, right, left, found):
    count = size("z")
    if step < count // 2:
        right, left = [shift(v, 1) for v in right], [shift(v, -1) for v in left]
        found[count - step], found[step] = right, left
    else:
        found[step] = [shift(right[0], 1), shift(left[1], -1)]
    return right, left


def flat(found):
    return [shard for step in range(size("z")) for shard in found[step]]


def sum_cores(keep, send):
    found = lax.ppermute(send, "core", [(0, 1), (1, 0)])
    pairs = (keep.astype(F32) + found.astype(F32)).astype(BF)
    return pairs.reshape((-1,) + pairs.shape[2:])


def to_chips(pairs):
    return lax.all_to_all(pairs, CHIPS, 0, 0, tiled=True)


def total_of(chips):
    return jnp.sum(chips.astype(F32), axis=0)


def share_first(gate_first, up_first, down_second):
    nh, nz = size("x_hi"), size("z")
    y, kind = lax.axis_index("y"), lax.axis_index(("x_lo", "core"))
    each = gate_first.shape[2] // (nh * nz)
    take = functools.partial(lax.dynamic_index_in_dim, index=y, axis=0, keepdims=False)
    gate, up = take(gate_first).T, take(up_first).T
    first = jnp.where(kind == 0, gate, jnp.where(kind == 1, up, take(down_second)))
    first = first.reshape(nh, nz, each, BLOCK).transpose(1, 0, 2, 3).reshape(nz, nh * each, BLOCK)
    first = jnp.pad(first, ((0, 0), (0, ROWS - nh * each), (0, 0)))
    first = jnp.broadcast_to(first[None], (nh,) + first.shape).reshape(nh * nz, ROWS, BLOCK)
    return lax.all_to_all(first, TENSOR, 0, 0, tiled=True)


def share_second(gate_second, up_second, down_first):
    hid = gate_second.shape[0]
    d = lax.axis_index(GROUP)
    kind, at = d // 5, jnp.minimum((d % 5) * SLOTS, hid - SLOTS)
    take = functools.partial(lax.dynamic_slice_in_dim, start_index=at, slice_size=SLOTS, axis=0)
    second = jnp.where(
        kind == 0, take(gate_second), jnp.where(kind == 1, take(up_second), take(down_first))
    )
    other = swap(second)
    me = lax.axis_index("x_hi")
    second = jnp.concatenate([jnp.where(me == 0, second, other), jnp.where(me == 0, other, second)])
    return second.reshape(-1, ROWS, BLOCK)


def shards(
    activations, cotangent, gate_first, up_first, gate_second, up_second, down_first, down_second
):
    tokens = activations.shape[1]
    per = gate_first.shape[0]
    wide = gate_first.shape[2]
    hid = gate_second.shape[0]
    ny, nx, nc, nh, nz = (size(a) for a in ("y", "x_lo", "core", "x_hi", "z"))
    ngroup = ny * nx * nc
    scale = (ngroup * tokens) ** (-0.5)
    me = lax.axis_index("x_hi")
    half = tokens // 2
    each = hid * SUB
    rows = BLOCK // ngroup

    where = jnp.stack([me, lax.axis_index("z"), lax.axis_index("core")]).astype(jnp.int32)
    table = swap_table()
    x_own, x_other = halves(activations, me)
    dy_own, dy_other = halves(cotangent, me)
    first = share_first(gate_first, up_first, down_second)
    second = share_second(gate_second, up_second, down_first)
    held = lax.all_gather(jnp.concatenate([first, second]), GROUP, axis=0, tiled=False)

    steps = nz // 2
    xs, dys = {0: [x_own, x_other]}, {0: [dy_own, dy_other]}
    state = (xs[0], xs[0])
    for step in range(1, steps + 1):
        state = ring_step(step, *state, xs)
    state, _ = lax.optimization_barrier(((dys[0], dys[0]), (xs[1][0], xs[nz - 1][0])))
    for step in range(1, steps - 1):
        state = ring_step(step, *state, dys)
    shards_x, _ = lax.optimization_barrier((flat(xs), state))
    x, gate_in, up_in = forward_first(where, table, held, shards_x)
    state = ring_step(steps - 1, *state, dys)
    state, gate_in, up_in = lax.optimization_barrier((state, gate_in, up_in))
    ring_step(steps, *state, dys)
    act, to_gate, to_up, down_in = forward_second(table, held, gate_in, up_in)
    dy, back_in, gate_back, up_back, low, parts = backward(
        where, table, held, to_gate, to_up, flat(dys)
    )

    total = lax.psum_scatter(parts, "z", scatter_dimension=0, tiled=True)
    total = total.reshape(nh, per * BLOCK, half)
    kept = lax.dynamic_index_in_dim(total, me, 0, keepdims=False)
    other = swap(lax.dynamic_index_in_dim(total, 1 - me, 0, keepdims=False))

    later = second_grads(where, dy, down_in, act, back_in, gate_in, up_in, gate_back, up_back)
    x, later = lax.optimization_barrier((x, later))
    firsts = sum_cores(*first_grads(where, x, low))
    later = to_chips(sum_cores(*later))
    firsts, later = lax.optimization_barrier((firsts, later))
    firsts = to_chips(firsts)
    input_grad = jnp.concatenate(
        [jnp.where(me == 0, kept, other), jnp.where(me == 0, other, kept)], axis=1
    )
    later = total_of(later) * scale
    firsts = total_of(firsts) * scale
    out_gs, out_us, out_df = later[: 3 * hid].reshape(3, hid, rows, BLOCK)
    pairs = []
    for part in range(ngroup):
        for z in range(nz):
            to_z, side = part // nh, part % nh
            pairs.append((part * nz + z, (side * nz + z) * nz + to_z))
    out_ds = lax.ppermute(later[3 * hid :], GROUP + ("z",), pairs)
    out_ds = out_ds.reshape(per, -1, BLOCK)[:, :each]

    firsts = firsts.reshape(nz, per * rows, 2 * ROWS)
    firsts = lax.all_to_all(firsts, "z", 0, 0, tiled=True)
    out_gf, out_uf = [value.reshape(per, rows, wide) for value in join(firsts)]
    return input_grad, out_gf, out_uf, out_gs, out_us, out_df, out_ds


def solution(mesh):
    fine = Mesh(mesh.devices.reshape(4, 2, 2, 2, 8), ("y", "x_lo", "core", "x_hi", "z"))
    arrays = P(TENSOR, GROUP)
    weights = P(TENSOR, None, None)
    return jax.shard_map(
        shards,
        mesh=fine,
        in_specs=(arrays, arrays) + (weights,) * 6,
        out_specs=(arrays,) + (P(TENSOR, GROUP, None),) * 6,
        check_vma=False,
    )
```

```python
import functools
import jax
import jax.numpy as jnp
import numpy as np
from jax import lax
from jax.experimental import pallas as pl
from jax.experimental.pallas import tpu as pltpu
from jax.sharding import Mesh
from jax.sharding import PartitionSpec as P

BLOCK = 128
SUB = 2
BF = jnp.bfloat16
F32 = jnp.float32
NBD = 64
HID = 14
MINE = 28
EACH = MINE * SUB
ROWS = 64
SLOTS = 3
PER = 4
TOK = 256
VM = pl.BlockSpec(memory_space=pltpu.VMEM)
SM = pl.BlockSpec(memory_space=pltpu.SMEM)


def first_weight(held, kind, i):
    return held[(i % PER) * 4 + kind, i // PER]


def second_weight(held, kind, c):
    side, own = c // HID, c % HID
    at = own // SLOTS
    slot = own - jnp.minimum(at * SLOTS, HID - SLOTS)
    start = (side * SLOTS + slot) * 2
    return held[kind * 5 + at, pl.ds(start, 2)].reshape(BLOCK, BLOCK)


def dot(left, right):
    return lax.dot_general(left, right, (((1,), (0,)), ((), ())), preferred_element_type=F32)


def dot_first(left, right):
    return lax.dot_general(left, right, (((0,), (0,)), ((), ())), preferred_element_type=F32)


def dot_last(left, right):
    return lax.dot_general(left, right, (((1,), (1,)), ((), ())), preferred_element_type=F32)


def loop(count, unroll):
    def run(body):
        def step(at, carry):
            body([at * unroll + k for k in range(unroll)])
            return carry

        lax.fori_loop(0, count // unroll, step, 0)

    return run


def copy(pairs, sems, first=0):
    copies = [pltpu.make_async_copy(a, b, sems.at[first + k]) for k, (a, b) in enumerate(pairs)]
    for one in copies:
        one.start()
    return copies


def wait(copies):
    for one in copies:
        one.wait()


def placed(where, shards, out):
    me, z = where[0], where[1]
    for k, shard in enumerate(shards):
        side = me if k % 2 == 0 else 1 - me
        yield shard, out.at[pl.ds(side * 32 + lax.rem(z + k // 2, 8) * PER, PER)]


def turn(swap, source, target, outer):
    tiles = [source[:, k * 16 : k * 16 + 16, :].reshape(256, TOK) for k in range(4)]
    tiles = [dot(swap[...], tile).astype(BF).reshape(16, 16, TOK) for tile in tiles]
    for k, tile in enumerate(tiles):
        target[k * 16 : k * 16 + 16, pl.ds(outer, 16), :] = tile


def forward_first_kernel(where, swap, held_all, *refs):
    shards, (x_out, gate_out, up_out) = refs[:16], refs[16:19]
    x, held, gate_in, up_in, mid_g, mid_u, ins, outs = refs[19:]
    arrive = copy(list(placed(where, shards, x)) + [(held_all.at[:, pl.ds(0, 16)], held)], ins)
    wait(arrive)
    leave = copy([(x, x_out)], outs)
    for at in range(4):

        @loop(16, 4)
        def _(ks, at=at):
            weights = [
                jnp.concatenate([first_weight(held, 0, at * 16 + k), first_weight(held, 1, at * 16 + k)])
                for k in ks
            ]
            mids = [dot(w, x[at * 16 + k]).astype(BF) for w, k in zip(weights, ks)]
            for mid, k in zip(mids, ks):
                mid_g[k] = mid[:ROWS]
                mid_u[k] = mid[ROWS:]

        turn(swap, mid_g, gate_in, at * 16)
        turn(swap, mid_u, up_in, at * 16)
        part = pl.ds(at * 16, 16)
        pairs = [(gate_in.at[:, part], gate_out.at[:, part]), (up_in.at[:, part], up_out.at[:, part])]
        leave += copy(pairs, outs, 1 + 2 * at)
    wait(leave)


def hidden(ref, c):
    return ref[pl.ds(c * SUB, SUB)].reshape(BLOCK, TOK)


def turn_back(swap, source, target, unit):
    def group(at, carry):
        tiles = [
            source[k * 16 : k * 16 + 16, pl.ds(pl.multiple_of(at * 16, 16), 16), :].reshape(256, TOK)
            for k in range(4)
        ]
        tiles = [dot(swap[...], tile).astype(BF).reshape(16, 16, TOK) for tile in tiles]
        for k, tile in enumerate(tiles):
            target[pl.ds(at * 16, 16), unit + k * 16 : unit + k * 16 + 16, :] = tile
        return carry

    lax.fori_loop(0, 4, group, 0)


def forward_second_kernel(swap, held_all, gate_from, up_from, *refs):
    act_out, to_gate_out, to_up_out, down_out = refs[:4]
    held, gate_in, up_in, act, to_gate, to_up, down_in, down_mid, ins, outs = refs[4:]
    wait(copy([(held_all.at[:, pl.ds(16, 12)], held), (gate_from, gate_in), (up_from, up_in)], ins))
    down_mid[EACH:] = jnp.zeros((ROWS - EACH, NBD, TOK), BF)
    leave = []
    for part in range(2):

        @loop(HID, 2)
        def _(owns, part=part):
            cs = [part * HID + own for own in owns]
            gates = [dot_first(second_weight(held, 0, c), hidden(gate_in, c)) for c in cs]
            ups = [dot_first(second_weight(held, 1, c), hidden(up_in, c)) for c in cs]
            sigmas = [jax.nn.sigmoid(g) for g in gates]
            acts = [(g * s * u).astype(BF) for g, s, u in zip(gates, sigmas, ups)]
            downs = [dot_first(second_weight(held, 2, c), a) for c, a in zip(cs, acts)]
            for c, g, s, u, a, d in zip(cs, gates, sigmas, ups, acts, downs):
                to_gate[c], to_up[c], act[c] = u * s * (1.0 + g * (1.0 - s)), g * s, a
                down_mid[pl.ds(c * SUB, SUB)] = d.astype(BF).reshape(SUB, NBD, TOK)

        rows = pl.ds(part * HID, HID)
        pairs = [(to_gate, to_gate_out), (to_up, to_up_out), (act, act_out)]
        leave += copy([(a.at[rows], b.at[rows]) for a, b in pairs], outs, 3 * part)
    turn_back(swap, down_mid, down_in, 0)
    wait(leave + copy([(down_in, down_out)], outs, 6))


def backward_kernel(where, swap, held_all, to_gate_from, to_up_from, *refs):
    shards, out = refs[:16], refs[16:22]
    dy, held, held_second, to_gate, to_up, back_in, gate_back, up_back = refs[22:30]
    low, parts, mid, low_g, low_u, ins, outs = refs[30:]
    arrive = copy(list(placed(where, shards, dy)) + [(held_all.at[:, pl.ds(0, 16)], held)], ins)
    pairs = [(held_all.at[:, pl.ds(16, 12)], held_second), (to_gate_from, to_gate), (to_up_from, to_up)]
    later = copy(pairs, ins, 17)
    low_g[EACH:] = jnp.zeros((ROWS - EACH, NBD, TOK), BF)
    low_u[EACH:] = jnp.zeros((ROWS - EACH, NBD, TOK), BF)
    wait(arrive)
    leave = copy([(dy, out[0])], outs)

    def group(at, carry):
        @loop(16, 4)
        def _(ks):
            mids = [dot(first_weight(held, 2, at * 16 + k), dy[at * 16 + k]).astype(BF) for k in ks]
            for value, k in zip(mids, ks):
                mid[k] = value

        turn(swap, mid, back_in, pl.multiple_of(at * 16, 16))
        return carry

    lax.fori_loop(0, 4, group, 0)
    leave += copy([(back_in, out[1])], outs, 1)
    wait(later)

    @loop(MINE, 2)
    def _(cs):
        grads = [dot(second_weight(held_second, 2, c), hidden(back_in, c)) for c in cs]
        to_gates = [(grad * to_gate[c]).astype(BF) for c, grad in zip(cs, grads)]
        to_ups = [(grad * to_up[c]).astype(BF) for c, grad in zip(cs, grads)]
        lows_g = [dot(second_weight(held_second, 0, c), v) for c, v in zip(cs, to_gates)]
        lows_u = [dot(second_weight(held_second, 1, c), v) for c, v in zip(cs, to_ups)]
        for c, g, u, lg, lu in zip(cs, to_gates, to_ups, lows_g, lows_u):
            gate_back[c], up_back[c] = g, u
            low_g[pl.ds(c * SUB, SUB)] = lg.astype(BF).reshape(SUB, NBD, TOK)
            low_u[pl.ds(c * SUB, SUB)] = lu.astype(BF).reshape(SUB, NBD, TOK)

    leave += copy([(gate_back, out[2]), (up_back, out[3])], outs, 2)
    turn_back(swap, low_g, low, 0)
    turn_back(swap, low_u, low, ROWS)
    leave += copy([(low, out[4])], outs, 4)
    for part in range(4):

        @loop(16, 4)
        def _(ks, part=part):
            at = [part * 16 + k for k in ks]
            blocks = [k % 8 // PER * 32 + k // 8 * PER + k % PER for k in at]
            weights = [
                jnp.concatenate([first_weight(held, 0, i), first_weight(held, 1, i)]) for i in blocks
            ]
            values = [dot_first(w, low[i]).astype(BF) for w, i in zip(weights, blocks)]
            for k, value in zip(at, values):
                parts[k] = value

        rows = pl.ds(part * 16, 16)
        leave += copy([(parts.at[rows], out[5].at[rows])], outs, 5 + part)
    wait(leave)


def put(keep, send, core, index, even, odd):
    keep[index] = jnp.where(core == 0, even, odd).astype(BF)
    send[index] = jnp.where(core == 0, odd, even).astype(BF)


def put_rows(keep, send, core, side, at, value):
    for pair in range(8):
        rows = value[pair * 16 : pair * 16 + 16]
        put(keep, send, core, (pair, side, at), rows[:8], rows[8:])


def second_grads_kernel(
    where, dy, down_in, act, back_in, gate_in, up_in, gate_back, up_back, keep, send
):
    step, core = pl.program_id(0), where[2]

    @pl.when(step < MINE // 4)
    def _():
        for k in range(4):
            rows = slice(k * SUB, k * SUB + SUB)
            c = step * 4 + k
            three = (
                dot_last(gate_in[rows].reshape(BLOCK, TOK), gate_back[k]),
                dot_last(up_in[rows].reshape(BLOCK, TOK), up_back[k]),
                dot_last(act[k], back_in[rows].reshape(BLOCK, TOK)),
            )
            for kind in range(3):
                put_rows(keep, send, core, c // HID, kind * HID + c % HID, three[kind])

    fill = jnp.zeros((4, BLOCK), F32)
    grads = [dot_last(down_in[k], dy[k]) for k in range(8)]
    for n, grad in enumerate(grads):
        side, z, p = step // 4, step % 4 * 2 + n // PER, n % PER
        even, odd = [jnp.concatenate([grad[g * 28 : g * 28 + 28], fill]) for g in range(2)]
        for k in range(4):
            rows = slice(k * 8, k * 8 + 8)
            put(keep, send, core, (z, side, 3 * HID + p * 4 + k), even[rows], odd[rows])


def first_grads_kernel(where, x, low, keep, send):
    step, core = pl.program_id(0), where[2]
    grads = [dot_last(x[k], low[k]) for k in range(8)]
    for k, grad in enumerate(grads):
        i = step * 8 + k
        put_rows(keep, send, core, i // 32, i % 32, grad)


def join_kernel(pieces, gate, up):
    for z in range(8):
        value = pieces[z]
        for side in range(2):
            at = side * 224 + z * 28
            gate[:, at : at + 28] = value[:, side * 28 : side * 28 + 28]
            up[:, at : at + 28] = value[:, ROWS + side * 28 : ROWS + side * 28 + 28]


def call(kernel, outs, scratch, flops, *args):
    shapes = [jax.ShapeDtypeStruct(shape, dtype) for shape, dtype in outs]
    moved = sum(a.size * a.dtype.itemsize for a in args)
    return pl.pallas_call(
        kernel,
        out_shape=shapes,
        in_specs=[SM if a.dtype == jnp.int32 else VM for a in args],
        out_specs=[VM] * len(outs),
        scratch_shapes=[pltpu.VMEM(shape, dtype) for shape, dtype in scratch],
        compiler_params=pltpu.CompilerParams(vmem_limit_bytes=60 << 20),
        cost_estimate=pl.CostEstimate(flops=flops, bytes_accessed=moved, transcendentals=0),
    )(*args)


ANY = pl.BlockSpec(memory_space=pl.ANY)
HIDDEN = ((MINE, BLOCK, TOK), BF)
WIDER = ((MINE, BLOCK, TOK), F32)
SPREAD = ((ROWS, NBD, TOK), BF)
MODEL = ((NBD, BLOCK, TOK), BF)
TILE = ((16, ROWS, TOK), BF)
FIRST = ((16, 16, ROWS, BLOCK), BF)
SECOND = ((16, 12, ROWS, BLOCK), BF)
ONE = 2 * 448 * 4 * 128 * 512


def swap_table():
    at = np.arange(256)
    table = np.zeros((256, 256), np.float32)
    table[at, at % 16 * 16 + at // 16] = 1.0
    return jnp.asarray(table, BF)


def copying(kernel, outs, scratch, arrivals, flops, near, *args):
    moved = sum(a.size * a.dtype.itemsize for a in args)
    specs = [SM if a.dtype == jnp.int32 else VM for a in args[:near]] + [ANY] * (len(args) - near)
    return pl.pallas_call(
        kernel,
        out_shape=[jax.ShapeDtypeStruct(shape, dtype) for shape, dtype in outs],
        in_specs=specs,
        out_specs=[ANY] * len(outs),
        scratch_shapes=[pltpu.VMEM(shape, dtype) for shape, dtype in scratch]
        + [pltpu.SemaphoreType.DMA((arrivals,)), pltpu.SemaphoreType.DMA((9,))],
        compiler_params=pltpu.CompilerParams(vmem_limit_bytes=60 << 20),
        cost_estimate=pl.CostEstimate(flops=flops, bytes_accessed=moved, transcendentals=0),
    )(*args)


def forward_first(where, swap, held, shards):
    outs = [MODEL, SPREAD, SPREAD]
    scratch = [MODEL, FIRST, SPREAD, SPREAD, TILE, TILE]
    return copying(forward_first_kernel, outs, scratch, 17, 6 * ONE, 2, where, swap, held, *shards)


def forward_second(swap, held, gate_in, up_in):
    outs = [HIDDEN, WIDER, WIDER, SPREAD]
    scratch = [SECOND, SPREAD, SPREAD, HIDDEN, WIDER, WIDER, SPREAD, SPREAD]
    return copying(forward_second_kernel, outs, scratch, 3, 5 * ONE, 1, swap, held, gate_in, up_in)


def backward(where, swap, held, to_gate, to_up, shards):
    outs = [MODEL, SPREAD, HIDDEN, HIDDEN, MODEL, MODEL]
    scratch = [MODEL, FIRST, SECOND, WIDER, WIDER, SPREAD, HIDDEN, HIDDEN, MODEL, MODEL]
    scratch += [TILE, SPREAD, SPREAD]
    return copying(
        backward_kernel, outs, scratch, 20, 12 * ONE, 2, where, swap, held, to_gate, to_up, *shards
    )


def blocks_of(array, count, last=None):
    def index(step):
        return (step if last is None else jnp.minimum(step, last),) + (0,) * (array.ndim - 1)

    return pl.BlockSpec((count,) + array.shape[1:], index)


def grads_call(kernel, specs, blocks, flops, where, *args):
    shape = (8, 2, blocks, 8, BLOCK)
    moved = sum(a.size * a.dtype.itemsize for a in args)
    return pl.pallas_call(
        kernel,
        grid=(8,),
        out_shape=[jax.ShapeDtypeStruct(shape, BF)] * 2,
        in_specs=[SM] + specs,
        out_specs=[pl.BlockSpec(shape, lambda step: (0,) * 5)] * 2,
        compiler_params=pltpu.CompilerParams(vmem_limit_bytes=60 << 20),
        cost_estimate=pl.CostEstimate(flops=flops, bytes_accessed=moved, transcendentals=0),
    )(where, *args)


def second_grads(where, *args):
    specs = [blocks_of(a, 8) for a in args[:2]]
    specs += [blocks_of(a, 8 if a.shape[0] == ROWS else 4, MINE // 4 - 1) for a in args[2:]]
    return grads_call(second_grads_kernel, specs, 3 * HID + 16, 4 * ONE, where, *args)


def first_grads(where, x, low):
    return grads_call(first_grads_kernel, [blocks_of(x, 8), blocks_of(low, 8)], 32, 2 * ONE, where, x, low)


def join(pieces):
    outs = [((pieces.shape[1], 448), F32)] * 2
    return call(join_kernel, outs, [], ONE // 64, pieces)


GROUP = ("y", "x_lo", "core")
CHIPS = ("y", "x_lo", "x_hi")
TENSOR = ("x_hi", "z")


def size(name):
    return lax.axis_size(name)


def shift(value, step):
    count = size("z")
    return lax.ppermute(value, "z", [(i, (i + step) % count) for i in range(count)])


def swap(value):
    return lax.ppermute(value, "x_hi", [(0, 1), (1, 0)])


def halves(array, me):
    blocks = array.shape[0] // BLOCK
    half = array.shape[1] // 2
    own = lax.dynamic_slice_in_dim(array, me * half, half, 1)
    other = swap(lax.dynamic_slice_in_dim(array, (1 - me) * half, half, 1))
    return own.reshape(blocks, BLOCK, half), other.reshape(blocks, BLOCK, half)


def ring_step(step, right, left, found):
    count = size("z")
    if step < count // 2:
        right, left = [shift(v, 1) for v in right], [shift(v, -1) for v in left]
        found[count - step], found[step] = right, left
    else:
        found[step] = [shift(right[0], 1), shift(left[1], -1)]
    return right, left


def flat(found):
    return [shard for step in range(size("z")) for shard in found[step]]


def sum_cores(keep, send):
    found = lax.ppermute(send, "core", [(0, 1), (1, 0)])
    pairs = (keep.astype(F32) + found.astype(F32)).astype(BF)
    return pairs.reshape((-1,) + pairs.shape[2:])


def to_chips(pairs):
    return lax.all_to_all(pairs, CHIPS, 0, 0, tiled=True)


def total_of(chips):
    return jnp.sum(chips.astype(F32), axis=0)


def share_first(gate_first, up_first, down_second):
    nh, nz = size("x_hi"), size("z")
    y, kind = lax.axis_index("y"), lax.axis_index(("x_lo", "core"))
    each = gate_first.shape[2] // (nh * nz)
    take = functools.partial(lax.dynamic_index_in_dim, index=y, axis=0, keepdims=False)
    gate, up = take(gate_first).T, take(up_first).T
    first = jnp.where(kind == 0, gate, jnp.where(kind == 1, up, take(down_second)))
    first = first.reshape(nh, nz, each, BLOCK).transpose(1, 0, 2, 3).reshape(nz, nh * each, BLOCK)
    first = jnp.pad(first, ((0, 0), (0, ROWS - nh * each), (0, 0)))
    first = jnp.broadcast_to(first[None], (nh,) + first.shape).reshape(nh * nz, ROWS, BLOCK)
    return lax.all_to_all(first, TENSOR, 0, 0, tiled=True)


def share_second(gate_second, up_second, down_first):
    hid = gate_second.shape[0]
    d = lax.axis_index(GROUP)
    kind, at = d // 5, jnp.minimum((d % 5) * SLOTS, hid - SLOTS)
    take = functools.partial(lax.dynamic_slice_in_dim, start_index=at, slice_size=SLOTS, axis=0)
    second = jnp.where(
        kind == 0, take(gate_second), jnp.where(kind == 1, take(up_second), take(down_first))
    )
    other = swap(second)
    me = lax.axis_index("x_hi")
    second = jnp.concatenate([jnp.where(me == 0, second, other), jnp.where(me == 0, other, second)])
    return second.reshape(-1, ROWS, BLOCK)


def shards(
    activations, cotangent, gate_first, up_first, gate_second, up_second, down_first, down_second
):
    tokens = activations.shape[1]
    per = gate_first.shape[0]
    wide = gate_first.shape[2]
    hid = gate_second.shape[0]
    ny, nx, nc, nh, nz = (size(a) for a in ("y", "x_lo", "core", "x_hi", "z"))
    ngroup = ny * nx * nc
    scale = (ngroup * tokens) ** (-0.5)
    me = lax.axis_index("x_hi")
    half = tokens // 2
    each = hid * SUB
    rows = BLOCK // ngroup

    where = jnp.stack([me, lax.axis_index("z"), lax.axis_index("core")]).astype(jnp.int32)
    table = swap_table()
    x_own, x_other = halves(activations, me)
    dy_own, dy_other = halves(cotangent, me)
    first = share_first(gate_first, up_first, down_second)
    second = share_second(gate_second, up_second, down_first)
    held = lax.all_gather(jnp.concatenate([first, second]), GROUP, axis=0, tiled=False)

    steps = nz // 2
    xs, dys = {0: [x_own, x_other]}, {0: [dy_own, dy_other]}
    state = (xs[0], xs[0])
    for step in range(1, steps + 1):
        state = ring_step(step, *state, xs)
    state, _ = lax.optimization_barrier(((dys[0], dys[0]), (xs[1][0], xs[nz - 1][0])))
    state = ring_step(1, *state, dys)
    shards_x, _ = lax.optimization_barrier((flat(xs), state))
    x, gate_in, up_in = forward_first(where, table, held, shards_x)
    for step in range(2, steps - 1):
        state = ring_step(step, *state, dys)
    state, gate_in, up_in = lax.optimization_barrier((state, gate_in, up_in))
    state = ring_step(steps - 1, *state, dys)
    act, to_gate, to_up, down_in = forward_second(table, held, gate_in, up_in)
    state, to_gate, to_up = lax.optimization_barrier((state, to_gate, to_up))
    ring_step(steps, *state, dys)
    dy, back_in, gate_back, up_back, low, parts = backward(
        where, table, held, to_gate, to_up, flat(dys)
    )

    total = lax.psum_scatter(parts, "z", scatter_dimension=0, tiled=True)
    total = total.reshape(nh, per * BLOCK, half)
    kept = lax.dynamic_index_in_dim(total, me, 0, keepdims=False)
    other = swap(lax.dynamic_index_in_dim(total, 1 - me, 0, keepdims=False))

    later = second_grads(where, dy, down_in, act, back_in, gate_in, up_in, gate_back, up_back)
    x, later = lax.optimization_barrier((x, later))
    firsts = sum_cores(*first_grads(where, x, low))
    summed = total_of(to_chips(jnp.concatenate([sum_cores(*later), firsts], axis=1))) * scale
    later, firsts = summed[: 3 * hid + 16], summed[3 * hid + 16 :]
    input_grad = jnp.concatenate(
        [jnp.where(me == 0, kept, other), jnp.where(me == 0, other, kept)], axis=1
    )
    out_gs, out_us, out_df = later[: 3 * hid].reshape(3, hid, rows, BLOCK)
    pairs = []
    for part in range(ngroup):
        for z in range(nz):
            to_z, side = part // nh, part % nh
            pairs.append((part * nz + z, (side * nz + z) * nz + to_z))
    out_ds = lax.ppermute(later[3 * hid :], GROUP + ("z",), pairs)
    out_ds = out_ds.reshape(per, -1, BLOCK)[:, :each]

    firsts = firsts.reshape(nz, per * rows, 2 * ROWS)
    firsts = lax.all_to_all(firsts, "z", 0, 0, tiled=True)
    out_gf, out_uf = [value.reshape(per, rows, wide) for value in join(firsts)]
    return input_grad, out_gf, out_uf, out_gs, out_us, out_df, out_ds


def solution(mesh):
    fine = Mesh(mesh.devices.reshape(4, 2, 2, 2, 8), ("y", "x_lo", "core", "x_hi", "z"))
    arrays = P(TENSOR, GROUP)
    weights = P(TENSOR, None, None)
    return jax.shard_map(
        shards,
        mesh=fine,
        in_specs=(arrays, arrays) + (weights,) * 6,
        out_specs=(arrays,) + (P(TENSOR, GROUP, None),) * 6,
        check_vma=False,
    )
```

```python
import functools
import jax
import jax.numpy as jnp
import numpy as np
from jax import lax
from jax.experimental import pallas as pl
from jax.experimental.pallas import tpu as pltpu
from jax.sharding import Mesh
from jax.sharding import PartitionSpec as P

BLOCK = 128
SUB = 2
BF = jnp.bfloat16
F32 = jnp.float32
NBD = 64
HID = 14
MINE = 28
EACH = MINE * SUB
ROWS = 64
SLOTS = 3
PER = 4
TOK = 256
VM = pl.BlockSpec(memory_space=pltpu.VMEM)
SM = pl.BlockSpec(memory_space=pltpu.SMEM)


def first_weight(held, kind, i):
    return held[(i % PER) * 4 + kind, i // PER]


def second_weight(held, kind, c):
    side, own = c // HID, c % HID
    at = own // SLOTS
    slot = own - jnp.minimum(at * SLOTS, HID - SLOTS)
    start = (side * SLOTS + slot) * 2
    return held[kind * 5 + at, pl.ds(start, 2)].reshape(BLOCK, BLOCK)


def dot(left, right):
    return lax.dot_general(left, right, (((1,), (0,)), ((), ())), preferred_element_type=F32)


def dot_first(left, right):
    return lax.dot_general(left, right, (((0,), (0,)), ((), ())), preferred_element_type=F32)


def dot_last(left, right):
    return lax.dot_general(left, right, (((1,), (1,)), ((), ())), preferred_element_type=F32)


def loop(count, unroll):
    def run(body):
        def step(at, carry):
            body([at * unroll + k for k in range(unroll)])
            return carry

        lax.fori_loop(0, count // unroll, step, 0)

    return run


def copy(pairs, sems, first=0):
    copies = [pltpu.make_async_copy(a, b, sems.at[first + k]) for k, (a, b) in enumerate(pairs)]
    for one in copies:
        one.start()
    return copies


def wait(copies):
    for one in copies:
        one.wait()


def placed(where, shards, out):
    me, z = where[0], where[1]
    for k, shard in enumerate(shards):
        side = me if k % 2 == 0 else 1 - me
        yield shard, out.at[pl.ds(side * 32 + lax.rem(z + k // 2, 8) * PER, PER)]


def turn(swap, source, target, outer):
    tiles = [source[:, k * 16 : k * 16 + 16, :].reshape(256, TOK) for k in range(4)]
    tiles = [dot(swap[...], tile).astype(BF).reshape(16, 16, TOK) for tile in tiles]
    for k, tile in enumerate(tiles):
        target[k * 16 : k * 16 + 16, pl.ds(outer, 16), :] = tile


def forward_first_kernel(where, swap, held_all, *refs):
    shards, (x_out, gate_out, up_out) = refs[:16], refs[16:19]
    x, held, gate_in, up_in, mid_g, mid_u, ins, outs = refs[19:]
    arrive = copy(list(placed(where, shards, x)) + [(held_all.at[:, pl.ds(0, 16)], held)], ins)
    wait(arrive)
    leave = copy([(x, x_out)], outs)
    for at in range(4):

        @loop(16, 4)
        def _(ks, at=at):
            weights = [
                jnp.concatenate([first_weight(held, 0, at * 16 + k), first_weight(held, 1, at * 16 + k)])
                for k in ks
            ]
            mids = [dot(w, x[at * 16 + k]).astype(BF) for w, k in zip(weights, ks)]
            for mid, k in zip(mids, ks):
                mid_g[k] = mid[:ROWS]
                mid_u[k] = mid[ROWS:]

        turn(swap, mid_g, gate_in, at * 16)
        turn(swap, mid_u, up_in, at * 16)
        part = pl.ds(at * 16, 16)
        pairs = [(gate_in.at[:, part], gate_out.at[:, part]), (up_in.at[:, part], up_out.at[:, part])]
        leave += copy(pairs, outs, 1 + 2 * at)
    wait(leave)


def hidden(ref, c):
    return ref[pl.ds(c * SUB, SUB)].reshape(BLOCK, TOK)


def turn_back(swap, source, target, unit):
    def group(at, carry):
        tiles = [
            source[k * 16 : k * 16 + 16, pl.ds(pl.multiple_of(at * 16, 16), 16), :].reshape(256, TOK)
            for k in range(4)
        ]
        tiles = [dot(swap[...], tile).astype(BF).reshape(16, 16, TOK) for tile in tiles]
        for k, tile in enumerate(tiles):
            target[pl.ds(at * 16, 16), unit + k * 16 : unit + k * 16 + 16, :] = tile
        return carry

    lax.fori_loop(0, 4, group, 0)


def forward_second_kernel(swap, held_all, gate_from, up_from, *refs):
    act_out, to_gate_out, to_up_out, down_out = refs[:4]
    held, gate_in, up_in, act, to_gate, to_up, down_in, down_mid, ins, outs = refs[4:]
    wait(copy([(held_all.at[:, pl.ds(16, 12)], held), (gate_from, gate_in), (up_from, up_in)], ins))
    down_mid[EACH:] = jnp.zeros((ROWS - EACH, NBD, TOK), BF)
    leave = []
    for part in range(2):

        @loop(HID, 2)
        def _(owns, part=part):
            cs = [part * HID + own for own in owns]
            gates = [dot_first(second_weight(held, 0, c), hidden(gate_in, c)) for c in cs]
            ups = [dot_first(second_weight(held, 1, c), hidden(up_in, c)) for c in cs]
            sigmas = [jax.nn.sigmoid(g) for g in gates]
            acts = [(g * s * u).astype(BF) for g, s, u in zip(gates, sigmas, ups)]
            downs = [dot_first(second_weight(held, 2, c), a) for c, a in zip(cs, acts)]
            for c, g, s, u, a, d in zip(cs, gates, sigmas, ups, acts, downs):
                to_gate[c], to_up[c], act[c] = u * s * (1.0 + g * (1.0 - s)), g * s, a
                down_mid[pl.ds(c * SUB, SUB)] = d.astype(BF).reshape(SUB, NBD, TOK)

        rows = pl.ds(part * HID, HID)
        pairs = [(to_gate, to_gate_out), (to_up, to_up_out), (act, act_out)]
        leave += copy([(a.at[rows], b.at[rows]) for a, b in pairs], outs, 3 * part)
    turn_back(swap, down_mid, down_in, 0)
    wait(leave + copy([(down_in, down_out)], outs, 6))


def backward_kernel(where, swap, held_all, to_gate_from, to_up_from, *refs):
    shards, out = refs[:16], refs[16:22]
    dy, held, held_second, to_gate, to_up, back_in, gate_back, up_back = refs[22:30]
    low, parts, mid, low_g, low_u, ins, outs = refs[30:]
    arrive = copy(list(placed(where, shards, dy)) + [(held_all.at[:, pl.ds(0, 16)], held)], ins)
    pairs = [(held_all.at[:, pl.ds(16, 12)], held_second), (to_gate_from, to_gate), (to_up_from, to_up)]
    later = copy(pairs, ins, 17)
    low_g[EACH:] = jnp.zeros((ROWS - EACH, NBD, TOK), BF)
    low_u[EACH:] = jnp.zeros((ROWS - EACH, NBD, TOK), BF)
    wait(arrive)
    leave = copy([(dy, out[0])], outs)

    def group(at, carry):
        @loop(16, 4)
        def _(ks):
            mids = [dot(first_weight(held, 2, at * 16 + k), dy[at * 16 + k]).astype(BF) for k in ks]
            for value, k in zip(mids, ks):
                mid[k] = value

        turn(swap, mid, back_in, pl.multiple_of(at * 16, 16))
        return carry

    lax.fori_loop(0, 4, group, 0)
    leave += copy([(back_in, out[1])], outs, 1)
    wait(later)

    @loop(MINE, 2)
    def _(cs):
        grads = [dot(second_weight(held_second, 2, c), hidden(back_in, c)) for c in cs]
        to_gates = [(grad * to_gate[c]).astype(BF) for c, grad in zip(cs, grads)]
        to_ups = [(grad * to_up[c]).astype(BF) for c, grad in zip(cs, grads)]
        lows_g = [dot(second_weight(held_second, 0, c), v) for c, v in zip(cs, to_gates)]
        lows_u = [dot(second_weight(held_second, 1, c), v) for c, v in zip(cs, to_ups)]
        for c, g, u, lg, lu in zip(cs, to_gates, to_ups, lows_g, lows_u):
            gate_back[c], up_back[c] = g, u
            low_g[pl.ds(c * SUB, SUB)] = lg.astype(BF).reshape(SUB, NBD, TOK)
            low_u[pl.ds(c * SUB, SUB)] = lu.astype(BF).reshape(SUB, NBD, TOK)

    leave += copy([(gate_back, out[2]), (up_back, out[3])], outs, 2)
    turn_back(swap, low_g, low, 0)
    turn_back(swap, low_u, low, ROWS)
    leave += copy([(low, out[4])], outs, 4)
    for part in range(4):

        @loop(16, 4)
        def _(ks, part=part):
            at = [part * 16 + k for k in ks]
            blocks = [k % 8 // PER * 32 + k // 8 * PER + k % PER for k in at]
            weights = [
                jnp.concatenate([first_weight(held, 0, i), first_weight(held, 1, i)]) for i in blocks
            ]
            values = [dot_first(w, low[i]).astype(BF) for w, i in zip(weights, blocks)]
            for k, value in zip(at, values):
                parts[k] = value

        rows = pl.ds(part * 16, 16)
        leave += copy([(parts.at[rows], out[5].at[rows])], outs, 5 + part)
    wait(leave)


def put(keep, send, core, index, even, odd):
    keep[index] = jnp.where(core == 0, even, odd).astype(BF)
    send[index] = jnp.where(core == 0, odd, even).astype(BF)


def put_rows(keep, send, core, side, at, value):
    for pair in range(8):
        rows = value[pair * 16 : pair * 16 + 16]
        put(keep, send, core, (pair, side, at), rows[:8], rows[8:])


def second_grads_kernel(
    where, dy, down_in, act, back_in, gate_in, up_in, gate_back, up_back, keep, send
):
    step, core = pl.program_id(0), where[2]

    @pl.when(step < MINE // 4)
    def _():
        for k in range(4):
            rows = slice(k * SUB, k * SUB + SUB)
            c = step * 4 + k
            three = (
                dot_last(gate_in[rows].reshape(BLOCK, TOK), gate_back[k]),
                dot_last(up_in[rows].reshape(BLOCK, TOK), up_back[k]),
                dot_last(act[k], back_in[rows].reshape(BLOCK, TOK)),
            )
            for kind in range(3):
                put_rows(keep, send, core, c // HID, kind * HID + c % HID, three[kind])

    fill = jnp.zeros((4, BLOCK), F32)
    grads = [dot_last(down_in[k], dy[k]) for k in range(8)]
    for n, grad in enumerate(grads):
        side, z, p = step // 4, step % 4 * 2 + n // PER, n % PER
        even, odd = [jnp.concatenate([grad[g * 28 : g * 28 + 28], fill]) for g in range(2)]
        for k in range(4):
            rows = slice(k * 8, k * 8 + 8)
            put(keep, send, core, (z, side, 3 * HID + p * 4 + k), even[rows], odd[rows])


def first_grads_kernel(where, x, low, keep, send):
    step, core = pl.program_id(0), where[2]
    grads = [dot_last(x[k], low[k]) for k in range(8)]
    for k, grad in enumerate(grads):
        i = step * 8 + k
        put_rows(keep, send, core, i // 32, i % 32, grad)


def join_kernel(pieces, gate, up):
    for z in range(8):
        value = pieces[z]
        for side in range(2):
            at = side * 224 + z * 28
            gate[:, at : at + 28] = value[:, side * 28 : side * 28 + 28]
            up[:, at : at + 28] = value[:, ROWS + side * 28 : ROWS + side * 28 + 28]


def call(kernel, outs, scratch, flops, *args):
    shapes = [jax.ShapeDtypeStruct(shape, dtype) for shape, dtype in outs]
    moved = sum(a.size * a.dtype.itemsize for a in args)
    return pl.pallas_call(
        kernel,
        out_shape=shapes,
        in_specs=[SM if a.dtype == jnp.int32 else VM for a in args],
        out_specs=[VM] * len(outs),
        scratch_shapes=[pltpu.VMEM(shape, dtype) for shape, dtype in scratch],
        compiler_params=pltpu.CompilerParams(vmem_limit_bytes=60 << 20),
        cost_estimate=pl.CostEstimate(flops=flops, bytes_accessed=moved, transcendentals=0),
    )(*args)


ANY = pl.BlockSpec(memory_space=pl.ANY)
HIDDEN = ((MINE, BLOCK, TOK), BF)
WIDER = ((MINE, BLOCK, TOK), F32)
SPREAD = ((ROWS, NBD, TOK), BF)
MODEL = ((NBD, BLOCK, TOK), BF)
TILE = ((16, ROWS, TOK), BF)
FIRST = ((16, 16, ROWS, BLOCK), BF)
SECOND = ((16, 12, ROWS, BLOCK), BF)
ONE = 2 * 448 * 4 * 128 * 512


def swap_table():
    at = np.arange(256)
    table = np.zeros((256, 256), np.float32)
    table[at, at % 16 * 16 + at // 16] = 1.0
    return jnp.asarray(table, BF)


def copying(kernel, outs, scratch, arrivals, flops, near, *args):
    moved = sum(a.size * a.dtype.itemsize for a in args)
    specs = [SM if a.dtype == jnp.int32 else VM for a in args[:near]] + [ANY] * (len(args) - near)
    return pl.pallas_call(
        kernel,
        out_shape=[jax.ShapeDtypeStruct(shape, dtype) for shape, dtype in outs],
        in_specs=specs,
        out_specs=[ANY] * len(outs),
        scratch_shapes=[pltpu.VMEM(shape, dtype) for shape, dtype in scratch]
        + [pltpu.SemaphoreType.DMA((arrivals,)), pltpu.SemaphoreType.DMA((9,))],
        compiler_params=pltpu.CompilerParams(vmem_limit_bytes=60 << 20),
        cost_estimate=pl.CostEstimate(flops=flops, bytes_accessed=moved, transcendentals=0),
    )(*args)


def forward_first(where, swap, held, shards):
    outs = [MODEL, SPREAD, SPREAD]
    scratch = [MODEL, FIRST, SPREAD, SPREAD, TILE, TILE]
    return copying(forward_first_kernel, outs, scratch, 17, 6 * ONE, 2, where, swap, held, *shards)


def forward_second(swap, held, gate_in, up_in):
    outs = [HIDDEN, WIDER, WIDER, SPREAD]
    scratch = [SECOND, SPREAD, SPREAD, HIDDEN, WIDER, WIDER, SPREAD, SPREAD]
    return copying(forward_second_kernel, outs, scratch, 3, 5 * ONE, 1, swap, held, gate_in, up_in)


def backward(where, swap, held, to_gate, to_up, shards):
    outs = [MODEL, SPREAD, HIDDEN, HIDDEN, MODEL, MODEL]
    scratch = [MODEL, FIRST, SECOND, WIDER, WIDER, SPREAD, HIDDEN, HIDDEN, MODEL, MODEL]
    scratch += [TILE, SPREAD, SPREAD]
    return copying(
        backward_kernel, outs, scratch, 20, 12 * ONE, 2, where, swap, held, to_gate, to_up, *shards
    )


def blocks_of(array, count, last=None):
    def index(step):
        return (step if last is None else jnp.minimum(step, last),) + (0,) * (array.ndim - 1)

    return pl.BlockSpec((count,) + array.shape[1:], index)


def grads_call(kernel, specs, blocks, flops, where, *args):
    shape = (8, 2, blocks, 8, BLOCK)
    moved = sum(a.size * a.dtype.itemsize for a in args)
    return pl.pallas_call(
        kernel,
        grid=(8,),
        out_shape=[jax.ShapeDtypeStruct(shape, BF)] * 2,
        in_specs=[SM] + specs,
        out_specs=[pl.BlockSpec(shape, lambda step: (0,) * 5)] * 2,
        compiler_params=pltpu.CompilerParams(vmem_limit_bytes=60 << 20),
        cost_estimate=pl.CostEstimate(flops=flops, bytes_accessed=moved, transcendentals=0),
    )(where, *args)


def second_grads(where, *args):
    specs = [blocks_of(a, 8) for a in args[:2]]
    specs += [blocks_of(a, 8 if a.shape[0] == ROWS else 4, MINE // 4 - 1) for a in args[2:]]
    return grads_call(second_grads_kernel, specs, 3 * HID + 16, 4 * ONE, where, *args)


def first_grads(where, x, low):
    return grads_call(first_grads_kernel, [blocks_of(x, 8), blocks_of(low, 8)], 32, 2 * ONE, where, x, low)


def join(pieces):
    outs = [((pieces.shape[1], 448), F32)] * 2
    return call(join_kernel, outs, [], ONE // 64, pieces)


GROUP = ("y", "x_lo", "core")
CHIPS = ("y", "x_lo", "x_hi")
TENSOR = ("x_hi", "z")


def size(name):
    return lax.axis_size(name)


def shift(value, step):
    count = size("z")
    return lax.ppermute(value, "z", [(i, (i + step) % count) for i in range(count)])


def swap(value):
    return lax.ppermute(value, "x_hi", [(0, 1), (1, 0)])


def halves(array, me):
    blocks = array.shape[0] // BLOCK
    half = array.shape[1] // 2
    own = lax.dynamic_slice_in_dim(array, me * half, half, 1)
    other = swap(lax.dynamic_slice_in_dim(array, (1 - me) * half, half, 1))
    return own.reshape(blocks, BLOCK, half), other.reshape(blocks, BLOCK, half)


def ring_step(step, right, left, found):
    count = size("z")
    if step < count // 2:
        right, left = [shift(v, 1) for v in right], [shift(v, -1) for v in left]
        found[count - step], found[step] = right, left
    else:
        found[step] = [shift(right[0], 1), shift(left[1], -1)]
    return right, left


def flat(found):
    return [shard for step in range(size("z")) for shard in found[step]]


def sum_cores(keep, send):
    found = lax.ppermute(send, "core", [(0, 1), (1, 0)])
    pairs = (keep.astype(F32) + found.astype(F32)).astype(BF)
    return pairs.reshape((-1,) + pairs.shape[2:])


def to_chips(pairs):
    return lax.all_to_all(pairs, CHIPS, 0, 0, tiled=True)


def total_of(chips):
    return jnp.sum(chips.astype(F32), axis=0)


def share_first(gate_first, up_first, down_second):
    nh, nz = size("x_hi"), size("z")
    y, kind = lax.axis_index("y"), lax.axis_index(("x_lo", "core"))
    each = gate_first.shape[2] // (nh * nz)
    take = functools.partial(lax.dynamic_index_in_dim, index=y, axis=0, keepdims=False)
    gate, up = take(gate_first).T, take(up_first).T
    first = jnp.where(kind == 0, gate, jnp.where(kind == 1, up, take(down_second)))
    first = first.reshape(nh, nz, each, BLOCK).transpose(1, 0, 2, 3).reshape(nz, nh * each, BLOCK)
    first = jnp.pad(first, ((0, 0), (0, ROWS - nh * each), (0, 0)))
    first = jnp.broadcast_to(first[None], (nh,) + first.shape).reshape(nh * nz, ROWS, BLOCK)
    return lax.all_to_all(first, TENSOR, 0, 0, tiled=True)


def share_second(gate_second, up_second, down_first):
    hid = gate_second.shape[0]
    d = lax.axis_index(GROUP)
    kind, at = d // 5, jnp.minimum((d % 5) * SLOTS, hid - SLOTS)
    take = functools.partial(lax.dynamic_slice_in_dim, start_index=at, slice_size=SLOTS, axis=0)
    second = jnp.where(
        kind == 0, take(gate_second), jnp.where(kind == 1, take(up_second), take(down_first))
    )
    other = swap(second)
    me = lax.axis_index("x_hi")
    second = jnp.concatenate([jnp.where(me == 0, second, other), jnp.where(me == 0, other, second)])
    return second.reshape(-1, ROWS, BLOCK)


def shards(
    activations, cotangent, gate_first, up_first, gate_second, up_second, down_first, down_second
):
    tokens = activations.shape[1]
    per = gate_first.shape[0]
    wide = gate_first.shape[2]
    hid = gate_second.shape[0]
    ny, nx, nc, nh, nz = (size(a) for a in ("y", "x_lo", "core", "x_hi", "z"))
    ngroup = ny * nx * nc
    scale = (ngroup * tokens) ** (-0.5)
    me = lax.axis_index("x_hi")
    half = tokens // 2
    each = hid * SUB
    rows = BLOCK // ngroup

    where = jnp.stack([me, lax.axis_index("z"), lax.axis_index("core")]).astype(jnp.int32)
    table = swap_table()
    x_own, x_other = halves(activations, me)
    dy_own, dy_other = halves(cotangent, me)
    first = share_first(gate_first, up_first, down_second)
    second = share_second(gate_second, up_second, down_first)
    held = lax.all_gather(jnp.concatenate([first, second]), GROUP, axis=0, tiled=False)

    steps = nz // 2
    xs, dys = {0: [x_own, x_other]}, {0: [dy_own, dy_other]}
    state = (xs[0], xs[0])
    for step in range(1, steps + 1):
        state = ring_step(step, *state, xs)
    state, _ = lax.optimization_barrier(((dys[0], dys[0]), (xs[1][0], xs[nz - 1][0])))
    state = ring_step(1, *state, dys)
    shards_x, _ = lax.optimization_barrier((flat(xs), state))
    x, gate_in, up_in = forward_first(where, table, held, shards_x)
    for step in range(2, steps - 1):
        state = ring_step(step, *state, dys)
    state, gate_in, up_in = lax.optimization_barrier((state, gate_in, up_in))
    state = ring_step(steps - 1, *state, dys)
    act, to_gate, to_up, down_in = forward_second(table, held, gate_in, up_in)
    state, to_gate, to_up = lax.optimization_barrier((state, to_gate, to_up))
    ring_step(steps, *state, dys)
    dy, back_in, gate_back, up_back, low, parts = backward(
        where, table, held, to_gate, to_up, flat(dys)
    )

    total = lax.psum_scatter(parts, "z", scatter_dimension=0, tiled=True)
    total = total.reshape(nh, per * BLOCK, half)
    kept = lax.dynamic_index_in_dim(total, me, 0, keepdims=False)
    other = swap(lax.dynamic_index_in_dim(total, 1 - me, 0, keepdims=False))

    later = second_grads(where, dy, down_in, act, back_in, gate_in, up_in, gate_back, up_back)
    x, later = lax.optimization_barrier((x, later))
    firsts = sum_cores(*first_grads(where, x, low))
    summed = total_of(to_chips(jnp.concatenate([sum_cores(*later), firsts], axis=1))) * scale
    later, firsts = summed[: 3 * hid + 16], summed[3 * hid + 16 :]
    input_grad = jnp.concatenate(
        [jnp.where(me == 0, kept, other), jnp.where(me == 0, other, kept)], axis=1
    )
    out_gs, out_us, out_df = later[: 3 * hid].reshape(3, hid, rows, BLOCK)
    pairs = []
    for part in range(ngroup):
        for z in range(nz):
            to_z, side = part // nh, part % nh
            pairs.append((part * nz + z, (side * nz + z) * nz + to_z))
    out_ds = lax.ppermute(later[3 * hid :], GROUP + ("z",), pairs)
    out_ds = out_ds.reshape(per, -1, BLOCK)[:, :each]

    firsts = firsts.reshape(nz, per * rows, 2 * ROWS)
    firsts = lax.all_to_all(firsts, "z", 0, 0, tiled=True)
    firsts, input_grad = lax.optimization_barrier((firsts, input_grad))
    out_gf, out_uf = [value.reshape(per, rows, wide) for value in join(firsts)]
    return input_grad, out_gf, out_uf, out_gs, out_us, out_df, out_ds


def solution(mesh):
    fine = Mesh(mesh.devices.reshape(4, 2, 2, 2, 8), ("y", "x_lo", "core", "x_hi", "z"))
    arrays = P(TENSOR, GROUP)
    weights = P(TENSOR, None, None)
    return jax.shard_map(
        shards,
        mesh=fine,
        in_specs=(arrays, arrays) + (weights,) * 6,
        out_specs=(arrays,) + (P(TENSOR, GROUP, None),) * 6,
        check_vma=False,
    )
```
